256 devices in a mesh: row: 8 (over x, z_lo), col: 32 (over y, z_hi, core).
Axes of the slice: x: 4, y: 4, z: 8 (z_hi: 4, z_lo: 2; z = z_hi * 2 + z_lo), core: 2. Of those that a mesh axis runs over, the one named last changes fastest.
Arguments:
- queries: bfloat16 [32768, 1024], P(('row', 'col')), may hold values from -24 to 24
- query_exps: int32 [32768], P(('row', 'col')), may hold values from -1 to 3
- key_head: bfloat16 [32768, 128], P(('col', 'row')), may hold values from -5 to 5
- value_head: bfloat16 [32768, 128], P(('col', 'row')), may hold values from -6 to 6
- forward_out: bfloat16 [32768, 1024], P(('row', 'col')), may hold values from -6 to 6
- output_grad: bfloat16 [32768, 1024], P(('row', 'col')), may hold values from -6 to 6
- stripe_order: int32 [256], replicated, may hold values from 0 to 255, each once
- window_size: int32 [1], replicated, may hold values from 4096 to 8192
Outputs:
- query_grad: bfloat16 [32768, 1024], P(('row', 'col'))
- key_grad: bfloat16 [32768, 128], P(('col', 'row'))
- value_grad: bfloat16 [32768, 128], P(('col', 'row'))
The draws below stay inside these ranges and needn't reach their ends.
Inputs may be any that keep to these rules, and one draw needn't show every extreme that they name: `stripe_order`: each stripe number appears once.
All inputs are finite; a program needn't handle non-finite values.
Results may differ from the reference program's by a relative error of at most 0.0095.
Values may be sent and summed in bfloat16 or wider, within the bound.
A program may use at most 128 MiB of HBM per device.

```python
import math
import jax
import jax.numpy as jnp
from jax import lax

HEADS = 8
HEAD_DIM = 128
STRIPE = 128
TOK_DEV = 128
TOKENS = 32768
STRIPES = 256
WIN = 8192
N_ROW = 8


def base_keys(key):
    return jax.random.truncated_normal(jax.random.fold_in(key, 11), -4.0, 4.0, (TOKENS, HEAD_DIM), jnp.float32)


def draw_key_head(key, part):
    keys_drawn = base_keys(key)
    return keys_drawn.astype(jnp.bfloat16)


def draw_queries(key, part):
    result = jax.random.truncated_normal(jax.random.fold_in(key, 21), -4.0, 4.0, (TOKENS, HEADS * HEAD_DIM), jnp.float32)
    return result.astype(jnp.bfloat16)


def with_ends(drawn, stream_key, least, top_value):
    index_at = [jax.random.randint(jax.random.fold_in(stream_key, axis), (), 0, length) for axis, length in enumerate(drawn.shape)]
    main_axis = drawn.shape.index(max(drawn.shape))
    beside = index_at[:main_axis] + [(index_at[main_axis] + 1) % drawn.shape[main_axis]] + index_at[main_axis + 1:]
    return drawn.at[tuple(index_at)].set(least).at[tuple(beside)].set(top_value)


def shard_levels(rng, shape, pieces, low, high):
    def one(dim, parts):
        heights = jax.random.uniform(jax.random.fold_in(jax.random.fold_in(rng, 6), dim), (parts,), jnp.float32, low / len(pieces), high / len(pieces))
        return jnp.repeat(jnp.exp(heights), shape[dim] // parts).reshape((-1,) + (1,) * (len(shape) - dim - 1))

    level = one(*pieces[0])
    for cut in pieces[1:]:
        level = level * one(*cut)
    return level


def normal_values(own_key, extent, spread, reach, pieces=(), held_as=jnp.bfloat16):
    entries = jax.random.normal(own_key, extent, jnp.float32) * spread
    if len(pieces) > 0:
        entries = shard_levels(own_key, extent, pieces, -0.22, 0.18) * entries
    return jnp.clip(entries, min=-reach, max=reach).astype(held_as)


def setup_inputs(seed: int = 0) -> dict:
    arg_keys = jax.random.split(jax.random.key(seed), 9)
    return {
        "queries": draw_queries(jax.random.fold_in(arg_keys[8], 71), 0),
        "query_exps": with_ends(jax.random.randint(arg_keys[1], (TOKENS,), -1, 4), jax.random.fold_in(arg_keys[1], 1), -1, 3).astype(jnp.int32),
        "key_head": draw_key_head(jax.random.fold_in(arg_keys[8], 71), 0),
        "value_head": normal_values(arg_keys[3], (TOKENS, HEAD_DIM), 1.0, 6.0, ((0, 256),)),
        "forward_out": normal_values(arg_keys[4], (TOKENS, HEADS * HEAD_DIM), 1.0, 6.0, ((0, 256),)),
        "output_grad": normal_values(arg_keys[5], (TOKENS, HEADS * HEAD_DIM), 1.0, 6.0, ((0, 256),)),
        "stripe_order": jax.random.permutation(arg_keys[6], STRIPES).astype(jnp.int32),
        "window_size": jax.random.randint(arg_keys[7], (1,), WIN // 2, WIN + 1).astype(jnp.int32),
    }


neg_big = -1e+30

def reference(queries, query_exps, key_head, value_head, forward_out, output_grad, stripe_order, window_size):
    feat_width = HEADS * HEAD_DIM
    back_stripes = WIN // STRIPE
    span_stripes = back_stripes + 1
    inv_scale = 1.0 / math.sqrt(HEAD_DIM)
    window_len = window_size[0]
    highest_prec = lax.Precision.HIGHEST
    scaled = (queries.astype(jnp.float32) * jnp.exp2(query_exps.astype(jnp.float32))[:, None]).astype(jnp.bfloat16)
    product = output_grad.astype(jnp.float32) * forward_out.astype(jnp.float32)
    head_delta = product.reshape(TOKENS, HEADS, HEAD_DIM).sum(-1).astype(jnp.bfloat16)
    inverse = jnp.zeros((STRIPES,), jnp.int32).at[stripe_order].set(jnp.arange(STRIPES, dtype=jnp.int32))

    def by_position(array):
        blocks = array.reshape((STRIPES, STRIPE) + array.shape[1:])
        return blocks[inverse]
    q_pos = by_position(scaled)
    g_pos = by_position(output_grad)
    d_pos = by_position(head_delta)
    padding = ((back_stripes, 0), (0, 0), (0, 0))
    k_pad = jnp.pad(by_position(key_head), padding).reshape(-1, HEAD_DIM)
    v_pad = jnp.pad(by_position(value_head), padding).reshape(-1, HEAD_DIM)
    key_panel = inverse * STRIPE // TOK_DEV % N_ROW
    owner_pad = jnp.pad(key_panel, (back_stripes, 0))
    offsets = jnp.arange(STRIPE, dtype=jnp.int32)
    key_offsets = jnp.arange(span_stripes * STRIPE, dtype=jnp.int32)
    panels = jnp.arange(N_ROW, dtype=jnp.int32)

    def one_stripe(carried, stripe_id):
        dk_acc, dv_acc = carried
        row_start = stripe_id * STRIPE
        query_tile = q_pos[stripe_id].astype(jnp.float32).reshape(STRIPE, HEADS, HEAD_DIM)
        grad_tile = g_pos[stripe_id].astype(jnp.float32).reshape(STRIPE, HEADS, HEAD_DIM)
        delta_tile = d_pos[stripe_id].astype(jnp.float32)
        key_rows = lax.dynamic_slice_in_dim(k_pad, row_start, span_stripes * STRIPE).astype(jnp.float32)
        value_rows = lax.dynamic_slice_in_dim(v_pad, row_start, span_stripes * STRIPE).astype(jnp.float32)
        owners = lax.dynamic_slice_in_dim(owner_pad, stripe_id, span_stripes)
        query_at = row_start + offsets
        key_at = row_start - back_stripes * STRIPE + key_offsets
        distance = query_at[:, None] - key_at[None, :]
        visible = ((distance >= 0) & (distance < window_len) & (key_at[None, :] >= 0))[None]
        scores = jnp.einsum('ihd,jd->hij', query_tile, key_rows, precision=highest_prec) * inv_scale
        highest = lax.optimization_barrier(jnp.max(jnp.where(visible, scores, neg_big), axis=2, keepdims=True))
        normaliser = lax.optimization_barrier(jnp.sum(jnp.exp(jnp.where(visible, scores - highest, neg_big)), axis=2, keepdims=True))
        log_norm = highest + jnp.log(normaliser)
        weights = jnp.exp(jnp.where(visible, scores - log_norm, neg_big))
        rounded_weights = lax.optimization_barrier(weights.astype(jnp.bfloat16)).astype(jnp.float32)
        weight_grad = jnp.einsum('ihd,jd->hij', grad_tile, value_rows, precision=highest_prec)
        score_grad = (weights * (weight_grad - delta_tile.T[:, :, None])).astype(jnp.bfloat16)
        score_grad = lax.optimization_barrier(score_grad).astype(jnp.float32)
        dq_parts = jnp.einsum('hinj,njd->nihd', score_grad.reshape(HEADS, STRIPE, span_stripes, STRIPE), key_rows.reshape(span_stripes, STRIPE, HEAD_DIM), precision=highest_prec) * inv_scale
        onehot = (owners[:, None] == panels[None, :]).astype(jnp.float32)
        partial_value = jnp.einsum('nc,nihd->cihd', onehot, dq_parts, precision=highest_prec)
        partial_value = lax.optimization_barrier(partial_value.astype(jnp.bfloat16)).astype(jnp.float32)
        query_part = partial_value.sum(0).reshape(STRIPE, feat_width).astype(jnp.bfloat16)
        key_part = jnp.einsum('hij,ihd->jd', score_grad, query_tile, precision=highest_prec) * inv_scale
        value_part = jnp.einsum('hij,ihd->jd', rounded_weights, grad_tile, precision=highest_prec)
        old_keys = lax.dynamic_slice_in_dim(dk_acc, row_start, span_stripes * STRIPE)
        old_values = lax.dynamic_slice_in_dim(dv_acc, row_start, span_stripes * STRIPE)
        dk_acc = lax.dynamic_update_slice_in_dim(dk_acc, old_keys + key_part, row_start, 0)
        dv_acc = lax.dynamic_update_slice_in_dim(dv_acc, old_values + value_part, row_start, 0)
        return ((dk_acc, dv_acc), query_part)
    zero_rows = jnp.zeros(((STRIPES + back_stripes) * STRIPE, HEAD_DIM), jnp.float32)
    (dk_acc, dv_acc), query_stack = lax.scan(one_stripe, (zero_rows, zero_rows), jnp.arange(STRIPES, dtype=jnp.int32))
    dk_stack = dk_acc[back_stripes * STRIPE:].reshape(STRIPES, STRIPE, HEAD_DIM)
    dv_stack = dv_acc[back_stripes * STRIPE:].reshape(STRIPES, STRIPE, HEAD_DIM)
    query_grad = query_stack[stripe_order].reshape(TOKENS, feat_width)
    key_grad = dk_stack[stripe_order].reshape(TOKENS, HEAD_DIM).astype(jnp.bfloat16)
    value_grad = dv_stack[stripe_order].reshape(TOKENS, HEAD_DIM).astype(jnp.bfloat16)
    return (query_grad, key_grad, value_grad)
```

```python
import functools
import math

import jax
import jax.numpy as jnp
from jax import lax
from jax.experimental import pallas as pl
from jax.experimental.pallas import tpu as pltpu
from jax.sharding import PartitionSpec as P

STRIPE = 128
HEADS = 8
DIM = 128
WIDE = HEADS * STRIPE
NEG = -1e30
FAR = -(1 << 20)
SCALE = 1.0 / math.sqrt(DIM)
SCALE2 = math.log2(math.e) / math.sqrt(DIM)


def build_list(j, nk, q_pos, k_pos, window, idx, gap):
    q_at = q_pos[j] * STRIPE

    def one(k, n):
        distance = q_at - k_pos[k] * STRIPE
        seen = (distance >= 0) & (distance - (STRIPE - 1) < window)
        idx[n] = k
        gap[n] = distance
        return n + seen.astype(jnp.int32)

    n = lax.fori_loop(0, nk, one, jnp.int32(0), unroll=8)
    idx[n] = 0
    gap[n] = FAR
    return (n + 1) // 2


def pair_mask(g0, g1, window):
    delta = lax.broadcasted_iota(jnp.int32, (STRIPE, STRIPE), 1) - lax.broadcasted_iota(
        jnp.int32, (STRIPE, STRIPE), 0
    )
    parts = []
    for g in (g0, g1):
        distance = delta + g
        parts.append((distance >= 0) & (distance < window))
    both = jnp.concatenate(parts, axis=0)
    return jnp.concatenate([both, both], axis=1)


def dot_nt(a, b):
    return lax.dot_general(a, b, (((1,), (1,)), ((), ())), preferred_element_type=jnp.float32)


def dot_nn(a, b):
    return lax.dot_general(a, b, (((1,), (0,)), ((), ())), preferred_element_type=jnp.float32)


def stats_kernel(nq, nk, q_pos, k_pos, win, q_ref, k_ref, out_ref, idx, gap, m_ref, l_ref):
    window = win[0]

    def per_query(j, carry):
        steps = build_list(j, nk, q_pos, k_pos, window, idx, gap)
        m_ref[...] = jnp.full_like(m_ref, NEG)
        l_ref[...] = jnp.zeros_like(l_ref)

        def step(t, c):
            i0, i1 = idx[2 * t], idx[2 * t + 1]
            keys = jnp.concatenate([k_ref[i0], k_ref[i1]], axis=0)
            mask = pair_mask(gap[2 * t], gap[2 * t + 1], window)
            for b in range(HEADS // 2):
                cols = pl.ds(b * 256, 256)
                s = dot_nt(keys, q_ref[j, cols, :])
                s = jnp.where(mask, s, NEG).reshape(32, 8, 256)
                m_old = m_ref[:, cols]
                m_new = jnp.maximum(m_old, jnp.max(s, axis=0))
                e = jnp.exp2((s - m_new[None]) * SCALE2)
                l_ref[:, cols] = l_ref[:, cols] * jnp.exp2((m_old - m_new) * SCALE2) + jnp.sum(e, axis=0)
                m_ref[:, cols] = m_new
            return c

        lax.fori_loop(0, steps, step, 0)
        m_all = m_ref[...]
        top = jnp.max(m_all, axis=0, keepdims=True)
        total = jnp.sum(l_ref[...] * jnp.exp2((m_all - top) * SCALE2), axis=0, keepdims=True)
        out_ref[j, 0:1, :] = top
        out_ref[j, 1:2, :] = total
        return carry

    lax.fori_loop(0, nq, per_query, 0)


def grads_kernel(
    nq, nk, q_pos, k_pos, win, q_ref, g_ref, k_ref, v_ref, stat_ref, dq_ref, dkv_ref, idx, gap, kt_ref, acc_ref, dq_acc
):
    window = win[0]

    def clear(k, c):
        acc_ref[k] = jnp.zeros((STRIPE, 2 * DIM), jnp.float32)
        kt_ref[k] = jnp.transpose(k_ref[k].astype(jnp.float32)).astype(jnp.bfloat16)
        return c

    lax.fori_loop(0, nk, clear, 0)

    def per_query(j, carry):
        steps = build_list(j, nk, q_pos, k_pos, window, idx, gap)
        dq_acc[...] = jnp.zeros_like(dq_acc)

        def step(t, c):
            i0, i1 = idx[2 * t], idx[2 * t + 1]
            keys = jnp.concatenate([k_ref[i0], k_ref[i1]], axis=0)
            vals = jnp.concatenate([v_ref[i0], v_ref[i1]], axis=0)
            keys_t = jnp.concatenate([kt_ref[i0], kt_ref[i1]], axis=1)
            mask = pair_mask(gap[2 * t], gap[2 * t + 1], window)
            dk = jnp.zeros((2 * STRIPE, DIM), jnp.float32)
            dv = jnp.zeros((2 * STRIPE, DIM), jnp.float32)
            for b in range(HEADS // 2):
                cols = pl.ds(b * 256, 256)
                q = q_ref[j, cols, :]
                g = g_ref[j, cols, :]
                s = dot_nt(keys, q)
                p = jnp.where(mask, jnp.exp2(s * SCALE2 - stat_ref[j, 0:1, cols]), 0.0)
                w = dot_nt(vals, g)
                ds = (p * (w - stat_ref[j, 1:2, cols])).astype(jnp.bfloat16)
                dv += dot_nn(p.astype(jnp.bfloat16), g)
                dk += dot_nn(ds, q)
                dq_acc[:, cols] += dot_nn(keys_t, ds)
            for n, i in enumerate((i0, i1)):
                rows = slice(n * STRIPE, (n + 1) * STRIPE)
                acc_ref[i, :, 0:DIM] += dk[rows]
                acc_ref[i, :, DIM:] += dv[rows]
            return c

        lax.fori_loop(0, steps, step, 0)
        dq_ref[j] = (dq_acc[...] * SCALE).astype(jnp.bfloat16)
        return carry

    lax.fori_loop(0, nq, per_query, 0)

    def finish(k, c):
        dkv_ref[k, :, 0:DIM] = (acc_ref[k, :, 0:DIM] * SCALE).astype(jnp.bfloat16)
        dkv_ref[k, :, DIM:] = acc_ref[k, :, DIM:].astype(jnp.bfloat16)
        return c

    lax.fori_loop(0, nk, finish, 0)


def smem():
    return pl.BlockSpec(memory_space=pltpu.SMEM)


def vmem():
    return pl.BlockSpec(memory_space=pltpu.VMEM)


def stats_call(nq, nk, q_pos, k_pos, win, q, k):
    return pl.pallas_call(
        functools.partial(stats_kernel, nq, nk),
        out_shape=jax.ShapeDtypeStruct((nq, 2, WIDE), jnp.float32),
        in_specs=[smem()] * 3 + [vmem()] * 2,
        out_specs=vmem(),
        scratch_shapes=[
            pltpu.SMEM((nk + 1,), jnp.int32),
            pltpu.SMEM((nk + 1,), jnp.int32),
            pltpu.VMEM((8, WIDE), jnp.float32),
            pltpu.VMEM((8, WIDE), jnp.float32),
        ],
        compiler_params=pltpu.CompilerParams(vmem_limit_bytes=48 << 20),
        name="stats",
    )(q_pos, k_pos, win, q, k)


def grads_call(nq, nk, q_pos, k_pos, win, q, g, k, v, stats):
    return pl.pallas_call(
        functools.partial(grads_kernel, nq, nk),
        out_shape=(
            jax.ShapeDtypeStruct((nq, DIM, WIDE), jnp.bfloat16),
            jax.ShapeDtypeStruct((nk, STRIPE, 2 * DIM), jnp.bfloat16),
        ),
        in_specs=[smem()] * 3 + [vmem()] * 5,
        out_specs=(vmem(), vmem()),
        scratch_shapes=[
            pltpu.SMEM((nk + 1,), jnp.int32),
            pltpu.SMEM((nk + 1,), jnp.int32),
            pltpu.VMEM((nk, DIM, STRIPE), jnp.bfloat16),
            pltpu.VMEM((nk, STRIPE, 2 * DIM), jnp.float32),
            pltpu.VMEM((DIM, WIDE), jnp.float32),
        ],
        compiler_params=pltpu.CompilerParams(vmem_limit_bytes=48 << 20),
        name="grads",
    )(q_pos, k_pos, win, q, g, k, v, stats)


def from_everyone(value, axis):
    copies = jnp.broadcast_to(value, (lax.axis_size(axis), *value.shape))
    return lax.all_to_all(copies, axis, split_axis=0, concat_axis=0, tiled=True)


def per_device(
    queries, query_exps, key_head, value_head, forward_out, output_grad, stripe_order, window_size
):
    nq = lax.axis_size("row")
    nk = lax.axis_size("col")
    q_pos = lax.dynamic_index_in_dim(stripe_order.reshape(nq, nk), lax.axis_index("col"), 1, keepdims=False)
    k_pos = lax.dynamic_index_in_dim(stripe_order.reshape(nk, nq), lax.axis_index("row"), 1, keepdims=False)

    scaled = (
        queries.astype(jnp.float32) * jnp.exp2(query_exps.astype(jnp.float32))[:, None]
    ).astype(jnp.bfloat16)

    def by_head(a):
        return a.reshape(STRIPE, HEADS, DIM).transpose(1, 0, 2).reshape(WIDE, DIM)

    product = output_grad.astype(jnp.float32) * forward_out.astype(jnp.float32)
    delta = product.reshape(STRIPE, HEADS, DIM).sum(-1).astype(jnp.bfloat16)
    delta = delta.T.reshape(1, WIDE).astype(jnp.float32)

    k_all = from_everyone(key_head, "col").reshape(nk, STRIPE, DIM)
    q_all = from_everyone(by_head(scaled), "row").reshape(nq, WIDE, DIM)
    v_all = from_everyone(value_head, "col").reshape(nk, STRIPE, DIM)
    g_all = from_everyone(by_head(output_grad), "row").reshape(nq, WIDE, DIM)

    part = stats_call(nq, nk, q_pos, k_pos, window_size, q_all, k_all)
    mine = lax.all_to_all(part, "row", split_axis=0, concat_axis=0, tiled=True)
    top = jnp.max(mine[:, 0], axis=0)
    total = jnp.sum(mine[:, 1] * jnp.exp2((mine[:, 0] - top) * SCALE2), axis=0)
    log_norm = (top * SCALE2 + jnp.log2(total))[None]
    stats = from_everyone(jnp.concatenate([log_norm, delta], axis=0)[None], "row").reshape(nq, 2, WIDE)

    dq, dkv = grads_call(nq, nk, q_pos, k_pos, window_size, q_all, g_all, k_all, v_all, stats)
    dq = lax.all_to_all(dq, "row", split_axis=0, concat_axis=0, tiled=True)
    dkv = lax.all_to_all(dkv, "col", split_axis=0, concat_axis=0, tiled=True)
    dq = dq.astype(jnp.float32).sum(0).astype(jnp.bfloat16)
    dq = dq.reshape(DIM, HEADS, STRIPE).transpose(2, 1, 0).reshape(STRIPE, WIDE)
    dkv = dkv.astype(jnp.float32).sum(0).astype(jnp.bfloat16)
    return dq, dkv[:, :DIM], dkv[:, DIM:]


def solution(mesh):
    return jax.shard_map(
        per_device,
        mesh=mesh,
        in_specs=(
            P(("row", "col"), None),
            P(("row", "col")),
            P(("col", "row"), None),
            P(("col", "row"), None),
            P(("row", "col"), None),
            P(("row", "col"), None),
            P(),
            P(),
        ),
        out_specs=(P(("row", "col"), None), P(("col", "row"), None), P(("col", "row"), None)),
        check_vma=False,
    )
```

```python
import functools
import math

import jax
import jax.numpy as jnp
from jax import lax
from jax.experimental import pallas as pl
from jax.experimental.pallas import tpu as pltpu
from jax.sharding import PartitionSpec as P

STRIPE = 128
HEADS = 8
DIM = 128
WIDE = HEADS * STRIPE
NQ = 4
NK = 64
MESH = pl.DeviceIdType.MESH
NEG = -1e30
FAR = -(1 << 20)
SCALE = 1.0 / math.sqrt(DIM)
SCALE2 = math.log2(math.e) / math.sqrt(DIM)


def coords():
    row, col = lax.axis_index("row"), lax.axis_index("col")
    x, y, core = row // 2, col // 8, col % 2
    z = ((col // 2) % 4) * 2 + row % 2
    return x, y, z, core


def device(x, y, z, core):
    return (x * 2 + z % 2, y * 8 + (z // 2) * 2 + core)


def slot_of(y, z, core):
    return core * 32 + y * 8 + z


def key_positions(order, k_pos):
    row = lax.axis_index("row")

    def one(s, c):
        y, z, core = (s // 8) % 4, s % 8, s // 32
        stored = (y * 8 + (z // 2) * 2 + core) * 8 + (row // 2) * 2 + z % 2
        k_pos[s] = order[stored] * STRIPE
        return c

    lax.fori_loop(0, NK, one, 0, unroll=8)


def query_position(order, j):
    row, col = lax.axis_index("row"), lax.axis_index("col")
    return order[(j * 2 + row % 2) * 32 + col] * STRIPE


def build_list(q_at, k_pos, window, idx, gap):
    def one(k, n):
        distance = q_at - k_pos[k]
        seen = (distance >= 0) & (distance - (STRIPE - 1) < window)
        idx[n] = k
        gap[n] = distance
        return n + seen.astype(jnp.int32)

    n = lax.fori_loop(0, NK, one, jnp.int32(0), unroll=8)
    idx[n] = 0
    gap[n] = FAR
    return (n + 1) // 2


def pair_mask(g0, g1, window):
    delta = lax.broadcasted_iota(jnp.int32, (STRIPE, STRIPE), 1) - lax.broadcasted_iota(
        jnp.int32, (STRIPE, STRIPE), 0
    )
    parts = []
    for g in (g0, g1):
        distance = delta + g
        parts.append((distance >= 0) & (distance < window))
    both = jnp.concatenate(parts, axis=0)
    return jnp.concatenate([both, both], axis=1)


def dot_nt(a, b):
    return lax.dot_general(a, b, (((1,), (1,)), ((), ())), preferred_element_type=jnp.float32)


def dot_nn(a, b):
    return lax.dot_general(a, b, (((1,), (0,)), ((), ())), preferred_element_type=jnp.float32)


def stats_kernel(order, win, q_ref, k_ref, out_ref, k_pos, idx, gap, m_ref, l_ref):
    window = win[0]
    key_positions(order, k_pos)

    def per_query(j, carry):
        steps = build_list(query_position(order, j), k_pos, window, idx, gap)
        m_ref[...] = jnp.full_like(m_ref, NEG)
        l_ref[...] = jnp.zeros_like(l_ref)

        def step(t, c):
            i0, i1 = idx[2 * t], idx[2 * t + 1]
            keys = jnp.concatenate([k_ref[i0, 0], k_ref[i1, 0]], axis=0)
            mask = pair_mask(gap[2 * t], gap[2 * t + 1], window)
            for b in range(HEADS // 2):
                cols = pl.ds(b * 256, 256)
                s = dot_nt(keys, q_ref[j, 0, cols, :])
                s = jnp.where(mask, s, NEG).reshape(32, 8, 256)
                m_old = m_ref[:, cols]
                m_new = jnp.maximum(m_old, jnp.max(s, axis=0))
                e = jnp.exp2((s - m_new[None]) * SCALE2)
                l_ref[:, cols] = l_ref[:, cols] * jnp.exp2((m_old - m_new) * SCALE2) + jnp.sum(e, axis=0)
                m_ref[:, cols] = m_new
            return c

        lax.fori_loop(0, steps, step, 0)
        m_all = m_ref[...]
        top = jnp.max(m_all, axis=0, keepdims=True)
        total = jnp.sum(l_ref[...] * jnp.exp2((m_all - top) * SCALE2), axis=0, keepdims=True)
        out_ref[0, pl.ds(j, 1), :] = top
        out_ref[1, pl.ds(j, 1), :] = total
        return carry

    lax.fori_loop(0, NQ, per_query, 0)


def grads_kernel(
    order, win, qg_ref, kv_ref, norm_ref, delta_ref, dq_ref, dkv_ref, k_pos, idx, gap, kt_ref, acc_ref, dq_acc, stat_ref
):
    window = win[0]
    key_positions(order, k_pos)

    def clear(k, c):
        acc_ref[k] = jnp.zeros((STRIPE, 2 * DIM), jnp.float32)
        kt_ref[k] = jnp.transpose(kv_ref[k, 0].astype(jnp.float32)).astype(jnp.bfloat16)
        return c

    lax.fori_loop(0, NK, clear, 0)

    def per_query(j, carry):
        steps = build_list(query_position(order, j), k_pos, window, idx, gap)
        dq_acc[...] = jnp.zeros_like(dq_acc)
        stat_ref[0:1, :] = norm_ref[pl.ds(j, 1), :]
        for h in range(HEADS):
            stat_ref[1:2, h * DIM : (h + 1) * DIM] = delta_ref[j, h : h + 1, :]

        def step(t, c):
            i0, i1 = idx[2 * t], idx[2 * t + 1]
            keys = jnp.concatenate([kv_ref[i0, 0], kv_ref[i1, 0]], axis=0)
            vals = jnp.concatenate([kv_ref[i0, 1], kv_ref[i1, 1]], axis=0)
            keys_t = jnp.concatenate([kt_ref[i0], kt_ref[i1]], axis=1)
            mask = pair_mask(gap[2 * t], gap[2 * t + 1], window)
            dk = jnp.zeros((2 * STRIPE, DIM), jnp.float32)
            dv = jnp.zeros((2 * STRIPE, DIM), jnp.float32)
            for b in range(HEADS // 2):
                cols = pl.ds(b * 256, 256)
                q = qg_ref[j, 0, cols, :]
                g = qg_ref[j, 1, cols, :]
                s = dot_nt(keys, q)
                p = jnp.where(mask, jnp.exp2(s * SCALE2 - stat_ref[0:1, cols]), 0.0)
                w = dot_nt(vals, g)
                ds = (p * (w - stat_ref[1:2, cols])).astype(jnp.bfloat16)
                dv += dot_nn(p.astype(jnp.bfloat16), g)
                dk += dot_nn(ds, q)
                dq_acc[:, cols] += dot_nn(keys_t, ds)
            for n, i in enumerate((i0, i1)):
                rows = slice(n * STRIPE, (n + 1) * STRIPE)
                acc_ref[i, :, 0:DIM] += dk[rows]
                acc_ref[i, :, DIM:] += dv[rows]
            return c

        lax.fori_loop(0, steps, step, 0)
        dq_ref[j] = (dq_acc[...] * SCALE).astype(jnp.bfloat16)
        return carry

    lax.fori_loop(0, NQ, per_query, 0)

    def finish(k, c):
        dkv_ref[k, :, 0:DIM] = (acc_ref[k, :, 0:DIM] * SCALE).astype(jnp.bfloat16)
        dkv_ref[k, :, DIM:] = acc_ref[k, :, DIM:].astype(jnp.bfloat16)
        return c

    lax.fori_loop(0, NK, finish, 0)


def remote(src, dst, send_sem, recv_sem, to):
    return pltpu.make_async_remote_copy(
        src_ref=src, dst_ref=dst, send_sem=send_sem, recv_sem=recv_sem, device_id=to, device_id_type=MESH
    )


def greet(peers):
    barrier = pltpu.get_barrier_semaphore()
    for peer in peers:
        pl.semaphore_signal(barrier, inc=1, device_id=peer, device_id_type=MESH)
    pl.semaphore_wait(barrier, len(peers))


def plane_peers(x, y, z, core):
    peers = [device(x, y, z, 1 - core)]
    peers += [device((x + d) % 4, y, z, core) for d in (1, 3)]
    peers += [device(x, (y + d) % 4, z, core) for d in (1, 3)]
    peers += [device(x, y, (z + d) % 8, core) for d in range(1, 8)]
    return peers


def gather_kernel(
    q_ref, exp_ref, k_ref, v_ref, o_ref, g_ref, qg_out, kv_out, delta_out,
    kv_own, qg_own, delta_own, kv_recv, z_send, y_send, y_pass, sib_send, x_send, x_pass, x_recv, d_send, d_recv, local,
):
    x, y, z, core = coords()
    mine = slot_of(y, z, core)
    sibling = device(x, y, z, 1 - core)
    y_up, y_down = (y + 1) % 4, (y + 3) % 4
    sign = 1 - 2 * core
    x_to, x_from = (x + sign + 4) % 4, (x - sign + 4) % 4

    greet(plane_peers(x, y, z, core) + [device((x + 2) % 4, y, z, core)])

    kv_own[0] = k_ref[...]
    kv_own[1] = v_ref[...]

    def z_copy(d):
        return remote(
            kv_own, kv_out.at[mine], z_send.at[d], kv_recv.at[mine], device(x, y, (z + d) % 8, core)
        )

    for d in (1, 7, 2, 6, 3, 5, 4):
        z_copy(d).start()

    scale = jnp.transpose(jnp.broadcast_to(jnp.exp2(exp_ref[...].astype(jnp.float32)), (STRIPE, STRIPE)))

    def x_copy(p, n):
        return remote(
            qg_own.at[p], qg_out.at[x, p], x_send.at[p, n], x_recv.at[x, p], device((x + 1 + 2 * n) % 4, y, z, core)
        )

    for h in range(HEADS):
        cols = slice(h * DIM, (h + 1) * DIM)
        qg_own[0, cols, :] = (q_ref[:, cols].astype(jnp.float32) * scale).astype(jnp.bfloat16)
    for n in range(2):
        x_copy(0, n).start()
    for h in range(HEADS):
        cols = slice(h * DIM, (h + 1) * DIM)
        qg_own[1, cols, :] = g_ref[:, cols]
    for n in range(2):
        x_copy(1, n).start()

    own_kv = pltpu.make_async_copy(kv_own, kv_out.at[mine], local.at[0])
    own_qg = pltpu.make_async_copy(qg_own, qg_out.at[x], local.at[1])
    own_kv.start()
    own_qg.start()

    def y_copy(s, src, d, up):
        to = y_up if up else y_down
        return remote(src, kv_out.at[s], y_send.at[d, 0 if up else 1], kv_recv.at[s], device(x, to, z, core))

    def sib_copy(s, src):
        return remote(src, kv_out.at[s], sib_send.at[s % 32], kv_recv.at[s], sibling)

    def arrived(s):
        remote(kv_own, kv_out.at[s], local.at[0], kv_recv.at[s], sibling).wait_recv()

    y_copy(mine, kv_own, 0, True).start()
    y_copy(mine, kv_own, 0, False).start()
    sib_copy(mine, kv_own).start()

    for h in range(HEADS):
        cols = slice(h * DIM, (h + 1) * DIM)
        product = g_ref[:, cols].astype(jnp.float32) * o_ref[:, cols].astype(jnp.float32)
        sums = jnp.sum(jnp.transpose(product), axis=0, keepdims=True)
        delta_own[h : h + 1, :] = sums.astype(jnp.bfloat16).astype(jnp.float32)

    def d_copy(n):
        return remote(delta_own, delta_out.at[x], d_send.at[n], d_recv.at[x], device((x + 1 + n) % 4, y, z, core))

    for n in range(3):
        d_copy(n).start()
    own_delta = pltpu.make_async_copy(delta_own, delta_out.at[x], local.at[2])
    own_delta.start()

    def from_z(d, c):
        s = slot_of(y, (z + d) % 8, core)
        arrived(s)
        y_copy(s, kv_out.at[s], d, True).start()
        y_copy(s, kv_out.at[s], d, False).start()
        sib_copy(s, kv_out.at[s]).start()
        return c

    def x_arrived(who, p):
        remote(qg_own.at[p], qg_out.at[who, p], local.at[0], x_recv.at[who, p], sibling).wait_recv()

    def x_forward(p):
        return remote(
            qg_out.at[x_from, p], qg_out.at[x_from, p], x_pass.at[p], x_recv.at[x_from, p], device(x_to, y, z, core)
        )

    def from_y(lower, upper):
        def body(d, c):
            zz = (z + d) % 8
            below, above = slot_of(y_down, zz, core), slot_of(y_up, zz, core)
            arrived(below)
            if lower:
                y_onward(below, d, True).start()
            sib_copy(below, kv_out.at[below]).start()
            arrived(above)
            if upper:
                y_onward(above, d, False).start()
            sib_copy(above, kv_out.at[above]).start()
            return c

        return body

    def y_onward(s, d, up):
        to = y_up if up else y_down
        return remote(kv_out.at[s], kv_out.at[s], y_pass.at[d], kv_recv.at[s], device(x, to, z, core))

    for d in (1, 7, 2, 6, 3, 5, 4):
        from_z(d, 0)
    x_arrived(x_from, 0)
    x_forward(0).start()
    lax.fori_loop(0, 4, from_y(True, False), 0)
    x_arrived(x_from, 1)
    x_forward(1).start()
    lax.fori_loop(4, 8, from_y(False, True), 0)

    def from_far(d, c):
        s = slot_of((y + 2) % 4, (z + d) % 8, core)
        arrived(s)
        sib_copy(s, kv_out.at[s]).start()
        return c

    lax.fori_loop(0, 8, from_far, 0)

    for p in range(2):
        x_arrived(x_to, p)
        x_arrived((x + 2) % 4, p)
    for n in range(1, 4):
        who = (x + n) % 4
        remote(delta_own, delta_out.at[who], local.at[0], d_recv.at[who], sibling).wait_recv()

    def from_sibling(s, c):
        arrived((1 - core) * 32 + s)
        return c

    lax.fori_loop(0, 32, from_sibling, 0)

    def sent(d, c):
        y_copy(mine, kv_own, d, True).wait_send()
        y_copy(mine, kv_own, d, False).wait_send()
        y_onward(mine, d, True).wait_send()
        return c

    lax.fori_loop(0, 8, sent, 0)

    def sib_sent(s, c):
        sib_copy(s, kv_own).wait_send()
        return c

    lax.fori_loop(0, 32, sib_sent, 0)
    for d in range(1, 8):
        z_copy(d).wait_send()
    for p in range(2):
        for n in range(2):
            x_copy(p, n).wait_send()
        x_forward(p).wait_send()
    for n in range(3):
        d_copy(n).wait_send()
    own_kv.wait()
    own_qg.wait()
    own_delta.wait()


def norm_kernel(part_ref, out_ref, got, send, recv):
    x, y, z, core = coords()
    peers = [device((x + d) % 4, y, z, core) for d in (1, 3, 2)]
    greet(peers)

    def copy(n):
        return remote(part_ref, got.at[x], send.at[n], recv.at[x], peers[n])

    for n in range(3):
        copy(n).start()
    for n in range(1, 4):
        who = (x + n) % 4
        remote(part_ref, got.at[who], send.at[0], recv.at[who], peers[0]).wait_recv()
    tops = [part_ref[0]] + [got[(x + n) % 4, 0] for n in range(1, 4)]
    sums = [part_ref[1]] + [got[(x + n) % 4, 1] for n in range(1, 4)]
    top = functools.reduce(jnp.maximum, tops)
    total = functools.reduce(jnp.add, [s * jnp.exp2((t - top) * SCALE2) for t, s in zip(tops, sums)])
    out_ref[...] = top * SCALE2 + jnp.log2(total)
    for n in range(3):
        copy(n).wait_send()


def reduce_kernel(
    dq_ref, kv_ref, dq_out, dk_out, dv_out,
    sib_got, kv_sum, opp_got, near_got, far_got, z_got, x_opp, x_near, x_far, x_sum,
    sib_send, sib_recv, a_send, a_recv, b_send, b_recv, c_send, c_recv, z_send, z_recv, x_send, x_recv,
):
    x, y, z, core = coords()
    sign = 1 - 2 * core
    sibling = device(x, y, z, 1 - core)
    y_to, y_back, y_opp = (y + sign + 4) % 4, (y - sign + 4) % 4, (y + 2) % 4
    x_to, x_back, x_over = (x + sign + 4) % 4, (x - sign + 4) % 4, (x + 2) % 4
    to_next, to_back = device(x, y_to, z, core), device(x, y_back, z, core)
    dev_to, dev_back = device(x_to, y, z, core), device(x_back, y, z, core)

    greet(plane_peers(x, y, z, core))

    def add(*parts):
        return functools.reduce(jnp.add, [p.astype(jnp.float32) for p in parts])

    def sib_copy(s):
        return remote(kv_ref.at[(1 - core) * 32 + s], sib_got.at[s], sib_send.at[s], sib_recv.at[s], sibling)

    def sib_start(yy):
        def body(d, c):
            sib_copy(yy * 8 + (z + d) % 8).start()
            return c

        lax.fori_loop(0, 8, body, 0)

    sib_start(y_opp)
    x_a = remote(dq_ref.at[x_over], x_opp, x_send.at[0], x_recv.at[0], dev_to)
    x_b = remote(dq_ref.at[x_back], x_near, x_send.at[1], x_recv.at[1], dev_back)
    x_c = remote(x_sum, x_far, x_send.at[2], x_recv.at[2], dev_to)
    x_a.start()
    sib_start(y_back)
    x_b.start()
    sib_start(y_to)
    sib_start(y)

    def with_sibling(s):
        sib_copy(s).wait_recv()
        return add(kv_ref[core * 32 + s], sib_got[s])

    def a_copy(zz):
        return remote(kv_sum.at[y_opp * 8 + zz], opp_got.at[zz], a_send.at[zz], a_recv.at[zz], to_next)

    def b_copy(zz):
        return remote(kv_sum.at[y_back * 8 + zz], near_got.at[zz], b_send.at[zz], b_recv.at[zz], to_back)

    def c_copy(zz):
        return remote(kv_sum.at[y_to * 8 + zz], far_got.at[zz], c_send.at[zz], c_recv.at[zz], to_next)

    def z_copy(zz):
        return remote(kv_sum.at[y * 8 + zz], z_got.at[z], z_send.at[zz], z_recv.at[z], device(x, y, zz, core))

    def step_a(d, c):
        zz = (z + d) % 8
        s = y_opp * 8 + zz
        kv_sum[s] = with_sibling(s).astype(jnp.bfloat16)
        a_copy(zz).start()
        return c

    def step_b(d, c):
        zz = (z + d) % 8
        s = y_back * 8 + zz
        kv_sum[s] = with_sibling(s).astype(jnp.bfloat16)
        b_copy(zz).start()
        return c

    def step_c(d, c):
        zz = (z + d) % 8
        s = y_to * 8 + zz
        total = with_sibling(s)
        a_copy(zz).wait_recv()
        kv_sum[s] = add(total, opp_got[zz]).astype(jnp.bfloat16)
        c_copy(zz).start()
        return c

    def total_here(zz):
        s = y * 8 + zz
        total = with_sibling(s)
        b_copy(zz).wait_recv()
        c_copy(zz).wait_recv()
        return add(total, near_got[zz], far_got[zz])

    def step_z(d, c):
        zz = (z + d) % 8
        kv_sum[y * 8 + zz] = total_here(zz).astype(jnp.bfloat16)
        z_copy(zz).start()
        return c

    lax.fori_loop(1, 9, step_a, 0)
    lax.fori_loop(1, 9, step_b, 0)

    x_a.wait_recv()
    def sum_x(h, c):
        rows = pl.ds(pl.multiple_of(h * 16, 16), 16)
        x_sum[rows, :] = add(dq_ref[x_to, rows, :], x_opp[rows, :]).astype(jnp.bfloat16)
        return c

    lax.fori_loop(0, 8, sum_x, 0)
    x_c.start()

    lax.fori_loop(1, 9, step_c, 0)
    lax.fori_loop(1, 8, step_z, 0)

    x_b.wait_recv()
    x_c.wait_recv()
    for h in range(HEADS):
        cols = slice(h * DIM, (h + 1) * DIM)
        total = add(dq_ref[x, :, cols], x_near[:, cols], x_far[:, cols])
        dq_out[:, cols] = jnp.transpose(total).astype(jnp.bfloat16)

    total = total_here(z)
    for d in range(1, 8):
        who = (z + d) % 8
        remote(kv_sum.at[0], z_got.at[who], z_send.at[0], z_recv.at[who], sibling).wait_recv()
        total = add(total, z_got[who])
    dk_out[...] = total[:, 0:DIM].astype(jnp.bfloat16)
    dv_out[...] = total[:, DIM:].astype(jnp.bfloat16)

    def sib_sent(s, c):
        sib_copy(s).wait_send()
        return c

    lax.fori_loop(0, 32, sib_sent, 0)

    def sent(d, c):
        zz = (z + d) % 8
        a_copy(zz).wait_send()
        b_copy(zz).wait_send()
        c_copy(zz).wait_send()
        return c

    lax.fori_loop(0, 8, sent, 0)

    def z_sent(d, c):
        z_copy((z + d) % 8).wait_send()
        return c

    lax.fori_loop(1, 8, z_sent, 0)
    x_a.wait_send()
    x_b.wait_send()
    x_c.wait_send()


def smem():
    return pl.BlockSpec(memory_space=pltpu.SMEM)


def vmem():
    return pl.BlockSpec(memory_space=pltpu.VMEM)


def hbm():
    return pl.BlockSpec(memory_space=pl.ANY)


def bf16(*shape):
    return jax.ShapeDtypeStruct(shape, jnp.bfloat16)


def f32(*shape):
    return jax.ShapeDtypeStruct(shape, jnp.float32)


def dma(*shape):
    return pltpu.SemaphoreType.DMA(shape)


def params(collective_id=None, vmem_mib=48):
    return pltpu.CompilerParams(
        collective_id=collective_id, has_side_effects=collective_id is not None, vmem_limit_bytes=vmem_mib << 20
    )


def gather_call(queries, exps, keys, values, outs, grads):
    return pl.pallas_call(
        gather_kernel,
        out_shape=(bf16(NQ, 2, WIDE, DIM), bf16(NK, 2, STRIPE, DIM), f32(NQ, HEADS, STRIPE)),
        in_specs=[vmem()] * 6,
        out_specs=(hbm(), hbm(), hbm()),
        scratch_shapes=[
            pltpu.VMEM((2, STRIPE, DIM), jnp.bfloat16),
            pltpu.VMEM((2, WIDE, DIM), jnp.bfloat16),
            pltpu.VMEM((HEADS, STRIPE), jnp.float32),
            dma(NK), dma(8), dma(8, 2), dma(8), dma(32), dma(2, 2), dma(2), dma(NQ, 2), dma(3), dma(NQ), dma(3),
        ],
        compiler_params=params(0),
        name="gather",
    )(queries, exps, keys, values, outs, grads)


def stats_call(order, win, qg, kv):
    return pl.pallas_call(
        stats_kernel,
        grid=(1,),
        out_shape=f32(2, NQ, WIDE),
        in_specs=[
            smem(),
            smem(),
            pl.BlockSpec((NQ, 1, WIDE, DIM), lambda i: (0, 0, 0, 0)),
            pl.BlockSpec((NK, 1, STRIPE, DIM), lambda i: (0, 0, 0, 0)),
        ],
        out_specs=pl.BlockSpec((2, NQ, WIDE), lambda i: (0, 0, 0)),
        scratch_shapes=[
            pltpu.SMEM((NK,), jnp.int32),
            pltpu.SMEM((NK + 1,), jnp.int32),
            pltpu.SMEM((NK + 1,), jnp.int32),
            pltpu.VMEM((8, WIDE), jnp.float32),
            pltpu.VMEM((8, WIDE), jnp.float32),
        ],
        compiler_params=params(),
        name="stats",
    )(order, win, qg, kv)


def norm_call(part):
    return pl.pallas_call(
        norm_kernel,
        out_shape=f32(NQ, WIDE),
        in_specs=[vmem()],
        out_specs=vmem(),
        scratch_shapes=[pltpu.VMEM((NQ, 2, NQ, WIDE), jnp.float32), dma(3), dma(NQ)],
        compiler_params=params(1),
        name="norm",
    )(part)


def grads_call(order, win, qg, kv, norm, delta):
    return pl.pallas_call(
        grads_kernel,
        out_shape=(bf16(NQ, DIM, WIDE), bf16(NK, STRIPE, 2 * DIM)),
        in_specs=[smem()] * 2 + [vmem()] * 4,
        out_specs=(vmem(), vmem()),
        scratch_shapes=[
            pltpu.SMEM((NK,), jnp.int32),
            pltpu.SMEM((NK + 1,), jnp.int32),
            pltpu.SMEM((NK + 1,), jnp.int32),
            pltpu.VMEM((NK, DIM, STRIPE), jnp.bfloat16),
            pltpu.VMEM((NK, STRIPE, 2 * DIM), jnp.float32),
            pltpu.VMEM((DIM, WIDE), jnp.float32),
            pltpu.VMEM((2, WIDE), jnp.float32),
        ],
        compiler_params=params(),
        name="grads",
    )(order, win, qg, kv, norm, delta)


def reduce_call(dq, dkv):
    tile = (STRIPE, 2 * DIM)
    return pl.pallas_call(
        reduce_kernel,
        out_shape=(bf16(STRIPE, WIDE), bf16(STRIPE, DIM), bf16(STRIPE, DIM)),
        in_specs=[vmem()] * 2,
        out_specs=(vmem(), vmem(), vmem()),
        scratch_shapes=[
            pltpu.VMEM((32, *tile), jnp.bfloat16),
            pltpu.VMEM((32, *tile), jnp.bfloat16),
            pltpu.VMEM((8, *tile), jnp.bfloat16),
            pltpu.VMEM((8, *tile), jnp.bfloat16),
            pltpu.VMEM((8, *tile), jnp.bfloat16),
            pltpu.VMEM((8, *tile), jnp.bfloat16),
            pltpu.VMEM((DIM, WIDE), jnp.bfloat16),
            pltpu.VMEM((DIM, WIDE), jnp.bfloat16),
            pltpu.VMEM((DIM, WIDE), jnp.bfloat16),
            pltpu.VMEM((DIM, WIDE), jnp.bfloat16),
            dma(32), dma(32), dma(8), dma(8), dma(8), dma(8), dma(8), dma(8), dma(8), dma(8), dma(3), dma(3),
        ],
        compiler_params=params(2),
        name="reduce",
    )(dq, dkv)


def per_device(
    queries, query_exps, key_head, value_head, forward_out, output_grad, stripe_order, window_size
):
    qg, kv, delta = gather_call(
        queries, query_exps.reshape(1, STRIPE), key_head, value_head, forward_out, output_grad
    )
    part = stats_call(stripe_order, window_size, qg, kv)
    norm = norm_call(part)
    dq, dkv = grads_call(stripe_order, window_size, qg, kv, norm, delta)
    return reduce_call(dq, dkv)


def solution(mesh):
    return jax.shard_map(
        per_device,
        mesh=mesh,
        in_specs=(
            P(("row", "col"), None),
            P(("row", "col")),
            P(("col", "row"), None),
            P(("col", "row"), None),
            P(("row", "col"), None),
            P(("row", "col"), None),
            P(),
            P(),
        ),
        out_specs=(P(("row", "col"), None), P(("col", "row"), None), P(("col", "row"), None)),
        check_vma=False,
    )
```

```python
import functools
import math

import jax
import jax.numpy as jnp
from jax import lax
from jax.experimental import pallas as pl
from jax.experimental.pallas import tpu as pltpu
from jax.sharding import PartitionSpec as P

STRIPE = 128
HEADS = 8
DIM = 128
WIDE = HEADS * STRIPE
NQ = 4
NK = 64
MESH = pl.DeviceIdType.MESH
NEG = -1e30
FAR = -(1 << 20)
SCALE = 1.0 / math.sqrt(DIM)
SCALE2 = math.log2(math.e) / math.sqrt(DIM)


def coords():
    row, col = lax.axis_index("row"), lax.axis_index("col")
    x, y, core = row // 2, col // 8, col % 2
    z = ((col // 2) % 4) * 2 + row % 2
    return x, y, z, core


def device(x, y, z, core):
    return (x * 2 + z % 2, y * 8 + (z // 2) * 2 + core)


def slot_of(y, z, core):
    return core * 32 + y * 8 + z


def key_positions(order, k_pos):
    row = lax.axis_index("row")

    def one(s, c):
        y, z, core = (s // 8) % 4, s % 8, s // 32
        stored = (y * 8 + (z // 2) * 2 + core) * 8 + (row // 2) * 2 + z % 2
        k_pos[s] = order[stored] * STRIPE
        return c

    lax.fori_loop(0, NK, one, 0, unroll=8)


def query_position(order, j):
    row, col = lax.axis_index("row"), lax.axis_index("col")
    return order[(j * 2 + row % 2) * 32 + col] * STRIPE


def build_list(q_at, k_pos, window, idx, gap):
    def one(k, n):
        distance = q_at - k_pos[k]
        seen = (distance >= 0) & (distance - (STRIPE - 1) < window)
        idx[n] = k
        gap[n] = distance
        return n + seen.astype(jnp.int32)

    n = lax.fori_loop(0, NK, one, jnp.int32(0), unroll=8)
    idx[n] = 0
    gap[n] = FAR
    return n


def over_list(n, step):
    fours = n // 4
    lax.fori_loop(0, fours, lambda t, c: step(4, 4 * t, c), 0)
    lax.fori_loop(2 * fours, (n + 1) // 2, lambda t, c: step(2, 2 * t, c), 0)


def tile_mask(gaps, window):
    delta = lax.broadcasted_iota(jnp.int32, (STRIPE, STRIPE), 1) - lax.broadcasted_iota(
        jnp.int32, (STRIPE, STRIPE), 0
    )
    parts = []
    for g in gaps:
        distance = delta + g
        parts.append((distance >= 0) & (distance < window))
    rows = jnp.concatenate(parts, axis=0)
    return jnp.concatenate([rows, rows], axis=1)


def dot_nt(a, b):
    return lax.dot_general(a, b, (((1,), (1,)), ((), ())), preferred_element_type=jnp.float32)


def dot_nn(a, b):
    return lax.dot_general(a, b, (((1,), (0,)), ((), ())), preferred_element_type=jnp.float32)


def stats_kernel(order, win, qg_ref, kv_ref, out_ref, k_pos, idx, gap, m_ref, l_ref):
    window = win[0]
    key_positions(order, k_pos)

    def per_query(j, carry):
        n = build_list(query_position(order, j), k_pos, window, idx, gap)
        m_ref[...] = jnp.full_like(m_ref, NEG)
        l_ref[...] = jnp.zeros_like(l_ref)

        def step(group, first, c):
            keys = jnp.concatenate([kv_ref[idx[first + i], 0] for i in range(group)], axis=0)
            mask = tile_mask([gap[first + i] for i in range(group)], window)
            for b in range(HEADS // 2):
                cols = pl.ds(b * 256, 256)
                s = dot_nt(keys, qg_ref[j, 0, cols, :])
                s = jnp.where(mask, s, NEG).reshape(group * 16, 8, 256)
                m_old = m_ref[:, cols]
                m_new = jnp.maximum(m_old, jnp.max(s, axis=0))
                e = jnp.exp2((s - m_new[None]) * SCALE2)
                l_ref[:, cols] = l_ref[:, cols] * jnp.exp2((m_old - m_new) * SCALE2) + jnp.sum(e, axis=0)
                m_ref[:, cols] = m_new
            return c

        over_list(n, step)
        m_all = m_ref[...]
        top = jnp.max(m_all, axis=0, keepdims=True)
        total = jnp.sum(l_ref[...] * jnp.exp2((m_all - top) * SCALE2), axis=0, keepdims=True)
        out_ref[0, pl.ds(j, 1), :] = top
        out_ref[1, pl.ds(j, 1), :] = total
        return carry

    lax.fori_loop(0, NQ, per_query, 0)


def grads_kernel(
    order, win, qg_ref, kv_ref, norm_ref, delta_ref, dq_ref, dkv_ref, k_pos, idx, gap, acc_ref, dq_acc, stat_ref
):
    window = win[0]
    key_positions(order, k_pos)

    def clear(k, c):
        acc_ref[k] = jnp.zeros((STRIPE, 2 * DIM), jnp.float32)
        return c

    lax.fori_loop(0, NK, clear, 0)

    def per_query(j, carry):
        n = build_list(query_position(order, j), k_pos, window, idx, gap)
        dq_acc[...] = jnp.zeros_like(dq_acc)
        stat_ref[0:1, :] = norm_ref[pl.ds(j, 1), :]
        for h in range(HEADS):
            stat_ref[1:2, h * DIM : (h + 1) * DIM] = delta_ref[j, h : h + 1, :]

        def step(group, first, c):
            at = [idx[first + i] for i in range(group)]
            keys = jnp.concatenate([kv_ref[i, 0] for i in at], axis=0)
            vals = jnp.concatenate([kv_ref[i, 1] for i in at], axis=0)
            keys_t = jnp.transpose(keys)
            mask = tile_mask([gap[first + i] for i in range(group)], window)
            weights, score_grads = [], []
            for b in range(HEADS // 2):
                cols = pl.ds(b * 256, 256)
                s = dot_nt(keys, qg_ref[j, 0, cols, :])
                p = jnp.where(mask, jnp.exp2(s * SCALE2 - stat_ref[0:1, cols]), 0.0)
                w = dot_nt(vals, qg_ref[j, 1, cols, :])
                score_grads.append((p * (w - stat_ref[1:2, cols])).astype(jnp.bfloat16))
                weights.append(p.astype(jnp.bfloat16))
            weights = jnp.concatenate(weights, axis=1)
            score_grads = jnp.concatenate(score_grads, axis=1)
            dv = dot_nn(weights, qg_ref[j, 1])
            dk = dot_nn(score_grads, qg_ref[j, 0])
            dq_acc[...] += dot_nn(keys_t, score_grads)
            for i, k in enumerate(at):
                rows = slice(i * STRIPE, (i + 1) * STRIPE)
                acc_ref[k, :, 0:DIM] += dk[rows]
                acc_ref[k, :, DIM:] += dv[rows]
            return c

        over_list(n, step)
        dq_ref[j] = (dq_acc[...] * SCALE).astype(jnp.bfloat16)
        return carry

    lax.fori_loop(0, NQ, per_query, 0)

    def finish(k, c):
        dkv_ref[k, :, 0:DIM] = (acc_ref[k, :, 0:DIM] * SCALE).astype(jnp.bfloat16)
        dkv_ref[k, :, DIM:] = acc_ref[k, :, DIM:].astype(jnp.bfloat16)
        return c

    lax.fori_loop(0, NK, finish, 0)


def remote(src, dst, send_sem, recv_sem, to):
    return pltpu.make_async_remote_copy(
        src_ref=src, dst_ref=dst, send_sem=send_sem, recv_sem=recv_sem, device_id=to, device_id_type=MESH
    )


def greet(peers):
    barrier = pltpu.get_barrier_semaphore()
    for peer in peers:
        pl.semaphore_signal(barrier, inc=1, device_id=peer, device_id_type=MESH)
    pl.semaphore_wait(barrier, len(peers))


def plane_peers(x, y, z, core):
    peers = [device(x, y, z, 1 - core)]
    peers += [device((x + d) % 4, y, z, core) for d in (1, 3)]
    peers += [device(x, (y + d) % 4, z, core) for d in (1, 3)]
    peers += [device(x, y, (z + d) % 8, core) for d in range(1, 8)]
    return peers


def gather_kernel(
    q_in, exp_in, k_in, v_in, o_in, g_in, qg_out, kv_out, delta_out,
    q_ref, exp_ref, o_ref, g_ref, kv_own, qg_own, delta_own,
    kv_recv, z_send, y_send, y_pass, sib_send, x_send, x_pass, x_recv, d_send, d_recv, local, load,
):
    loads = [
        pltpu.make_async_copy(src, dst, load.at[n])
        for n, (src, dst) in enumerate(
            ((k_in, kv_own.at[0]), (v_in, kv_own.at[1]), (exp_in, exp_ref), (q_in, q_ref), (g_in, g_ref), (o_in, o_ref))
        )
    ]
    for copy in loads:
        copy.start()

    x, y, z, core = coords()
    mine = slot_of(y, z, core)
    sibling = device(x, y, z, 1 - core)
    y_up, y_down = (y + 1) % 4, (y + 3) % 4
    sign = 1 - 2 * core
    x_to, x_from = (x + sign + 4) % 4, (x - sign + 4) % 4

    greet(
        [device(x, y, z, 1 - core)]
        + [device((x + d) % 4, y, z, core) for d in (1, 3, 2)]
        + [device(x, (y + d) % 4, z, core) for d in (1, 3)]
        + [device(x, y, (z + d) % 8, core) for d in (1, 7)]
    )

    def slot_copy(s, src, send, to):
        return remote(src, kv_out.at[s], send, kv_recv.at[s], to)

    def arrived(s):
        slot_copy(s, kv_own, local.at[0], sibling).wait_recv()

    def z_copy(d, src, up):
        to = device(x, y, (z + (1 if up else 7)) % 8, core)
        return slot_copy(slot_of(y, (z + d) % 8, core), src, z_send.at[d, 0 if up else 1], to)

    def y_copy(d, src, up):
        to = device(x, y_up if up else y_down, z, core)
        return slot_copy(slot_of(y, (z + d) % 8, core), src, y_send.at[d, 0 if up else 1], to)

    def y_onward(d, up):
        s = slot_of(y_down if up else y_up, (z + d) % 8, core)
        return slot_copy(s, kv_out.at[s], y_pass.at[d], device(x, y_up if up else y_down, z, core))

    def sib_copy(s, src):
        return slot_copy(s, src, sib_send.at[s % 32], sibling)

    def spread(d, src):
        y_copy(d, src, True).start()
        y_copy(d, src, False).start()
        sib_copy(slot_of(y, (z + d) % 8, core), src).start()

    loads[0].wait()
    loads[1].wait()
    z_copy(0, kv_own, True).start()
    z_copy(0, kv_own, False).start()
    spread(0, kv_own)

    loads[2].wait()
    loads[3].wait()
    scale = jnp.transpose(jnp.broadcast_to(jnp.exp2(exp_ref[...].astype(jnp.float32)), (STRIPE, STRIPE)))

    def x_copy(p, n):
        to = device((x + 1 + 2 * n) % 4, y, z, core)
        return remote(qg_own.at[p], qg_out.at[x, p], x_send.at[p, n], x_recv.at[x, p], to)

    for h in range(HEADS):
        cols = slice(h * DIM, (h + 1) * DIM)
        qg_own[0, cols, :] = (q_ref[:, cols].astype(jnp.float32) * scale).astype(jnp.bfloat16)
    x_copy(0, 0).start()
    x_copy(0, 1).start()

    def x_arrived(who, p):
        remote(qg_own.at[p], qg_out.at[who, p], local.at[0], x_recv.at[who, p], sibling).wait_recv()

    def x_forward(p):
        block = qg_out.at[x_from, p]
        return remote(block, block, x_pass.at[p], x_recv.at[x_from, p], device(x_to, y, z, core))

    def from_z(d, up, onward):
        s = slot_of(y, (z + d) % 8, core)
        arrived(s)
        if onward is True:
            z_copy(d, kv_out.at[s], up).start()
        elif onward is not None:
            @pl.when(onward)
            def _():
                z_copy(d, kv_out.at[s], up).start()
        spread(d, kv_out.at[s])

    def from_y(d):
        zz = (z + d) % 8
        below, above = slot_of(y_down, zz, core), slot_of(y_up, zz, core)
        arrived(below)
        if d < 4:
            y_onward(d, True).start()
        sib_copy(below, kv_out.at[below]).start()
        arrived(above)
        if d >= 4:
            y_onward(d, False).start()
        sib_copy(above, kv_out.at[above]).start()

    loads[4].wait()
    for h in range(HEADS):
        cols = slice(h * DIM, (h + 1) * DIM)
        qg_own[1, cols, :] = g_ref[:, cols]

    from_z(7, True, True)
    from_z(1, False, True)

    own_kv = pltpu.make_async_copy(kv_own, kv_out.at[mine], local.at[0])
    own_qg = pltpu.make_async_copy(qg_own, qg_out.at[x], local.at[1])
    own_kv.start()
    own_qg.start()

    from_z(6, True, True)
    from_z(2, False, True)
    from_y(0)

    x_arrived(x_from, 0)
    x_forward(0).start()
    x_copy(1, 0).start()
    x_copy(1, 1).start()

    from_z(5, True, core == 0)
    from_z(3, False, core == 1)
    from_y(1)
    from_y(7)
    from_z(4, True, None)
    from_y(2)
    from_y(6)

    loads[5].wait()
    for h in range(HEADS):
        cols = slice(h * DIM, (h + 1) * DIM)
        product = g_ref[:, cols].astype(jnp.float32) * o_ref[:, cols].astype(jnp.float32)
        sums = jnp.sum(jnp.transpose(product), axis=0, keepdims=True)
        delta_own[h : h + 1, :] = sums.astype(jnp.bfloat16).astype(jnp.float32)

    def d_copy(n):
        return remote(delta_own, delta_out.at[x], d_send.at[n], d_recv.at[x], device((x + 1 + n) % 4, y, z, core))

    for n in range(3):
        d_copy(n).start()
    own_delta = pltpu.make_async_copy(delta_own, delta_out.at[x], local.at[2])
    own_delta.start()

    from_y(3)
    from_y(5)
    from_y(4)
    x_arrived(x_from, 1)
    x_forward(1).start()

    for d in (0, 1, 7, 2, 6, 3, 5, 4):
        s = slot_of((y + 2) % 4, (z + d) % 8, core)
        arrived(s)
        sib_copy(s, kv_out.at[s]).start()

    for p in range(2):
        x_arrived(x_to, p)
        x_arrived((x + 2) % 4, p)
    for n in range(1, 4):
        who = (x + n) % 4
        remote(delta_own, delta_out.at[who], local.at[0], d_recv.at[who], sibling).wait_recv()

    def from_sibling(s, c):
        arrived((1 - core) * 32 + s)
        return c

    lax.fori_loop(0, 32, from_sibling, 0)

    def sent(d, c):
        y_copy(d, kv_own, True).wait_send()
        y_copy(d, kv_own, False).wait_send()
        slot_copy(mine, kv_own, y_pass.at[d], sibling).wait_send()
        return c

    lax.fori_loop(0, 8, sent, 0)

    def sib_sent(s, c):
        sib_copy(s, kv_own).wait_send()
        return c

    lax.fori_loop(0, 32, sib_sent, 0)
    for d, up in ((0, True), (0, False), (7, True), (1, False), (6, True), (2, False)):
        z_copy(d, kv_own, up).wait_send()

    @pl.when(core == 0)
    def _():
        z_copy(5, kv_own, True).wait_send()

    @pl.when(core == 1)
    def _():
        z_copy(3, kv_own, False).wait_send()

    for p in range(2):
        x_copy(p, 0).wait_send()
        x_copy(p, 1).wait_send()
        x_forward(p).wait_send()
    for n in range(3):
        d_copy(n).wait_send()
    own_kv.wait()
    own_qg.wait()
    own_delta.wait()


def norm_kernel(part_ref, out_ref, got, send, recv):
    x, y, z, core = coords()
    peers = [device((x + d) % 4, y, z, core) for d in (1, 3, 2)]
    greet(peers)

    def copy(n):
        return remote(part_ref, got.at[x], send.at[n], recv.at[x], peers[n])

    for n in range(3):
        copy(n).start()
    for n in range(1, 4):
        who = (x + n) % 4
        remote(part_ref, got.at[who], send.at[0], recv.at[who], peers[0]).wait_recv()
    tops = [part_ref[0]] + [got[(x + n) % 4, 0] for n in range(1, 4)]
    sums = [part_ref[1]] + [got[(x + n) % 4, 1] for n in range(1, 4)]
    top = functools.reduce(jnp.maximum, tops)
    total = functools.reduce(jnp.add, [s * jnp.exp2((t - top) * SCALE2) for t, s in zip(tops, sums)])
    out_ref[...] = top * SCALE2 + jnp.log2(total)
    for n in range(3):
        copy(n).wait_send()


def reduce_kernel(
    dq_ref, kv_ref, dq_out, dk_out, dv_out,
    sib_got, kv_sum, opp_got, near_got, far_got, z_got, x_opp, x_near, x_far, x_sum,
    sib_send, sib_recv, a_send, a_recv, b_send, b_recv, c_send, c_recv, z_send, z_recv, x_send, x_recv,
):
    x, y, z, core = coords()
    sign = 1 - 2 * core
    sibling = device(x, y, z, 1 - core)
    y_to, y_back, y_opp = (y + sign + 4) % 4, (y - sign + 4) % 4, (y + 2) % 4
    x_to, x_back, x_over = (x + sign + 4) % 4, (x - sign + 4) % 4, (x + 2) % 4
    to_next, to_back = device(x, y_to, z, core), device(x, y_back, z, core)
    dev_to, dev_back = device(x_to, y, z, core), device(x_back, y, z, core)

    greet(plane_peers(x, y, z, core))

    def add(*parts):
        return functools.reduce(jnp.add, [p.astype(jnp.float32) for p in parts])

    def sib_copy(s):
        return remote(kv_ref.at[(1 - core) * 32 + s], sib_got.at[s], sib_send.at[s], sib_recv.at[s], sibling)

    far_first = (4, 3, 5, 2, 6, 1, 7, 0)

    x_a = remote(dq_ref.at[x_over], x_opp, x_send.at[0], x_recv.at[0], dev_to)
    x_b = remote(dq_ref.at[x_back], x_near, x_send.at[1], x_recv.at[1], dev_back)
    x_c = remote(x_sum, x_far, x_send.at[2], x_recv.at[2], dev_to)
    for d in far_first:
        zz = (z + d) % 8
        for yy in (y_opp, y_back, y_to, y):
            sib_copy(yy * 8 + zz).start()
        if d == 3:
            x_a.start()
            x_b.start()

    def with_sibling(s):
        sib_copy(s).wait_recv()
        return add(kv_ref[core * 32 + s], sib_got[s])

    def a_copy(zz):
        return remote(kv_sum.at[y_opp * 8 + zz], opp_got.at[zz], a_send.at[zz], a_recv.at[zz], to_next)

    def b_copy(zz):
        return remote(kv_sum.at[y_back * 8 + zz], near_got.at[zz], b_send.at[zz], b_recv.at[zz], to_back)

    def c_copy(zz):
        return remote(kv_sum.at[y_to * 8 + zz], far_got.at[zz], c_send.at[zz], c_recv.at[zz], to_next)

    def z_copy(zz):
        return remote(kv_sum.at[y * 8 + zz], z_got.at[z], z_send.at[zz], z_recv.at[z], device(x, y, zz, core))

    def step_a(d):
        zz = (z + d) % 8
        s = y_opp * 8 + zz
        kv_sum[s] = with_sibling(s).astype(jnp.bfloat16)
        a_copy(zz).start()

    def step_b(d):
        zz = (z + d) % 8
        s = y_back * 8 + zz
        kv_sum[s] = with_sibling(s).astype(jnp.bfloat16)
        b_copy(zz).start()

    def step_c(d):
        zz = (z + d) % 8
        s = y_to * 8 + zz
        total = with_sibling(s)
        a_copy(zz).wait_recv()
        kv_sum[s] = add(total, opp_got[zz]).astype(jnp.bfloat16)
        c_copy(zz).start()

    def total_here(zz):
        s = y * 8 + zz
        total = with_sibling(s)
        b_copy(zz).wait_recv()
        c_copy(zz).wait_recv()
        return add(total, near_got[zz], far_got[zz])

    def step_z(d):
        zz = (z + d) % 8
        kv_sum[y * 8 + zz] = total_here(zz).astype(jnp.bfloat16)
        z_copy(zz).start()

    def sum_x(h, c):
        rows = pl.ds(pl.multiple_of(h * 16, 16), 16)
        x_sum[rows, :] = add(dq_ref[x_to, rows, :], x_opp[rows, :]).astype(jnp.bfloat16)
        return c

    for n in range(11):
        if n < 8:
            step_a(far_first[n])
            step_b(far_first[n])
        if 0 <= n - 1 < 8:
            step_c(far_first[n - 1])
        if 0 <= n - 3 < 7:
            step_z(far_first[n - 3])
        if n == 6:
            x_a.wait_recv()
            lax.fori_loop(0, 8, sum_x, 0)
            x_c.start()

    x_b.wait_recv()
    x_c.wait_recv()
    for h in range(HEADS):
        cols = slice(h * DIM, (h + 1) * DIM)
        total = add(dq_ref[x, :, cols], x_near[:, cols], x_far[:, cols])
        dq_out[:, cols] = jnp.transpose(total).astype(jnp.bfloat16)

    total = total_here(z)
    for d in range(1, 8):
        who = (z + d) % 8
        remote(kv_sum.at[0], z_got.at[who], z_send.at[0], z_recv.at[who], sibling).wait_recv()
        total = add(total, z_got[who])
    dk_out[...] = total[:, 0:DIM].astype(jnp.bfloat16)
    dv_out[...] = total[:, DIM:].astype(jnp.bfloat16)

    def sib_sent(s, c):
        sib_copy(s).wait_send()
        return c

    lax.fori_loop(0, 32, sib_sent, 0)

    def sent(d, c):
        zz = (z + d) % 8
        a_copy(zz).wait_send()
        b_copy(zz).wait_send()
        c_copy(zz).wait_send()
        return c

    lax.fori_loop(0, 8, sent, 0)

    def z_sent(d, c):
        z_copy((z + d) % 8).wait_send()
        return c

    lax.fori_loop(1, 8, z_sent, 0)
    x_a.wait_send()
    x_b.wait_send()
    x_c.wait_send()


def smem():
    return pl.BlockSpec(memory_space=pltpu.SMEM)


def vmem():
    return pl.BlockSpec(memory_space=pltpu.VMEM)


def hbm():
    return pl.BlockSpec(memory_space=pl.ANY)


def bf16(*shape):
    return jax.ShapeDtypeStruct(shape, jnp.bfloat16)


def f32(*shape):
    return jax.ShapeDtypeStruct(shape, jnp.float32)


def dma(*shape):
    return pltpu.SemaphoreType.DMA(shape)


def params(collective_id=None, vmem_mib=48):
    return pltpu.CompilerParams(
        collective_id=collective_id, has_side_effects=collective_id is not None, vmem_limit_bytes=vmem_mib << 20
    )


def gather_call(queries, exps, keys, values, outs, grads):
    return pl.pallas_call(
        gather_kernel,
        out_shape=(bf16(NQ, 2, WIDE, DIM), bf16(NK, 2, STRIPE, DIM), f32(NQ, HEADS, STRIPE)),
        in_specs=[hbm()] * 6,
        out_specs=(hbm(), hbm(), hbm()),
        scratch_shapes=[
            pltpu.VMEM((STRIPE, WIDE), jnp.bfloat16),
            pltpu.VMEM((1, STRIPE), jnp.int32),
            pltpu.VMEM((STRIPE, WIDE), jnp.bfloat16),
            pltpu.VMEM((STRIPE, WIDE), jnp.bfloat16),
            pltpu.VMEM((2, STRIPE, DIM), jnp.bfloat16),
            pltpu.VMEM((2, WIDE, DIM), jnp.bfloat16),
            pltpu.VMEM((HEADS, STRIPE), jnp.float32),
            dma(NK), dma(8, 2), dma(8, 2), dma(8), dma(32), dma(2, 2), dma(2), dma(NQ, 2), dma(3), dma(NQ), dma(3), dma(6),
        ],
        compiler_params=params(0, 8),
        name="gather",
    )(queries, exps, keys, values, outs, grads)


def stats_call(order, win, qg, kv):
    return pl.pallas_call(
        stats_kernel,
        out_shape=f32(2, NQ, WIDE),
        in_specs=[smem()] * 2 + [vmem()] * 2,
        out_specs=vmem(),
        scratch_shapes=[
            pltpu.SMEM((NK,), jnp.int32),
            pltpu.SMEM((NK + 1,), jnp.int32),
            pltpu.SMEM((NK + 1,), jnp.int32),
            pltpu.VMEM((8, WIDE), jnp.float32),
            pltpu.VMEM((8, WIDE), jnp.float32),
        ],
        compiler_params=params(None, 16),
        name="stats",
    )(order, win, qg, kv)


def norm_call(part):
    return pl.pallas_call(
        norm_kernel,
        out_shape=f32(NQ, WIDE),
        in_specs=[vmem()],
        out_specs=vmem(),
        scratch_shapes=[pltpu.VMEM((NQ, 2, NQ, WIDE), jnp.float32), dma(3), dma(NQ)],
        compiler_params=params(1, 4),
        name="norm",
    )(part)


def grads_call(order, win, qg, kv, norm, delta):
    return pl.pallas_call(
        grads_kernel,
        out_shape=(bf16(NQ, DIM, WIDE), bf16(NK, STRIPE, 2 * DIM)),
        in_specs=[smem()] * 2 + [vmem()] * 4,
        out_specs=(vmem(), vmem()),
        scratch_shapes=[
            pltpu.SMEM((NK,), jnp.int32),
            pltpu.SMEM((NK + 1,), jnp.int32),
            pltpu.SMEM((NK + 1,), jnp.int32),
            pltpu.VMEM((NK, STRIPE, 2 * DIM), jnp.float32),
            pltpu.VMEM((DIM, WIDE), jnp.float32),
            pltpu.VMEM((2, WIDE), jnp.float32),
        ],
        compiler_params=params(None, 32),
        name="grads",
    )(order, win, qg, kv, norm, delta)


def reduce_call(dq, dkv):
    tile = (STRIPE, 2 * DIM)
    return pl.pallas_call(
        reduce_kernel,
        out_shape=(bf16(STRIPE, WIDE), bf16(STRIPE, DIM), bf16(STRIPE, DIM)),
        in_specs=[vmem()] * 2,
        out_specs=(vmem(), vmem(), vmem()),
        scratch_shapes=[
            pltpu.VMEM((32, *tile), jnp.bfloat16),
            pltpu.VMEM((32, *tile), jnp.bfloat16),
            pltpu.VMEM((8, *tile), jnp.bfloat16),
            pltpu.VMEM((8, *tile), jnp.bfloat16),
            pltpu.VMEM((8, *tile), jnp.bfloat16),
            pltpu.VMEM((8, *tile), jnp.bfloat16),
            pltpu.VMEM((DIM, WIDE), jnp.bfloat16),
            pltpu.VMEM((DIM, WIDE), jnp.bfloat16),
            pltpu.VMEM((DIM, WIDE), jnp.bfloat16),
            pltpu.VMEM((DIM, WIDE), jnp.bfloat16),
            dma(32), dma(32), dma(8), dma(8), dma(8), dma(8), dma(8), dma(8), dma(8), dma(8), dma(3), dma(3),
        ],
        compiler_params=params(2, 20),
        name="reduce",
    )(dq, dkv)


def per_device(
    queries, query_exps, key_head, value_head, forward_out, output_grad, stripe_order, window_size
):
    qg, kv, delta = gather_call(
        queries, query_exps.reshape(1, STRIPE), key_head, value_head, forward_out, output_grad
    )
    part = stats_call(stripe_order, window_size, qg, kv)
    norm = norm_call(part)
    dq, dkv = grads_call(stripe_order, window_size, qg, kv, norm, delta)
    return reduce_call(dq, dkv)


def solution(mesh):
    return jax.shard_map(
        per_device,
        mesh=mesh,
        in_specs=(
            P(("row", "col"), None),
            P(("row", "col")),
            P(("col", "row"), None),
            P(("col", "row"), None),
            P(("row", "col"), None),
            P(("row", "col"), None),
            P(),
            P(),
        ),
        out_specs=(P(("row", "col"), None), P(("col", "row"), None), P(("col", "row"), None)),
        check_vma=False,
    )
```

```python
import functools
import math

import jax
import jax.numpy as jnp
from jax import lax
from jax.experimental import pallas as pl
from jax.experimental.pallas import tpu as pltpu
from jax.sharding import PartitionSpec as P

STRIPE = 128
HEADS = 8
DIM = 128
WIDE = HEADS * STRIPE
NQ = 4
NK = 64
MESH = pl.DeviceIdType.MESH
NEG = -1e30
FAR = -(1 << 20)
SCALE = 1.0 / math.sqrt(DIM)
SCALE2 = math.log2(math.e) / math.sqrt(DIM)


def coords():
    row, col = lax.axis_index("row"), lax.axis_index("col")
    x, y, core = row // 2, col // 8, col % 2
    z = ((col // 2) % 4) * 2 + row % 2
    return x, y, z, core


def device(x, y, z, core):
    return (x * 2 + z % 2, y * 8 + (z // 2) * 2 + core)


def slot_of(y, z, core):
    return core * 32 + y * 8 + z


def key_slot(y, z, core):
    return core * 32 + z * 4 + y


def slot_of_key(k):
    return slot_of(k % 4, (k // 4) % 8, k // 32)


def key_positions(order, k_pos):
    row = lax.axis_index("row")

    def one(k, c):
        y, z, core = k % 4, (k // 4) % 8, k // 32
        stored = (y * 8 + (z // 2) * 2 + core) * 8 + (row // 2) * 2 + z % 2
        k_pos[k] = order[stored] * STRIPE
        return c

    lax.fori_loop(0, NK, one, 0, unroll=8)


def query_position(order, j):
    row, col = lax.axis_index("row"), lax.axis_index("col")
    return order[(j * 2 + row % 2) * 32 + col] * STRIPE


def build_list(q_at, k_pos, window, idx, gap):
    def one(k, n):
        distance = q_at - k_pos[k]
        seen = (distance >= 0) & (distance - (STRIPE - 1) < window)
        idx[n] = k
        gap[n] = distance
        return n + seen.astype(jnp.int32)

    n = lax.fori_loop(0, NK, one, jnp.int32(0), unroll=8)
    idx[n] = 0
    gap[n] = FAR
    return n


def over_list(n, step):
    fours = n // 4
    lax.fori_loop(0, fours, lambda t, c: step(4, 4 * t, c), 0)
    lax.fori_loop(2 * fours, (n + 1) // 2, lambda t, c: step(2, 2 * t, c), 0)


def tile_mask(gaps, window):
    delta = lax.broadcasted_iota(jnp.int32, (STRIPE, STRIPE), 1) - lax.broadcasted_iota(
        jnp.int32, (STRIPE, STRIPE), 0
    )
    parts = []
    for g in gaps:
        distance = delta + g
        parts.append((distance >= 0) & (distance < window))
    rows = jnp.concatenate(parts, axis=0)
    return jnp.concatenate([rows, rows], axis=1)


def dot_nt(a, b):
    return lax.dot_general(a, b, (((1,), (1,)), ((), ())), preferred_element_type=jnp.float32)


def dot_nn(a, b):
    return lax.dot_general(a, b, (((1,), (0,)), ((), ())), preferred_element_type=jnp.float32)


def fetch(src, dst, sem):
    copy = pltpu.make_async_copy(src, dst, sem)
    copy.start()
    copy.wait()


def stats_kernel(win, order_in, q_ref, k_ref, out_ref, order, order_sem, k_pos, idx, gap, m_ref, l_ref):
    window = win[0]
    fetch(order_in, order, order_sem)
    key_positions(order, k_pos)

    def per_query(j, carry):
        n = build_list(query_position(order, j), k_pos, window, idx, gap)
        m_ref[...] = jnp.full_like(m_ref, NEG)
        l_ref[...] = jnp.zeros_like(l_ref)

        def step(group, first, c):
            keys = jnp.concatenate([k_ref[idx[first + i]] for i in range(group)], axis=0)
            mask = tile_mask([gap[first + i] for i in range(group)], window)
            for b in range(HEADS // 2):
                cols = pl.ds(b * 256, 256)
                s = dot_nt(keys, q_ref[j, cols, :])
                s = jnp.where(mask, s, NEG).reshape(group * 16, 8, 256)
                m_old = m_ref[:, cols]
                m_new = jnp.maximum(m_old, jnp.max(s, axis=0))
                e = jnp.exp2((s - m_new[None]) * SCALE2)
                l_ref[:, cols] = l_ref[:, cols] * jnp.exp2((m_old - m_new) * SCALE2) + jnp.sum(e, axis=0)
                m_ref[:, cols] = m_new
            return c

        over_list(n, step)
        m_all = m_ref[...]
        top = jnp.max(m_all, axis=0, keepdims=True)
        total = jnp.sum(l_ref[...] * jnp.exp2((m_all - top) * SCALE2), axis=0, keepdims=True)
        out_ref[0, pl.ds(j, 1), :] = top
        out_ref[1, pl.ds(j, 1), :] = total
        return carry

    lax.fori_loop(0, NQ, per_query, 0)


def grads_kernel(
    win, order_in, q_ref, k_ref, v_ref, norm_ref, delta_ref, g0, g1, g2, g3, dq_ref, dkv_ref,
    order, order_sem, k_pos, idx, gap, g_ref, acc_ref, dq_acc, stat_ref,
):
    window = win[0]
    fetch(order_in, order, order_sem)
    key_positions(order, k_pos)
    for n, block in enumerate((g0, g1, g2, g3)):
        who = (lax.axis_index("row") // 2 + n) % 4
        for h in range(HEADS):
            cols = slice(h * DIM, (h + 1) * DIM)
            g_ref[who, cols, :] = block[:, cols]

    def clear(k, c):
        acc_ref[k] = jnp.zeros((STRIPE, 2 * DIM), jnp.float32)
        return c

    lax.fori_loop(0, NK, clear, 0)

    def per_query(j, carry):
        n = build_list(query_position(order, j), k_pos, window, idx, gap)
        dq_acc[...] = jnp.zeros_like(dq_acc)
        stat_ref[0:1, :] = norm_ref[pl.ds(j, 1), :]
        for h in range(HEADS):
            stat_ref[1:2, h * DIM : (h + 1) * DIM] = delta_ref[j, h : h + 1, :]

        def step(group, first, c):
            at = [idx[first + i] for i in range(group)]
            slots = [slot_of_key(k) for k in at]
            keys = jnp.concatenate([k_ref[k] for k in at], axis=0)
            vals = jnp.concatenate([v_ref[k] for k in slots], axis=0)
            keys_t = jnp.transpose(keys)
            mask = tile_mask([gap[first + i] for i in range(group)], window)
            weights, score_grads = [], []
            for b in range(HEADS // 2):
                cols = pl.ds(b * 256, 256)
                s = dot_nt(keys, q_ref[j, cols, :])
                p = jnp.where(mask, jnp.exp2(s * SCALE2 - stat_ref[0:1, cols]), 0.0)
                w = dot_nt(vals, g_ref[j, cols, :])
                score_grads.append((p * (w - stat_ref[1:2, cols])).astype(jnp.bfloat16))
                weights.append(p.astype(jnp.bfloat16))
            weights = jnp.concatenate(weights, axis=1)
            score_grads = jnp.concatenate(score_grads, axis=1)
            dv = dot_nn(weights, g_ref[j])
            dk = dot_nn(score_grads, q_ref[j])
            dq_acc[...] += dot_nn(keys_t, score_grads)
            for i, k in enumerate(slots):
                rows = slice(i * STRIPE, (i + 1) * STRIPE)
                acc_ref[k, :, 0:DIM] += dk[rows]
                acc_ref[k, :, DIM:] += dv[rows]
            return c

        over_list(n, step)
        dq_ref[j] = (dq_acc[...] * SCALE).astype(jnp.bfloat16)
        return carry

    lax.fori_loop(0, NQ, per_query, 0)

    def finish(k, c):
        dkv_ref[k, :, 0:DIM] = (acc_ref[k, :, 0:DIM] * SCALE).astype(jnp.bfloat16)
        dkv_ref[k, :, DIM:] = acc_ref[k, :, DIM:].astype(jnp.bfloat16)
        return c

    lax.fori_loop(0, NK, finish, 0)


def remote(src, dst, send_sem, recv_sem, to):
    return pltpu.make_async_remote_copy(
        src_ref=src, dst_ref=dst, send_sem=send_sem, recv_sem=recv_sem, device_id=to, device_id_type=MESH
    )


def greet(peers):
    barrier = pltpu.get_barrier_semaphore()
    for peer in peers:
        pl.semaphore_signal(barrier, inc=1, device_id=peer, device_id_type=MESH)
    pl.semaphore_wait(barrier, len(peers))


def plane_peers(x, y, z, core):
    peers = [device(x, y, z, 1 - core)]
    peers += [device((x + d) % 4, y, z, core) for d in (1, 3)]
    peers += [device(x, (y + d) % 4, z, core) for d in (1, 3)]
    peers += [device(x, y, (z + d) % 8, core) for d in range(1, 8)]
    return peers


def gather_kernel(
    q_in, exp_in, k_in, v_in, o_in, g_in, q_out, k_out, v_out, delta_out,
    q_ref, exp_ref, o_ref, g_ref, k_own, v_own, q_own, delta_own,
    ky_send, ky_recv, kz_send, kz_recv, ks_send, ks_recv,
    vz_send, vz_recv, vy_send, vy_recv, vy_pass, vs_send, vs_recv,
    x_send, x_recv, d_send, d_recv, local, load,
):
    pairs = ((k_in, k_own), (v_in, v_own), (exp_in, exp_ref), (q_in, q_ref), (g_in, g_ref), (o_in, o_ref))
    loads = [pltpu.make_async_copy(src, dst, load.at[n]) for n, (src, dst) in enumerate(pairs)]
    for copy in loads:
        copy.start()

    x, y, z, core = coords()
    sibling = device(x, y, z, 1 - core)
    sign = 1 - 2 * core
    x_to, x_from = (x + sign + 4) % 4, (x - sign + 4) % 4
    y_to, y_from = (y + sign + 4) % 4, (y - sign + 4) % 4
    y_ways = (device(x, (y + 1) % 4, z, core), device(x, (y + 3) % 4, z, core))
    z_ways = (device(x, y, (z + 1) % 8, core), device(x, y, (z + 7) % 8, core))

    greet(
        [sibling]
        + [device((x + d) % 4, y, z, core) for d in (1, 3, 2)]
        + list(y_ways)
        + list(z_ways)
    )

    def ky_copy(yy, src, n, to):
        return remote(src, k_out.at[key_slot(yy, z, core)], ky_send.at[n], ky_recv.at[yy], to)

    def ky_arrived(yy):
        ky_copy(yy, k_own, 0, sibling).wait_recv()

    def column(d, c):
        return k_out.at[pl.ds(key_slot(0, (z + d) % 8, c), 4)]

    def kz_copy(d, way):
        block = column(d, core)
        return remote(block, block, kz_send.at[d, way], kz_recv.at[(z + d) % 8], z_ways[way])

    def ks_copy(d, c):
        block = column(d, c)
        return remote(block, block, ks_send.at[(z + d) % 8], ks_recv.at[(z + d) % 8], sibling)

    def vz_copy(d, src, way):
        zz = (z + d) % 8
        return remote(src, v_out.at[slot_of(y, zz, core)], vz_send.at[d, way], vz_recv.at[zz], z_ways[way])

    def vz_arrived(d):
        vz_copy(d, v_own, 0).wait_recv()

    def half(yy, n):
        return v_out.at[pl.ds(slot_of(yy, 4 * n, core), 4)]

    def vy_copy(yy, n, sem, to):
        return remote(half(yy, n), half(yy, n), sem, vy_recv.at[yy, n], to)

    def vs_copy(yy, c):
        block = v_out.at[pl.ds(slot_of(yy, 0, c), 8)]
        return remote(block, block, vs_send.at[yy], vs_recv.at[yy], sibling)

    def q_copy(who, src, n, to):
        return remote(src, q_out.at[who], x_send.at[n], x_recv.at[who], to)

    def q_arrived(who):
        q_copy(who, q_own, 0, sibling).wait_recv()

    loads[0].wait()
    for n in range(2):
        ky_copy(y, k_own, n, y_ways[n]).start()
    own_k = pltpu.make_async_copy(k_own, k_out.at[key_slot(y, z, core)], local.at[0])
    own_k.start()
    loads[1].wait()
    for n in range(2):
        vz_copy(0, v_own, n).start()
    own_v = pltpu.make_async_copy(v_own, v_out.at[slot_of(y, z, core)], local.at[1])
    own_v.start()

    loads[2].wait()
    loads[3].wait()
    scale = jnp.transpose(jnp.broadcast_to(jnp.exp2(exp_ref[...].astype(jnp.float32)), (STRIPE, STRIPE)))
    for h in range(HEADS):
        cols = slice(h * DIM, (h + 1) * DIM)
        q_own[cols, :] = (q_ref[:, cols].astype(jnp.float32) * scale).astype(jnp.bfloat16)
    for n in range(2):
        q_copy(x, q_own, n, device((x + 1 + 2 * n) % 4, y, z, core)).start()
    own_q = pltpu.make_async_copy(q_own, q_out.at[x], local.at[2])
    own_q.start()

    def pass_values(d, way):
        vz_arrived(d)
        vz_copy(d, v_out.at[slot_of(y, (z + d) % 8, core)], way).start()

    ky_arrived(y_from)
    block = k_out.at[key_slot(y_from, z, core)]
    ky_copy(y_from, block, 2, device(x, y_to, z, core)).start()
    pass_values(7, 0)
    pass_values(1, 1)
    ky_arrived(y_to)
    ky_arrived((y + 2) % 4)
    own_k.wait()
    kz_copy(0, 0).start()
    kz_copy(0, 1).start()
    pass_values(6, 0)
    pass_values(2, 1)
    ks_copy(0, core).start()
    vz_arrived(5)
    vz_arrived(3)

    @pl.when(core == 0)
    def _():
        vz_copy(5, v_out.at[slot_of(y, (z + 5) % 8, core)], 0).start()

    @pl.when(core == 1)
    def _():
        vz_copy(3, v_out.at[slot_of(y, (z + 3) % 8, core)], 1).start()

    def kz_arrived(d):
        kz_copy(d, 0).wait_recv()

    def pass_keys(d, way):
        kz_arrived(d)
        kz_copy(d, way).start()
        ks_copy(d, core).start()

    vz_arrived(4)
    own_v.wait()
    for n in range(2):
        vy_copy(y, n, vy_send.at[n, n], y_ways[n]).start()
    for n in range(2):
        vy_copy(y, 1 - n, vy_send.at[1 - n, n], y_ways[n]).start()
    vs_copy(y, core).start()
    pass_keys(7, 0)
    pass_keys(1, 1)

    loads[4].wait()
    loads[5].wait()
    for h in range(HEADS):
        cols = slice(h * DIM, (h + 1) * DIM)
        product = g_ref[:, cols].astype(jnp.float32) * o_ref[:, cols].astype(jnp.float32)
        sums = jnp.sum(jnp.transpose(product), axis=0, keepdims=True)
        delta_own[h : h + 1, :] = sums.astype(jnp.bfloat16).astype(jnp.float32)

    def d_copy(n):
        return remote(delta_own, delta_out.at[x], d_send.at[n], d_recv.at[x], device((x + 1 + n) % 4, y, z, core))

    for n in range(3):
        d_copy(n).start()
    own_delta = pltpu.make_async_copy(delta_own, delta_out.at[x], local.at[3])
    own_delta.start()

    q_arrived(x_from)
    q_copy(x_from, q_out.at[x_from], 2, device(x_to, y, z, core)).start()

    pass_keys(6, 0)
    pass_keys(2, 1)

    def vy_arrived(yy, n):
        vy_copy(yy, n, local.at[0], sibling).wait_recv()

    beside = ((y + 3) % 4, (y + 1) % 4)
    for n in range(2):
        vy_arrived(beside[n], n)
        vy_copy(beside[n], n, vy_pass.at[n], y_ways[n]).start()

    kz_arrived(5)
    kz_arrived(3)

    @pl.when(core == 0)
    def _():
        kz_copy(5, 0).start()

    @pl.when(core == 1)
    def _():
        kz_copy(3, 1).start()

    ks_copy(5, core).start()
    ks_copy(3, core).start()
    for n in range(2):
        vy_arrived(beside[n], 1 - n)
        vs_copy(beside[n], core).start()
    kz_arrived(4)
    ks_copy(4, core).start()
    for n in range(2):
        vy_arrived((y + 2) % 4, n)
    vs_copy((y + 2) % 4, core).start()

    q_arrived(x_to)
    q_arrived((x + 2) % 4)
    for n in range(1, 4):
        who = (x + n) % 4
        remote(delta_own, delta_out.at[who], local.at[0], d_recv.at[who], sibling).wait_recv()
    for d in range(8):
        ks_copy(d, 1 - core).wait_recv()
    for yy in range(4):
        vs_copy(yy, 1 - core).wait_recv()

    for n in range(3):
        ky_copy(y, k_own, n, sibling).wait_send()
        q_copy(x, q_own, n, sibling).wait_send()
        d_copy(n).wait_send()
    for d, way in ((0, 0), (0, 1), (7, 0), (1, 1), (6, 0), (2, 1)):
        kz_copy(d, way).wait_send()
        vz_copy(d, v_own, way).wait_send()

    @pl.when(core == 0)
    def _():
        kz_copy(5, 0).wait_send()
        vz_copy(5, v_own, 0).wait_send()

    @pl.when(core == 1)
    def _():
        kz_copy(3, 1).wait_send()
        vz_copy(3, v_own, 1).wait_send()

    for n in range(2):
        vy_copy(y, n, vy_send.at[n, 0], sibling).wait_send()
        vy_copy(y, n, vy_send.at[n, 1], sibling).wait_send()
        vy_copy(y, n, vy_pass.at[n], sibling).wait_send()
    for d in range(8):
        ks_copy(d, core).wait_send()
    for yy in range(4):
        vs_copy(yy, core).wait_send()
    own_q.wait()
    own_delta.wait()


def norm_kernel(part_ref, out_ref, got, send, recv):
    x, y, z, core = coords()
    peers = [device((x + d) % 4, y, z, core) for d in (1, 3, 2)]
    greet(peers)

    def copy(n):
        return remote(part_ref, got.at[x], send.at[n], recv.at[x], peers[n])

    for n in range(3):
        copy(n).start()
    for n in range(1, 4):
        who = (x + n) % 4
        remote(part_ref, got.at[who], send.at[0], recv.at[who], peers[0]).wait_recv()
    tops = [part_ref[0]] + [got[(x + n) % 4, 0] for n in range(1, 4)]
    sums = [part_ref[1]] + [got[(x + n) % 4, 1] for n in range(1, 4)]
    top = functools.reduce(jnp.maximum, tops)
    total = functools.reduce(jnp.add, [s * jnp.exp2((t - top) * SCALE2) for t, s in zip(tops, sums)])
    out_ref[...] = top * SCALE2 + jnp.log2(total)
    for n in range(3):
        copy(n).wait_send()


def reduce_kernel(
    dq_ref, kv_ref, dq_out, dk_out, dv_out,
    sib_got, kv_sum, opp_got, near_got, far_got, z_got, x_opp, x_near, x_far, x_sum,
    sib_send, sib_recv, a_send, a_recv, b_send, b_recv, c_send, c_recv, z_send, z_recv, x_send, x_recv,
):
    x, y, z, core = coords()
    sign = 1 - 2 * core
    sibling = device(x, y, z, 1 - core)
    y_to, y_back, y_opp = (y + sign + 4) % 4, (y - sign + 4) % 4, (y + 2) % 4
    x_to, x_back, x_over = (x + sign + 4) % 4, (x - sign + 4) % 4, (x + 2) % 4
    to_next, to_back = device(x, y_to, z, core), device(x, y_back, z, core)
    dev_to, dev_back = device(x_to, y, z, core), device(x_back, y, z, core)

    greet(plane_peers(x, y, z, core))

    def add(*parts):
        return functools.reduce(jnp.add, [p.astype(jnp.float32) for p in parts])

    def sib_copy(s):
        return remote(kv_ref.at[(1 - core) * 32 + s], sib_got.at[s], sib_send.at[s], sib_recv.at[s], sibling)

    far_first = (4, 3, 5, 2, 6, 1, 7, 0)

    x_a = remote(dq_ref.at[x_over], x_opp, x_send.at[0], x_recv.at[0], dev_to)
    x_b = remote(dq_ref.at[x_back], x_near, x_send.at[1], x_recv.at[1], dev_back)
    x_c = remote(x_sum, x_far, x_send.at[2], x_recv.at[2], dev_to)
    for d in far_first:
        zz = (z + d) % 8
        for yy in (y_opp, y_back, y_to, y):
            sib_copy(yy * 8 + zz).start()
        if d == 3:
            x_a.start()
            x_b.start()

    def with_sibling(s):
        sib_copy(s).wait_recv()
        return add(kv_ref[core * 32 + s], sib_got[s])

    def a_copy(zz):
        return remote(kv_sum.at[y_opp * 8 + zz], opp_got.at[zz], a_send.at[zz], a_recv.at[zz], to_next)

    def b_copy(zz):
        return remote(kv_sum.at[y_back * 8 + zz], near_got.at[zz], b_send.at[zz], b_recv.at[zz], to_back)

    def c_copy(zz):
        return remote(kv_sum.at[y_to * 8 + zz], far_got.at[zz], c_send.at[zz], c_recv.at[zz], to_next)

    def z_copy(zz):
        return remote(kv_sum.at[y * 8 + zz], z_got.at[z], z_send.at[zz], z_recv.at[z], device(x, y, zz, core))

    def step_a(d):
        zz = (z + d) % 8
        s = y_opp * 8 + zz
        kv_sum[s] = with_sibling(s).astype(jnp.bfloat16)
        a_copy(zz).start()

    def step_b(d):
        zz = (z + d) % 8
        s = y_back * 8 + zz
        kv_sum[s] = with_sibling(s).astype(jnp.bfloat16)
        b_copy(zz).start()

    def step_c(d):
        zz = (z + d) % 8
        s = y_to * 8 + zz
        total = with_sibling(s)
        a_copy(zz).wait_recv()
        kv_sum[s] = add(total, opp_got[zz]).astype(jnp.bfloat16)
        c_copy(zz).start()

    def total_here(zz):
        s = y * 8 + zz
        total = with_sibling(s)
        b_copy(zz).wait_recv()
        c_copy(zz).wait_recv()
        return add(total, near_got[zz], far_got[zz])

    def step_z(d):
        zz = (z + d) % 8
        kv_sum[y * 8 + zz] = total_here(zz).astype(jnp.bfloat16)
        z_copy(zz).start()

    def sum_x(h, c):
        rows = pl.ds(pl.multiple_of(h * 16, 16), 16)
        x_sum[rows, :] = add(dq_ref[x_to, rows, :], x_opp[rows, :]).astype(jnp.bfloat16)
        return c

    for n in range(11):
        if n < 8:
            step_a(far_first[n])
            step_b(far_first[n])
        if 0 <= n - 1 < 8:
            step_c(far_first[n - 1])
        if 0 <= n - 3 < 7:
            step_z(far_first[n - 3])
        if n == 6:
            x_a.wait_recv()
            lax.fori_loop(0, 8, sum_x, 0)
            x_c.start()

    x_b.wait_recv()
    x_c.wait_recv()
    for h in range(HEADS):
        cols = slice(h * DIM, (h + 1) * DIM)
        total = add(dq_ref[x, :, cols], x_near[:, cols], x_far[:, cols])
        dq_out[:, cols] = jnp.transpose(total).astype(jnp.bfloat16)

    total = total_here(z)
    for d in range(1, 8):
        who = (z + d) % 8
        remote(kv_sum.at[0], z_got.at[who], z_send.at[0], z_recv.at[who], sibling).wait_recv()
        total = add(total, z_got[who])
    dk_out[...] = total[:, 0:DIM].astype(jnp.bfloat16)
    dv_out[...] = total[:, DIM:].astype(jnp.bfloat16)

    def sib_sent(s, c):
        sib_copy(s).wait_send()
        return c

    lax.fori_loop(0, 32, sib_sent, 0)

    def sent(d, c):
        zz = (z + d) % 8
        a_copy(zz).wait_send()
        b_copy(zz).wait_send()
        c_copy(zz).wait_send()
        return c

    lax.fori_loop(0, 8, sent, 0)

    def z_sent(d, c):
        z_copy((z + d) % 8).wait_send()
        return c

    lax.fori_loop(1, 8, z_sent, 0)
    x_a.wait_send()
    x_b.wait_send()
    x_c.wait_send()


def smem():
    return pl.BlockSpec(memory_space=pltpu.SMEM)


def vmem():
    return pl.BlockSpec(memory_space=pltpu.VMEM)


def hbm():
    return pl.BlockSpec(memory_space=pl.ANY)


def bf16(*shape):
    return jax.ShapeDtypeStruct(shape, jnp.bfloat16)


def f32(*shape):
    return jax.ShapeDtypeStruct(shape, jnp.float32)


def dma(*shape):
    return pltpu.SemaphoreType.DMA(shape)


def params(collective_id=None, vmem_mib=48):
    return pltpu.CompilerParams(
        collective_id=collective_id, has_side_effects=collective_id is not None, vmem_limit_bytes=vmem_mib << 20
    )


def gather_call(queries, exps, keys, values, outs, grads):
    return pl.pallas_call(
        gather_kernel,
        out_shape=(bf16(NQ, WIDE, DIM), bf16(NK, STRIPE, DIM), bf16(NK, STRIPE, DIM), f32(NQ, HEADS, STRIPE)),
        in_specs=[hbm()] * 6,
        out_specs=(hbm(),) * 4,
        scratch_shapes=[
            pltpu.VMEM((STRIPE, WIDE), jnp.bfloat16),
            pltpu.VMEM((1, STRIPE), jnp.int32),
            pltpu.VMEM((STRIPE, WIDE), jnp.bfloat16),
            pltpu.VMEM((STRIPE, WIDE), jnp.bfloat16),
            pltpu.VMEM((STRIPE, DIM), jnp.bfloat16),
            pltpu.VMEM((STRIPE, DIM), jnp.bfloat16),
            pltpu.VMEM((WIDE, DIM), jnp.bfloat16),
            pltpu.VMEM((HEADS, STRIPE), jnp.float32),
            dma(3), dma(4), dma(8, 2), dma(8), dma(8), dma(8),
            dma(8, 2), dma(8), dma(2, 2), dma(4, 2), dma(2), dma(4), dma(4),
            dma(3), dma(NQ), dma(3), dma(NQ), dma(4), dma(6),
        ],
        compiler_params=params(0, 8),
        name="gather",
    )(queries, exps, keys, values, outs, grads)


def stats_call(win, order, q, k):
    return pl.pallas_call(
        stats_kernel,
        out_shape=f32(2, NQ, WIDE),
        in_specs=[smem(), hbm()] + [vmem()] * 2,
        out_specs=vmem(),
        scratch_shapes=[
            pltpu.SMEM((256,), jnp.int32),
            pltpu.SemaphoreType.DMA,
            pltpu.SMEM((NK,), jnp.int32),
            pltpu.SMEM((NK + 1,), jnp.int32),
            pltpu.SMEM((NK + 1,), jnp.int32),
            pltpu.VMEM((8, WIDE), jnp.float32),
            pltpu.VMEM((8, WIDE), jnp.float32),
        ],
        compiler_params=params(None, 16),
        name="stats",
    )(win, order, q, k)


def norm_call(part):
    return pl.pallas_call(
        norm_kernel,
        out_shape=f32(NQ, WIDE),
        in_specs=[vmem()],
        out_specs=vmem(),
        scratch_shapes=[pltpu.VMEM((NQ, 2, NQ, WIDE), jnp.float32), dma(3), dma(NQ)],
        compiler_params=params(1, 4),
        name="norm",
    )(part)


def grads_call(win, order, q, k, v, norm, delta, *grads):
    return pl.pallas_call(
        grads_kernel,
        out_shape=(bf16(NQ, DIM, WIDE), bf16(NK, STRIPE, 2 * DIM)),
        in_specs=[smem(), hbm()] + [vmem()] * 9,
        out_specs=(vmem(), vmem()),
        scratch_shapes=[
            pltpu.SMEM((256,), jnp.int32),
            pltpu.SemaphoreType.DMA,
            pltpu.SMEM((NK,), jnp.int32),
            pltpu.SMEM((NK + 1,), jnp.int32),
            pltpu.SMEM((NK + 1,), jnp.int32),
            pltpu.VMEM((NQ, WIDE, DIM), jnp.bfloat16),
            pltpu.VMEM((NK, STRIPE, 2 * DIM), jnp.float32),
            pltpu.VMEM((DIM, WIDE), jnp.float32),
            pltpu.VMEM((2, WIDE), jnp.float32),
        ],
        compiler_params=params(None, 32),
        name="grads",
    )(win, order, q, k, v, norm, delta, *grads)


def reduce_call(dq, dkv):
    tile = (STRIPE, 2 * DIM)
    return pl.pallas_call(
        reduce_kernel,
        out_shape=(bf16(STRIPE, WIDE), bf16(STRIPE, DIM), bf16(STRIPE, DIM)),
        in_specs=[vmem()] * 2,
        out_specs=(vmem(), vmem(), vmem()),
        scratch_shapes=[
            pltpu.VMEM((32, *tile), jnp.bfloat16),
            pltpu.VMEM((32, *tile), jnp.bfloat16),
            pltpu.VMEM((8, *tile), jnp.bfloat16),
            pltpu.VMEM((8, *tile), jnp.bfloat16),
            pltpu.VMEM((8, *tile), jnp.bfloat16),
            pltpu.VMEM((8, *tile), jnp.bfloat16),
            pltpu.VMEM((DIM, WIDE), jnp.bfloat16),
            pltpu.VMEM((DIM, WIDE), jnp.bfloat16),
            pltpu.VMEM((DIM, WIDE), jnp.bfloat16),
            pltpu.VMEM((DIM, WIDE), jnp.bfloat16),
            dma(32), dma(32), dma(8), dma(8), dma(8), dma(8), dma(8), dma(8), dma(8), dma(8), dma(3), dma(3),
        ],
        compiler_params=params(2, 20),
        name="reduce",
    )(dq, dkv)


def per_device(
    queries, query_exps, key_head, value_head, forward_out, output_grad, stripe_order, window_size
):
    held = [pltpu.with_memory_space_constraint(a, pltpu.HBM) for a in (
        queries, query_exps.reshape(1, STRIPE), key_head, value_head, forward_out, output_grad, stripe_order
    )]
    grads = [output_grad] + [
        lax.ppermute(output_grad, "row", [(r, (r + 8 - 2 * n) % 8) for r in range(8)]) for n in (1, 2, 3)
    ]
    q, k, v, delta = gather_call(*held[:6])
    part = stats_call(window_size, held[6], q, k)
    norm = norm_call(part)
    dq, dkv = grads_call(window_size, held[6], q, k, v, norm, delta, *grads)
    return reduce_call(dq, dkv)


def solution(mesh):
    return jax.shard_map(
        per_device,
        mesh=mesh,
        in_specs=(
            P(("row", "col"), None),
            P(("row", "col")),
            P(("col", "row"), None),
            P(("col", "row"), None),
            P(("row", "col"), None),
            P(("row", "col"), None),
            P(),
            P(),
        ),
        out_specs=(P(("row", "col"), None), P(("col", "row"), None), P(("col", "row"), None)),
        check_vma=False,
    )
```

```python
import functools
import math

import jax
import jax.numpy as jnp
from jax import lax
from jax.experimental import pallas as pl
from jax.experimental.pallas import tpu as pltpu
from jax.sharding import PartitionSpec as P

STRIPE = 128
HEADS = 8
DIM = 128
WIDE = HEADS * STRIPE
NQ = 4
NK = 64
MESH = pl.DeviceIdType.MESH
NEG = -1e30
FAR = -(1 << 20)
SCALE = 1.0 / math.sqrt(DIM)
SCALE2 = math.log2(math.e) / math.sqrt(DIM)


def coords():
    row, col = lax.axis_index("row"), lax.axis_index("col")
    x, y, core = row // 2, col // 8, col % 2
    z = ((col // 2) % 4) * 2 + row % 2
    return x, y, z, core


def device(x, y, z, core):
    return (x * 2 + z % 2, y * 8 + (z // 2) * 2 + core)


def slot_of(y, z, core):
    return core * 32 + y * 8 + z


def key_positions(order, k_pos):
    row = lax.axis_index("row")

    def one(s, c):
        y, z, core = (s // 8) % 4, s % 8, s // 32
        stored = (y * 8 + (z // 2) * 2 + core) * 8 + (row // 2) * 2 + z % 2
        k_pos[s] = order[stored] * STRIPE
        return c

    lax.fori_loop(0, NK, one, 0, unroll=8)


def query_position(order, j):
    row, col = lax.axis_index("row"), lax.axis_index("col")
    return order[(j * 2 + row % 2) * 32 + col] * STRIPE


def build_list(q_at, k_pos, window, idx, gap):
    def one(k, n):
        distance = q_at - k_pos[k]
        seen = (distance >= 0) & (distance - (STRIPE - 1) < window)
        idx[n] = k
        gap[n] = distance
        return n + seen.astype(jnp.int32)

    n = lax.fori_loop(0, NK, one, jnp.int32(0), unroll=8)
    idx[n] = 0
    gap[n] = FAR
    return n


def over_list(n, step, most):
    done = 0
    while most > 2:
        full = n // most
        lax.fori_loop(done * 2 // most, full, lambda t, c, most=most: step(most, most * t, c), 0)
        done = full * (most // 2)
        most //= 2
    lax.fori_loop(done, (n + 1) // 2, lambda t, c: step(2, 2 * t, c), 0)


def tile_mask(gaps, window):
    delta = lax.broadcasted_iota(jnp.int32, (STRIPE, STRIPE), 1) - lax.broadcasted_iota(
        jnp.int32, (STRIPE, STRIPE), 0
    )
    parts = []
    for g in gaps:
        distance = delta + g
        parts.append((distance >= 0) & (distance < window))
    rows = jnp.concatenate(parts, axis=0)
    return jnp.concatenate([rows, rows], axis=1)


def dot_nt(a, b):
    return lax.dot_general(a, b, (((1,), (1,)), ((), ())), preferred_element_type=jnp.float32)


def dot_nn(a, b):
    return lax.dot_general(a, b, (((1,), (0,)), ((), ())), preferred_element_type=jnp.float32)


def fetch(src, dst, sem):
    copy = pltpu.make_async_copy(src, dst, sem)
    copy.start()
    copy.wait()


def stats_kernel(win, order_in, qg_ref, kv_ref, out_ref, order, order_sem, k_pos, idx, gap, m_ref, l_ref):
    window = win[0]
    fetch(order_in, order, order_sem)
    key_positions(order, k_pos)

    def per_query(j, carry):
        n = build_list(query_position(order, j), k_pos, window, idx, gap)
        m_ref[...] = jnp.full_like(m_ref, NEG)
        l_ref[...] = jnp.zeros_like(l_ref)

        def step(group, first, c):
            keys = jnp.concatenate([kv_ref[idx[first + i], 0] for i in range(group)], axis=0)
            mask = tile_mask([gap[first + i] for i in range(group)], window)
            for b in range(HEADS // 2):
                cols = pl.ds(b * 256, 256)
                s = dot_nt(keys, qg_ref[j, 0, cols, :])
                s = jnp.where(mask, s, NEG).reshape(group * 16, 8, 256)
                m_old = m_ref[:, cols]
                m_new = jnp.maximum(m_old, jnp.max(s, axis=0))
                e = jnp.exp2((s - m_new[None]) * SCALE2)
                l_ref[:, cols] = l_ref[:, cols] * jnp.exp2((m_old - m_new) * SCALE2) + jnp.sum(e, axis=0)
                m_ref[:, cols] = m_new
            return c

        over_list(n, step, 8)
        m_all = m_ref[...]
        top = jnp.max(m_all, axis=0, keepdims=True)
        total = jnp.sum(l_ref[...] * jnp.exp2((m_all - top) * SCALE2), axis=0, keepdims=True)
        out_ref[pl.ds(j, 1), :] = top * SCALE2 + jnp.log2(jnp.maximum(total, 1e-30))
        return carry

    lax.fori_loop(0, NQ, per_query, 0)


def grads_kernel(
    win, order_in, qg_ref, kv_ref, norm_ref, delta_ref, dq_ref, dkv_ref,
    order, order_sem, k_pos, idx, gap, acc_ref, dq_acc, stat_ref,
):
    window = win[0]
    load = pltpu.make_async_copy(order_in, order, order_sem)
    load.start()

    def clear(k, c):
        acc_ref[k] = jnp.zeros((STRIPE, 2 * DIM), jnp.float32)
        return c

    lax.fori_loop(0, NK, clear, 0)
    load.wait()
    key_positions(order, k_pos)

    def per_query(j, carry):
        n = build_list(query_position(order, j), k_pos, window, idx, gap)
        dq_acc[...] = jnp.zeros_like(dq_acc)
        stat_ref[0:1, :] = norm_ref[pl.ds(j, 1), :]
        for h in range(HEADS):
            stat_ref[1:2, h * DIM : (h + 1) * DIM] = delta_ref[j, h : h + 1, :]

        def step(group, first, c):
            at = [idx[first + i] for i in range(group)]
            keys = jnp.concatenate([kv_ref[i, 0] for i in at], axis=0)
            vals = jnp.concatenate([kv_ref[i, 1] for i in at], axis=0)
            keys_t = jnp.transpose(keys)
            mask = tile_mask([gap[first + i] for i in range(group)], window)
            weights, score_grads = [], []
            for b in range(HEADS // 2):
                cols = pl.ds(b * 256, 256)
                s = dot_nt(keys, qg_ref[j, 0, cols, :])
                p = jnp.where(mask, jnp.exp2(s * SCALE2 - stat_ref[0:1, cols]), 0.0)
                w = dot_nt(vals, qg_ref[j, 1, cols, :])
                score_grads.append((p * (w - stat_ref[1:2, cols])).astype(jnp.bfloat16))
                weights.append(p.astype(jnp.bfloat16))
            weights = jnp.concatenate(weights, axis=1)
            score_grads = jnp.concatenate(score_grads, axis=1)
            dv = dot_nn(weights, qg_ref[j, 1])
            dk = dot_nn(score_grads, qg_ref[j, 0])
            dq_acc[...] += dot_nn(keys_t, score_grads)
            for i, k in enumerate(at):
                rows = slice(i * STRIPE, (i + 1) * STRIPE)
                acc_ref[k, :, 0:DIM] += dk[rows]
                acc_ref[k, :, DIM:] += dv[rows]
            return c

        over_list(n, step, 4)
        dq_ref[j] = (dq_acc[...] * SCALE).astype(jnp.bfloat16)
        return carry

    lax.fori_loop(0, NQ, per_query, 0)

    def finish(k, c):
        dkv_ref[k, :, 0:DIM] = (acc_ref[k, :, 0:DIM] * SCALE).astype(jnp.bfloat16)
        dkv_ref[k, :, DIM:] = acc_ref[k, :, DIM:].astype(jnp.bfloat16)
        return c

    lax.fori_loop(0, NK, finish, 0)


def remote(src, dst, send_sem, recv_sem, to):
    return pltpu.make_async_remote_copy(
        src_ref=src, dst_ref=dst, send_sem=send_sem, recv_sem=recv_sem, device_id=to, device_id_type=MESH
    )


def greet(peers):
    barrier = pltpu.get_barrier_semaphore()
    for peer in peers:
        pl.semaphore_signal(barrier, inc=1, device_id=peer, device_id_type=MESH)
    pl.semaphore_wait(barrier, len(peers))


def plane_peers(x, y, z, core):
    peers = [device(x, y, z, 1 - core)]
    peers += [device((x + d) % 4, y, z, core) for d in (1, 3)]
    peers += [device(x, (y + d) % 4, z, core) for d in (1, 3)]
    peers += [device(x, y, (z + d) % 8, core) for d in range(1, 8)]
    return peers


def gather_kernel(
    q_in, exp_in, k_in, v_in, o_in, g_in, qg_out, kv_out, delta_out,
    q_ref, exp_ref, o_ref, g_ref, kv_own, qg_own, delta_own,
    kv_recv, z_send, y_send, y_pass, sib_send, x_send, x_pass, x_recv, d_send, d_recv, local, load,
):
    loads = [
        pltpu.make_async_copy(src, dst, load.at[n])
        for n, (src, dst) in enumerate(
            ((k_in, kv_own.at[0]), (v_in, kv_own.at[1]), (exp_in, exp_ref), (q_in, q_ref), (g_in, g_ref), (o_in, o_ref))
        )
    ]
    for copy in loads:
        copy.start()

    x, y, z, core = coords()
    mine = slot_of(y, z, core)
    sibling = device(x, y, z, 1 - core)
    y_up, y_down = (y + 1) % 4, (y + 3) % 4
    sign = 1 - 2 * core
    x_to, x_from = (x + sign + 4) % 4, (x - sign + 4) % 4

    greet(
        [device(x, y, z, 1 - core)]
        + [device((x + d) % 4, y, z, core) for d in (1, 3, 2)]
        + [device(x, (y + d) % 4, z, core) for d in (1, 3)]
        + [device(x, y, (z + d) % 8, core) for d in (1, 7)]
    )

    def slot_copy(s, src, send, to):
        return remote(src, kv_out.at[s], send, kv_recv.at[s], to)

    def arrived(s):
        slot_copy(s, kv_own, local.at[0], sibling).wait_recv()

    y_far = (y + 2) % 4

    def z_copy(d, src, up, far=0):
        to = device(x, y, (z + (1 if up else 7)) % 8, core)
        s = slot_of(y_far if far else y, (z + d) % 8, core)
        return slot_copy(s, src, z_send.at[far, d, 0 if up else 1], to)

    def y_copy(d, src, up):
        to = device(x, y_up if up else y_down, z, core)
        return slot_copy(slot_of(y, (z + d) % 8, core), src, y_send.at[d, 0 if up else 1], to)

    def y_onward():
        s = slot_of((y - sign + 4) % 4, z, core)
        return slot_copy(s, kv_out.at[s], y_pass, device(x, (y + sign + 4) % 4, z, core))

    def sib_copy(s, src):
        return slot_copy(s, src, sib_send.at[s % 32], sibling)

    def spread(d, src):
        y_copy(d, src, True).start()
        y_copy(d, src, False).start()
        sib_copy(slot_of(y, (z + d) % 8, core), src).start()

    loads[0].wait()
    loads[1].wait()
    z_copy(0, kv_own, True).start()
    z_copy(0, kv_own, False).start()
    spread(0, kv_own)

    loads[2].wait()
    loads[3].wait()
    scale = jnp.transpose(jnp.broadcast_to(jnp.exp2(exp_ref[...].astype(jnp.float32)), (STRIPE, STRIPE)))

    def x_copy(p, n):
        to = device((x + 1 + 2 * n) % 4, y, z, core)
        return remote(qg_own.at[p], qg_out.at[x, p], x_send.at[p, n], x_recv.at[x, p], to)

    for h in range(HEADS):
        cols = slice(h * DIM, (h + 1) * DIM)
        qg_own[0, cols, :] = (q_ref[:, cols].astype(jnp.float32) * scale).astype(jnp.bfloat16)
    x_copy(0, 0).start()
    x_copy(0, 1).start()
    loads[4].wait()
    for h in range(HEADS):
        cols = slice(h * DIM, (h + 1) * DIM)
        qg_own[1, cols, :] = g_ref[:, cols]
    x_copy(1, 0).start()
    x_copy(1, 1).start()

    def x_arrived(who, p):
        remote(qg_own.at[p], qg_out.at[who, p], local.at[0], x_recv.at[who, p], sibling).wait_recv()

    def x_forward(p):
        block = qg_out.at[x_from, p]
        return remote(block, block, x_pass.at[p], x_recv.at[x_from, p], device(x_to, y, z, core))

    def from_z(d, up, onward):
        s = slot_of(y, (z + d) % 8, core)
        arrived(s)
        if onward is True:
            z_copy(d, kv_out.at[s], up).start()
        elif onward is not None:
            @pl.when(onward)
            def _():
                z_copy(d, kv_out.at[s], up).start()
        spread(d, kv_out.at[s])

    def from_y(d):
        zz = (z + d) % 8
        for yy in (y_down, y_up):
            s = slot_of(yy, zz, core)
            arrived(s)
            if d == 0:
                @pl.when(yy == (y - sign + 4) % 4)
                def _():
                    y_onward().start()
            sib_copy(s, kv_out.at[s]).start()

    def from_far(d, up, onward):
        s = slot_of(y_far, (z + d) % 8, core)
        arrived(s)
        if onward is True:
            z_copy(d, kv_out.at[s], up, 1).start()
        elif onward is not None:
            @pl.when(onward)
            def _():
                z_copy(d, kv_out.at[s], up, 1).start()
        sib_copy(s, kv_out.at[s]).start()

    from_z(7, True, True)
    from_z(1, False, True)
    from_y(0)

    own_kv = pltpu.make_async_copy(kv_own, kv_out.at[mine], local.at[0])
    own_qg = pltpu.make_async_copy(qg_own, qg_out.at[x], local.at[1])
    own_kv.start()
    own_qg.start()

    from_z(6, True, True)
    from_z(2, False, True)
    from_far(0, True, True)
    z_copy(0, kv_out.at[slot_of(y_far, z, core)], False, 1).start()
    from_z(5, True, core == 0)
    from_z(3, False, core == 1)
    from_y(1)
    from_y(7)
    from_far(7, True, True)
    from_far(1, False, True)
    from_z(4, True, None)
    x_arrived(x_from, 0)
    x_forward(0).start()

    loads[5].wait()
    for h in range(HEADS):
        cols = slice(h * DIM, (h + 1) * DIM)
        product = g_ref[:, cols].astype(jnp.float32) * o_ref[:, cols].astype(jnp.float32)
        sums = jnp.sum(jnp.transpose(product), axis=0, keepdims=True)
        delta_own[h : h + 1, :] = sums.astype(jnp.bfloat16).astype(jnp.float32)

    def d_copy(n):
        return remote(delta_own, delta_out.at[x], d_send.at[n], d_recv.at[x], device((x + 1 + n) % 4, y, z, core))

    for n in range(3):
        d_copy(n).start()
    own_delta = pltpu.make_async_copy(delta_own, delta_out.at[x], local.at[2])
    own_delta.start()

    from_y(2)
    from_y(6)
    from_far(6, True, True)
    from_far(2, False, True)
    x_arrived(x_from, 1)
    x_forward(1).start()
    from_y(3)
    from_y(5)
    from_far(5, True, core == 0)
    from_far(3, False, core == 1)
    from_y(4)
    from_far(4, True, None)

    for p in range(2):
        x_arrived(x_to, p)
        x_arrived((x + 2) % 4, p)
    for n in range(1, 4):
        who = (x + n) % 4
        remote(delta_own, delta_out.at[who], local.at[0], d_recv.at[who], sibling).wait_recv()

    def from_sibling(s, c):
        arrived((1 - core) * 32 + s)
        return c

    lax.fori_loop(0, 32, from_sibling, 0)

    def sent(d, c):
        y_copy(d, kv_own, True).wait_send()
        y_copy(d, kv_own, False).wait_send()
        return c

    lax.fori_loop(0, 8, sent, 0)

    def sib_sent(s, c):
        sib_copy(s, kv_own).wait_send()
        return c

    lax.fori_loop(0, 32, sib_sent, 0)
    y_onward().wait_send()
    for far in range(2):
        for d, up in ((0, True), (0, False), (7, True), (1, False), (6, True), (2, False)):
            z_copy(d, kv_own, up, far).wait_send()

    @pl.when(core == 0)
    def _():
        z_copy(5, kv_own, True, 0).wait_send()
        z_copy(5, kv_own, True, 1).wait_send()

    @pl.when(core == 1)
    def _():
        z_copy(3, kv_own, False, 0).wait_send()
        z_copy(3, kv_own, False, 1).wait_send()

    for p in range(2):
        x_copy(p, 0).wait_send()
        x_copy(p, 1).wait_send()
        x_forward(p).wait_send()
    for n in range(3):
        d_copy(n).wait_send()
    own_kv.wait()
    own_qg.wait()
    own_delta.wait()


def norm_kernel(part_ref, out_ref, got, send, recv):
    x, y, z, core = coords()
    peers = [device((x + d) % 4, y, z, core) for d in (1, 3, 2)]
    greet(peers)

    def copy(n):
        return remote(part_ref, got.at[x], send.at[n], recv.at[x], peers[n])

    for n in range(3):
        copy(n).start()
    for n in range(1, 4):
        who = (x + n) % 4
        remote(part_ref, got.at[who], send.at[0], recv.at[who], peers[0]).wait_recv()
    logs = [part_ref[...]] + [got[(x + n) % 4] for n in range(1, 4)]
    top = functools.reduce(jnp.maximum, logs)
    out_ref[...] = top + jnp.log2(functools.reduce(jnp.add, [jnp.exp2(v - top) for v in logs]))
    for n in range(3):
        copy(n).wait_send()


def reduce_kernel(
    dq_ref, kv_ref, dq_out, dk_out, dv_out,
    sib_got, kv_sum, opp_got, near_got, far_got, z_got, x_opp, x_near, x_far, x_sum,
    sib_send, sib_recv, a_send, a_recv, b_send, b_recv, c_send, c_recv, z_send, z_recv, x_send, x_recv,
):
    x, y, z, core = coords()
    sign = 1 - 2 * core
    sibling = device(x, y, z, 1 - core)
    y_to, y_back, y_opp = (y + sign + 4) % 4, (y - sign + 4) % 4, (y + 2) % 4
    x_to, x_back, x_over = (x + sign + 4) % 4, (x - sign + 4) % 4, (x + 2) % 4
    to_next, to_back = device(x, y_to, z, core), device(x, y_back, z, core)
    dev_to, dev_back = device(x_to, y, z, core), device(x_back, y, z, core)

    greet(plane_peers(x, y, z, core))

    def add(*parts):
        return functools.reduce(jnp.add, [p.astype(jnp.float32) for p in parts])

    def sib_copy(s):
        return remote(kv_ref.at[(1 - core) * 32 + s], sib_got.at[s], sib_send.at[s], sib_recv.at[s], sibling)

    far_first = (4, 3, 5, 2, 6, 1, 7, 0)

    x_a = remote(dq_ref.at[x_over], x_opp, x_send.at[0], x_recv.at[0], dev_to)
    x_b = remote(dq_ref.at[x_back], x_near, x_send.at[1], x_recv.at[1], dev_back)
    x_c = remote(x_sum, x_far, x_send.at[2], x_recv.at[2], dev_to)
    for d in far_first:
        zz = (z + d) % 8
        for yy in (y_opp, y_back, y_to, y):
            sib_copy(yy * 8 + zz).start()
        if d == 3:
            x_a.start()
            x_b.start()

    def with_sibling(s):
        sib_copy(s).wait_recv()
        return add(kv_ref[core * 32 + s], sib_got[s])

    def a_copy(zz):
        return remote(kv_sum.at[y_opp * 8 + zz], opp_got.at[zz], a_send.at[zz], a_recv.at[zz], to_next)

    def b_copy(zz):
        return remote(kv_sum.at[y_back * 8 + zz], near_got.at[zz], b_send.at[zz], b_recv.at[zz], to_back)

    def c_copy(zz):
        return remote(kv_sum.at[y_to * 8 + zz], far_got.at[zz], c_send.at[zz], c_recv.at[zz], to_next)

    def z_copy(zz):
        return remote(kv_sum.at[y * 8 + zz], z_got.at[z], z_send.at[zz], z_recv.at[z], device(x, y, zz, core))

    def step_a(d):
        zz = (z + d) % 8
        s = y_opp * 8 + zz
        kv_sum[s] = with_sibling(s).astype(jnp.bfloat16)
        a_copy(zz).start()

    def step_b(d):
        zz = (z + d) % 8
        s = y_back * 8 + zz
        kv_sum[s] = with_sibling(s).astype(jnp.bfloat16)
        b_copy(zz).start()

    def step_c(d):
        zz = (z + d) % 8
        s = y_to * 8 + zz
        total = with_sibling(s)
        a_copy(zz).wait_recv()
        kv_sum[s] = add(total, opp_got[zz]).astype(jnp.bfloat16)
        c_copy(zz).start()

    def total_here(zz):
        s = y * 8 + zz
        total = with_sibling(s)
        b_copy(zz).wait_recv()
        c_copy(zz).wait_recv()
        return add(total, near_got[zz], far_got[zz])

    def step_z(d):
        zz = (z + d) % 8
        kv_sum[y * 8 + zz] = total_here(zz).astype(jnp.bfloat16)
        z_copy(zz).start()

    def sum_x(h, c):
        rows = pl.ds(pl.multiple_of(h * 16, 16), 16)
        x_sum[rows, :] = add(dq_ref[x_to, rows, :], x_opp[rows, :]).astype(jnp.bfloat16)
        return c

    for n in range(11):
        if n < 8:
            step_a(far_first[n])
            step_b(far_first[n])
        if 0 <= n - 1 < 8:
            step_c(far_first[n - 1])
        if 0 <= n - 3 < 7:
            step_z(far_first[n - 3])
        if n == 6:
            x_a.wait_recv()
            lax.fori_loop(0, 8, sum_x, 0)
            x_c.start()

    x_b.wait_recv()
    x_c.wait_recv()
    for h in range(HEADS):
        cols = slice(h * DIM, (h + 1) * DIM)
        total = add(dq_ref[x, :, cols], x_near[:, cols], x_far[:, cols])
        dq_out[:, cols] = jnp.transpose(total).astype(jnp.bfloat16)

    total = total_here(z)
    for d in range(1, 8):
        who = (z + d) % 8
        remote(kv_sum.at[0], z_got.at[who], z_send.at[0], z_recv.at[who], sibling).wait_recv()
        total = add(total, z_got[who])
    dk_out[...] = total[:, 0:DIM].astype(jnp.bfloat16)
    dv_out[...] = total[:, DIM:].astype(jnp.bfloat16)

    def sib_sent(s, c):
        sib_copy(s).wait_send()
        return c

    lax.fori_loop(0, 32, sib_sent, 0)

    def sent(d, c):
        zz = (z + d) % 8
        a_copy(zz).wait_send()
        b_copy(zz).wait_send()
        c_copy(zz).wait_send()
        return c

    lax.fori_loop(0, 8, sent, 0)

    def z_sent(d, c):
        z_copy((z + d) % 8).wait_send()
        return c

    lax.fori_loop(1, 8, z_sent, 0)
    x_a.wait_send()
    x_b.wait_send()
    x_c.wait_send()


def smem():
    return pl.BlockSpec(memory_space=pltpu.SMEM)


def vmem():
    return pl.BlockSpec(memory_space=pltpu.VMEM)


def hbm():
    return pl.BlockSpec(memory_space=pl.ANY)


def bf16(*shape):
    return jax.ShapeDtypeStruct(shape, jnp.bfloat16)


def f32(*shape):
    return jax.ShapeDtypeStruct(shape, jnp.float32)


def dma(*shape):
    return pltpu.SemaphoreType.DMA(shape)


def params(collective_id=None, vmem_mib=48):
    return pltpu.CompilerParams(
        collective_id=collective_id, has_side_effects=collective_id is not None, vmem_limit_bytes=vmem_mib << 20
    )


def gather_call(queries, exps, keys, values, outs, grads):
    return pl.pallas_call(
        gather_kernel,
        out_shape=(bf16(NQ, 2, WIDE, DIM), bf16(NK, 2, STRIPE, DIM), f32(NQ, HEADS, STRIPE)),
        in_specs=[hbm()] * 6,
        out_specs=(hbm(), hbm(), hbm()),
        scratch_shapes=[
            pltpu.VMEM((STRIPE, WIDE), jnp.bfloat16),
            pltpu.VMEM((1, STRIPE), jnp.int32),
            pltpu.VMEM((STRIPE, WIDE), jnp.bfloat16),
            pltpu.VMEM((STRIPE, WIDE), jnp.bfloat16),
            pltpu.VMEM((2, STRIPE, DIM), jnp.bfloat16),
            pltpu.VMEM((2, WIDE, DIM), jnp.bfloat16),
            pltpu.VMEM((HEADS, STRIPE), jnp.float32),
            dma(NK), dma(2, 8, 2), dma(8, 2), pltpu.SemaphoreType.DMA, dma(32), dma(2, 2), dma(2), dma(NQ, 2), dma(3), dma(NQ), dma(3), dma(6),
        ],
        compiler_params=params(0, 8),
        name="gather",
    )(queries, exps, keys, values, outs, grads)


def stats_call(win, order, qg, kv):
    return pl.pallas_call(
        stats_kernel,
        out_shape=f32(NQ, WIDE),
        in_specs=[smem(), hbm()] + [vmem()] * 2,
        out_specs=vmem(),
        scratch_shapes=[
            pltpu.SMEM((256,), jnp.int32),
            pltpu.SemaphoreType.DMA,
            pltpu.SMEM((NK,), jnp.int32),
            pltpu.SMEM((NK + 1,), jnp.int32),
            pltpu.SMEM((NK + 1,), jnp.int32),
            pltpu.VMEM((8, WIDE), jnp.float32),
            pltpu.VMEM((8, WIDE), jnp.float32),
        ],
        compiler_params=params(None, 16),
        name="stats",
    )(win, order, qg, kv)


def norm_call(part):
    return pl.pallas_call(
        norm_kernel,
        out_shape=f32(NQ, WIDE),
        in_specs=[vmem()],
        out_specs=vmem(),
        scratch_shapes=[pltpu.VMEM((NQ, NQ, WIDE), jnp.float32), dma(3), dma(NQ)],
        compiler_params=params(1, 4),
        name="norm",
    )(part)


def grads_call(win, order, qg, kv, norm, delta):
    return pl.pallas_call(
        grads_kernel,
        out_shape=(bf16(NQ, DIM, WIDE), bf16(NK, STRIPE, 2 * DIM)),
        in_specs=[smem(), hbm()] + [vmem()] * 4,
        out_specs=(vmem(), vmem()),
        scratch_shapes=[
            pltpu.SMEM((256,), jnp.int32),
            pltpu.SemaphoreType.DMA,
            pltpu.SMEM((NK,), jnp.int32),
            pltpu.SMEM((NK + 1,), jnp.int32),
            pltpu.SMEM((NK + 1,), jnp.int32),
            pltpu.VMEM((NK, STRIPE, 2 * DIM), jnp.float32),
            pltpu.VMEM((DIM, WIDE), jnp.float32),
            pltpu.VMEM((2, WIDE), jnp.float32),
        ],
        compiler_params=params(None, 32),
        name="grads",
    )(win, order, qg, kv, norm, delta)


def reduce_call(dq, dkv):
    tile = (STRIPE, 2 * DIM)
    return pl.pallas_call(
        reduce_kernel,
        out_shape=(bf16(STRIPE, WIDE), bf16(STRIPE, DIM), bf16(STRIPE, DIM)),
        in_specs=[vmem()] * 2,
        out_specs=(vmem(), vmem(), vmem()),
        scratch_shapes=[
            pltpu.VMEM((32, *tile), jnp.bfloat16),
            pltpu.VMEM((32, *tile), jnp.bfloat16),
            pltpu.VMEM((8, *tile), jnp.bfloat16),
            pltpu.VMEM((8, *tile), jnp.bfloat16),
            pltpu.VMEM((8, *tile), jnp.bfloat16),
            pltpu.VMEM((8, *tile), jnp.bfloat16),
            pltpu.VMEM((DIM, WIDE), jnp.bfloat16),
            pltpu.VMEM((DIM, WIDE), jnp.bfloat16),
            pltpu.VMEM((DIM, WIDE), jnp.bfloat16),
            pltpu.VMEM((DIM, WIDE), jnp.bfloat16),
            dma(32), dma(32), dma(8), dma(8), dma(8), dma(8), dma(8), dma(8), dma(8), dma(8), dma(3), dma(3),
        ],
        compiler_params=params(2, 20),
        name="reduce",
    )(dq, dkv)


def per_device(
    queries, query_exps, key_head, value_head, forward_out, output_grad, stripe_order, window_size
):
    held = [
        pltpu.with_memory_space_constraint(a, pltpu.HBM)
        for a in (
            queries, query_exps.reshape(1, STRIPE), key_head, value_head, forward_out, output_grad, stripe_order
        )
    ]
    qg, kv, delta = gather_call(*held[:6])
    part = stats_call(window_size, held[6], qg, kv)
    norm = norm_call(part)
    dq, dkv = grads_call(window_size, held[6], qg, kv, norm, delta)
    return reduce_call(dq, dkv)


def solution(mesh):
    return jax.shard_map(
        per_device,
        mesh=mesh,
        in_specs=(
            P(("row", "col"), None),
            P(("row", "col")),
            P(("col", "row"), None),
            P(("col", "row"), None),
            P(("row", "col"), None),
            P(("row", "col"), None),
            P(),
            P(),
        ),
        out_specs=(P(("row", "col"), None), P(("col", "row"), None), P(("col", "row"), None)),
        check_vma=False,
    )
```

```python
import functools
import math

import jax
import jax.numpy as jnp
from jax import lax
from jax.experimental import pallas as pl
from jax.experimental.pallas import tpu as pltpu
from jax.sharding import PartitionSpec as P

STRIPE = 128
HEADS = 8
DIM = 128
WIDE = HEADS * STRIPE
NQ = 4
NK = 64
MESH = pl.DeviceIdType.MESH
NEG = -1e30
LIMIT = 2.0**100
FAR = -(1 << 20)
SCALE = 1.0 / math.sqrt(DIM)
SCALE2 = math.log2(math.e) / math.sqrt(DIM)


def coords():
    row, col = lax.axis_index("row"), lax.axis_index("col")
    x, y, core = row // 2, col // 8, col % 2
    z = ((col // 2) % 4) * 2 + row % 2
    return x, y, z, core


def device(x, y, z, core):
    return (x * 2 + z % 2, y * 8 + (z // 2) * 2 + core)


def slot_of(y, z, core):
    return core * 32 + y * 8 + z


def key_positions(order, k_pos):
    row = lax.axis_index("row")

    def one(s, c):
        y, z, core = (s // 8) % 4, s % 8, s // 32
        stored = (y * 8 + (z // 2) * 2 + core) * 8 + (row // 2) * 2 + z % 2
        k_pos[s] = order[stored] * STRIPE
        return c

    lax.fori_loop(0, NK, one, 0, unroll=8)


def query_position(order, j):
    row, col = lax.axis_index("row"), lax.axis_index("col")
    return order[(j * 2 + row % 2) * 32 + col] * STRIPE


def build_list(q_at, k_pos, window, idx, gap):
    def one(k, n):
        distance = q_at - k_pos[k]
        seen = (distance >= 0) & (distance - (STRIPE - 1) < window)
        idx[n] = k
        gap[n] = distance
        return n + seen.astype(jnp.int32)

    n = lax.fori_loop(0, NK, one, jnp.int32(0), unroll=8)
    idx[n] = 0
    gap[n] = FAR
    return n


def over_list(n, step, most):
    done = 0
    while most > 2:
        full = n // most
        lax.fori_loop(done * 2 // most, full, lambda t, c, most=most: step(most, most * t, c), 0)
        done = full * (most // 2)
        most //= 2
    lax.fori_loop(done, (n + 1) // 2, lambda t, c: step(2, 2 * t, c), 0)


def tile_mask(gaps, window):
    delta = lax.broadcasted_iota(jnp.int32, (STRIPE, STRIPE), 1) - lax.broadcasted_iota(
        jnp.int32, (STRIPE, STRIPE), 0
    )
    parts = []
    for g in gaps:
        distance = delta + g
        parts.append((distance >= 0) & (distance < window))
    rows = jnp.concatenate(parts, axis=0)
    return jnp.concatenate([rows, rows], axis=1)


def dot_nt(a, b):
    return lax.dot_general(a, b, (((1,), (1,)), ((), ())), preferred_element_type=jnp.float32)


def dot_nn(a, b):
    return lax.dot_general(a, b, (((1,), (0,)), ((), ())), preferred_element_type=jnp.float32)


def fetch(src, dst, sem):
    copy = pltpu.make_async_copy(src, dst, sem)
    copy.start()
    copy.wait()


def stats_kernel(win, order_in, qg_ref, kv_ref, out_ref, order, order_sem, k_pos, idx, gap, m_ref, l_ref):
    window = win[0]
    fetch(order_in, order, order_sem)
    key_positions(order, k_pos)

    def per_query(j, carry):
        n = build_list(query_position(order, j), k_pos, window, idx, gap)

        def scores(group, first, b):
            keys = jnp.concatenate([kv_ref[idx[first + i], 0] for i in range(group)], axis=0)
            return dot_nt(keys, qg_ref[j, 0, pl.ds(b * 256, 256), :])

        def restart():
            m_ref[...] = jnp.full_like(m_ref, NEG)
            l_ref[...] = jnp.zeros_like(l_ref)

        def online(group, first, c=0):
            mask = tile_mask([gap[first + i] for i in range(group)], window)
            for b in range(HEADS // 2):
                cols = pl.ds(b * 256, 256)
                s = jnp.where(mask, scores(group, first, b), NEG).reshape(group * 16, 8, 256)
                m_old = m_ref[:, cols]
                m_new = jnp.maximum(m_old, jnp.max(s, axis=0))
                e = jnp.exp2((s - m_new[None]) * SCALE2)
                l_ref[:, cols] = l_ref[:, cols] * jnp.exp2((m_old - m_new) * SCALE2) + jnp.sum(e, axis=0)
                m_ref[:, cols] = m_new
            return c

        def settle():
            m_all = m_ref[...]
            top = jnp.max(m_all, axis=0, keepdims=True)
            l_ref[...] = l_ref[...] * jnp.exp2((m_all - top) * SCALE2)
            m_ref[...] = jnp.broadcast_to(top * SCALE2, m_all.shape)

        def shifted(group, first, c=0):
            gaps = [gap[first + i] for i in range(group)]

            def add(masked):
                mask = tile_mask(gaps, window) if masked else None
                for b in range(HEADS // 2):
                    cols = pl.ds(b * 256, 256)
                    s = scores(group, first, b)
                    s = jnp.where(mask, s, NEG) if masked else s
                    e = jnp.exp2(s.reshape(group * 16, 8, 256) * SCALE2 - m_ref[:, cols][None])
                    l_ref[:, cols] += jnp.sum(e, axis=0)

            whole = functools.reduce(
                jnp.logical_and, [(g >= STRIPE) & (g <= window - STRIPE) for g in gaps]
            )
            pl.when(whole)(lambda: add(False))
            pl.when(jnp.logical_not(whole))(lambda: add(True))
            return c

        restart()
        pl.when(n >= 8)(lambda: online(8, 0) or None)
        pl.when((n >= 4) & (n < 8))(lambda: online(4, 0) or None)
        pl.when((n >= 1) & (n < 4))(lambda: online(2, 0) or None)
        settle()
        eights, fours = n // 8, n // 4
        lax.fori_loop(1, eights, lambda t, c: shifted(8, 8 * t, c), 0)
        lax.fori_loop(jnp.where(n >= 8, 2 * eights, 1), fours, lambda t, c: shifted(4, 4 * t, c), 0)
        lax.fori_loop(jnp.where(n >= 4, 2 * fours, 1), (n + 1) // 2, lambda t, c: shifted(2, 2 * t, c), 0)

        @pl.when(jnp.max(l_ref[...]) > LIMIT)
        def _():
            restart()
            over_list(n, online, 8)
            settle()

        total = jnp.sum(l_ref[...], axis=0, keepdims=True)
        out_ref[pl.ds(j, 1), :] = m_ref[0:1, :] + jnp.log2(jnp.maximum(total, 1e-30))
        return carry

    lax.fori_loop(0, NQ, per_query, 0)


def grads_kernel(
    win, order_in, qg_ref, kv_ref, norm_ref, delta_ref, dq_ref, dkv_ref,
    order, order_sem, k_pos, idx, gap, acc_ref, dq_acc, stat_ref,
):
    window = win[0]
    load = pltpu.make_async_copy(order_in, order, order_sem)
    load.start()

    def clear(k, c):
        acc_ref[k] = jnp.zeros((STRIPE, 2 * DIM), jnp.float32)
        return c

    lax.fori_loop(0, NK, clear, 0)
    load.wait()
    key_positions(order, k_pos)

    def per_query(j, carry):
        n = build_list(query_position(order, j), k_pos, window, idx, gap)
        dq_acc[...] = jnp.zeros_like(dq_acc)
        stat_ref[0:1, :] = norm_ref[pl.ds(j, 1), :]
        for h in range(HEADS):
            stat_ref[1:2, h * DIM : (h + 1) * DIM] = delta_ref[j, h : h + 1, :]

        def step(group, first, c):
            at = [idx[first + i] for i in range(group)]
            keys = jnp.concatenate([kv_ref[i, 0] for i in at], axis=0)
            vals = jnp.concatenate([kv_ref[i, 1] for i in at], axis=0)
            keys_t = jnp.transpose(keys)
            mask = tile_mask([gap[first + i] for i in range(group)], window)
            weights, score_grads = [], []
            for b in range(HEADS // 2):
                cols = pl.ds(b * 256, 256)
                s = dot_nt(keys, qg_ref[j, 0, cols, :])
                p = jnp.where(mask, jnp.exp2(s * SCALE2 - stat_ref[0:1, cols]), 0.0)
                w = dot_nt(vals, qg_ref[j, 1, cols, :])
                score_grads.append((p * (w - stat_ref[1:2, cols])).astype(jnp.bfloat16))
                weights.append(p.astype(jnp.bfloat16))
            weights = jnp.concatenate(weights, axis=1)
            score_grads = jnp.concatenate(score_grads, axis=1)
            dv = dot_nn(weights, qg_ref[j, 1])
            dk = dot_nn(score_grads, qg_ref[j, 0])
            dq_acc[...] += dot_nn(keys_t, score_grads)
            for i, k in enumerate(at):
                rows = slice(i * STRIPE, (i + 1) * STRIPE)
                acc_ref[k, :, 0:DIM] += dk[rows]
                acc_ref[k, :, DIM:] += dv[rows]
            return c

        over_list(n, step, 4)
        dq_ref[j] = (dq_acc[...] * SCALE).astype(jnp.bfloat16)
        return carry

    lax.fori_loop(0, NQ, per_query, 0)

    def finish(k, c):
        dkv_ref[k, :, 0:DIM] = (acc_ref[k, :, 0:DIM] * SCALE).astype(jnp.bfloat16)
        dkv_ref[k, :, DIM:] = acc_ref[k, :, DIM:].astype(jnp.bfloat16)
        return c

    lax.fori_loop(0, NK, finish, 0)


def remote(src, dst, send_sem, recv_sem, to):
    return pltpu.make_async_remote_copy(
        src_ref=src, dst_ref=dst, send_sem=send_sem, recv_sem=recv_sem, device_id=to, device_id_type=MESH
    )


def greet(peers):
    barrier = pltpu.get_barrier_semaphore()
    for peer in peers:
        pl.semaphore_signal(barrier, inc=1, device_id=peer, device_id_type=MESH)
    pl.semaphore_wait(barrier, len(peers))


def plane_peers(x, y, z, core):
    peers = [device(x, y, z, 1 - core)]
    peers += [device((x + d) % 4, y, z, core) for d in (1, 3)]
    peers += [device(x, (y + d) % 4, z, core) for d in (1, 3)]
    peers += [device(x, y, (z + d) % 8, core) for d in range(1, 8)]
    return peers


def gather_kernel(
    q_in, exp_in, k_in, v_in, o_in, g_in, qg_out, kv_out, delta_out,
    q_ref, exp_ref, o_ref, g_ref, kv_own, qg_own, delta_own,
    kv_recv, z_send, y_send, y_pass, sib_send, x_send, x_pass, x_recv, d_send, d_recv, local, load,
):
    loads = [
        pltpu.make_async_copy(src, dst, load.at[n])
        for n, (src, dst) in enumerate(
            ((k_in, kv_own.at[0]), (v_in, kv_own.at[1]), (exp_in, exp_ref), (q_in, q_ref), (g_in, g_ref), (o_in, o_ref))
        )
    ]
    for copy in loads:
        copy.start()

    x, y, z, core = coords()
    mine = slot_of(y, z, core)
    sibling = device(x, y, z, 1 - core)
    y_up, y_down = (y + 1) % 4, (y + 3) % 4
    sign = 1 - 2 * core
    x_to, x_from = (x + sign + 4) % 4, (x - sign + 4) % 4

    greet(
        [device(x, y, z, 1 - core)]
        + [device((x + d) % 4, y, z, core) for d in (1, 3, 2)]
        + [device(x, (y + d) % 4, z, core) for d in (1, 3, 2)]
        + [device(x, y, (z + d) % 8, core) for d in (1, 7, 2, 6)]
    )

    def slot_copy(s, src, send, to):
        return remote(src, kv_out.at[s], send, kv_recv.at[s], to)

    def arrived(s):
        slot_copy(s, kv_own, local.at[0], sibling).wait_recv()

    y_far = (y + 2) % 4
    z_steps = (1, 7, 2, 6)

    def z_copy(d, src, n, far=0):
        to = device(x, y, (z + z_steps[n]) % 8, core)
        s = slot_of(y_far if far else y, (z + d) % 8, core)
        return slot_copy(s, src, z_send.at[far, d, n], to)

    def y_copy(d, src, up):
        to = device(x, y_up if up else y_down, z, core)
        return slot_copy(slot_of(y, (z + d) % 8, core), src, y_send.at[d, 0 if up else 1], to)

    def far_copy():
        return slot_copy(mine, kv_own, y_pass, device(x, y_far, z, core))

    def sib_copy(s, src):
        return slot_copy(s, src, sib_send.at[s % 32], sibling)

    def spread(d, src):
        y_copy(d, src, True).start()
        y_copy(d, src, False).start()
        sib_copy(slot_of(y, (z + d) % 8, core), src).start()

    loads[0].wait()
    loads[1].wait()
    for n in range(4):
        z_copy(0, kv_own, n).start()
    far_copy().start()
    spread(0, kv_own)

    loads[2].wait()
    loads[3].wait()
    scale = jnp.transpose(jnp.broadcast_to(jnp.exp2(exp_ref[...].astype(jnp.float32)), (STRIPE, STRIPE)))

    def x_copy(p, n):
        to = device((x + 1 + 2 * n) % 4, y, z, core)
        return remote(qg_own.at[p], qg_out.at[x, p], x_send.at[p, n], x_recv.at[x, p], to)

    for h in range(HEADS):
        cols = slice(h * DIM, (h + 1) * DIM)
        qg_own[0, cols, :] = (q_ref[:, cols].astype(jnp.float32) * scale).astype(jnp.bfloat16)
    x_copy(0, 0).start()
    x_copy(0, 1).start()
    loads[4].wait()
    for h in range(HEADS):
        cols = slice(h * DIM, (h + 1) * DIM)
        qg_own[1, cols, :] = g_ref[:, cols]
    x_copy(1, 0).start()
    x_copy(1, 1).start()

    def x_arrived(who, p):
        remote(qg_own.at[p], qg_out.at[who, p], local.at[0], x_recv.at[who, p], sibling).wait_recv()

    def x_forward(p):
        block = qg_out.at[x_from, p]
        return remote(block, block, x_pass.at[p], x_recv.at[x_from, p], device(x_to, y, z, core))

    def onward(d, n, far):
        s = slot_of(y_far if far else y, (z + d) % 8, core)
        if d in (6, 2):
            z_copy(d, kv_out.at[s], n, far).start()
        elif d in (5, 3):
            @pl.when(core == n)
            def _():
                z_copy(d, kv_out.at[s], n, far).start()

    def from_z(d):
        s = slot_of(y, (z + d) % 8, core)
        arrived(s)
        onward(d, 0 if d > 4 else 1, 0)
        spread(d, kv_out.at[s])

    def from_far(d):
        s = slot_of(y_far, (z + d) % 8, core)
        arrived(s)
        onward(d, 0 if d > 4 else 1, 1)
        sib_copy(s, kv_out.at[s]).start()

    def from_y(d):
        for yy in (y_down, y_up):
            s = slot_of(yy, (z + d) % 8, core)
            arrived(s)
            sib_copy(s, kv_out.at[s]).start()

    from_z(7)
    from_z(1)
    from_z(6)
    from_z(2)

    own_kv = pltpu.make_async_copy(kv_own, kv_out.at[mine], local.at[0])
    own_qg = pltpu.make_async_copy(qg_own, qg_out.at[x], local.at[1])
    own_kv.start()
    own_qg.start()

    from_far(0)
    for n in range(4):
        z_copy(0, kv_out.at[slot_of(y_far, z, core)], n, 1).start()
    from_y(0)
    from_z(5)
    from_z(3)
    from_y(7)
    from_y(1)
    from_far(7)
    from_far(1)
    from_far(6)
    from_far(2)
    from_z(4)
    x_arrived(x_from, 0)
    x_forward(0).start()

    loads[5].wait()
    for h in range(HEADS):
        cols = slice(h * DIM, (h + 1) * DIM)
        product = g_ref[:, cols].astype(jnp.float32) * o_ref[:, cols].astype(jnp.float32)
        sums = jnp.sum(jnp.transpose(product), axis=0, keepdims=True)
        delta_own[h : h + 1, :] = sums.astype(jnp.bfloat16).astype(jnp.float32)

    def d_copy(n):
        return remote(delta_own, delta_out.at[x], d_send.at[n], d_recv.at[x], device((x + 1 + n) % 4, y, z, core))

    for n in range(3):
        d_copy(n).start()
    own_delta = pltpu.make_async_copy(delta_own, delta_out.at[x], local.at[2])
    own_delta.start()

    from_y(6)
    from_y(2)
    from_far(5)
    from_far(3)
    x_arrived(x_from, 1)
    x_forward(1).start()
    from_y(5)
    from_y(3)
    from_far(4)
    from_y(4)

    for p in range(2):
        x_arrived(x_to, p)
        x_arrived((x + 2) % 4, p)
    for n in range(1, 4):
        who = (x + n) % 4
        remote(delta_own, delta_out.at[who], local.at[0], d_recv.at[who], sibling).wait_recv()

    def from_sibling(s, c):
        arrived((1 - core) * 32 + s)
        return c

    lax.fori_loop(0, 32, from_sibling, 0)

    def sent(d, c):
        y_copy(d, kv_own, True).wait_send()
        y_copy(d, kv_own, False).wait_send()
        return c

    lax.fori_loop(0, 8, sent, 0)

    def sib_sent(s, c):
        sib_copy(s, kv_own).wait_send()
        return c

    lax.fori_loop(0, 32, sib_sent, 0)
    far_copy().wait_send()
    for far in range(2):
        for d, n in ((0, 0), (0, 1), (0, 2), (0, 3), (6, 0), (2, 1)):
            z_copy(d, kv_own, n, far).wait_send()

    @pl.when(core == 0)
    def _():
        z_copy(5, kv_own, 0, 0).wait_send()
        z_copy(5, kv_own, 0, 1).wait_send()

    @pl.when(core == 1)
    def _():
        z_copy(3, kv_own, 1, 0).wait_send()
        z_copy(3, kv_own, 1, 1).wait_send()

    for p in range(2):
        x_copy(p, 0).wait_send()
        x_copy(p, 1).wait_send()
        x_forward(p).wait_send()
    for n in range(3):
        d_copy(n).wait_send()
    own_kv.wait()
    own_qg.wait()
    own_delta.wait()


def norm_kernel(part_ref, out_ref, got, send, recv):
    x, y, z, core = coords()
    peers = [device((x + d) % 4, y, z, core) for d in (1, 3, 2)]
    greet(peers)

    def copy(n):
        return remote(part_ref, got.at[x], send.at[n], recv.at[x], peers[n])

    for n in range(3):
        copy(n).start()
    for n in range(1, 4):
        who = (x + n) % 4
        remote(part_ref, got.at[who], send.at[0], recv.at[who], peers[0]).wait_recv()
    logs = [part_ref[...]] + [got[(x + n) % 4] for n in range(1, 4)]
    top = functools.reduce(jnp.maximum, logs)
    out_ref[...] = top + jnp.log2(functools.reduce(jnp.add, [jnp.exp2(v - top) for v in logs]))
    for n in range(3):
        copy(n).wait_send()


def reduce_kernel(
    dq_ref, kv_ref, dq_out, dk_out, dv_out,
    sib_got, kv_sum, opp_got, near_got, far_got, z_got, x_opp, x_near, x_far, x_sum,
    sib_send, sib_recv, a_send, a_recv, b_send, b_recv, c_send, c_recv, z_send, z_recv, x_send, x_recv,
):
    x, y, z, core = coords()
    sign = 1 - 2 * core
    sibling = device(x, y, z, 1 - core)
    y_to, y_back, y_opp = (y + sign + 4) % 4, (y - sign + 4) % 4, (y + 2) % 4
    x_to, x_back, x_over = (x + sign + 4) % 4, (x - sign + 4) % 4, (x + 2) % 4
    to_next, to_back = device(x, y_to, z, core), device(x, y_back, z, core)
    dev_to, dev_back = device(x_to, y, z, core), device(x_back, y, z, core)

    greet(plane_peers(x, y, z, core))

    def add(*parts):
        return functools.reduce(jnp.add, [p.astype(jnp.float32) for p in parts])

    def sib_copy(s):
        return remote(kv_ref.at[(1 - core) * 32 + s], sib_got.at[s], sib_send.at[s], sib_recv.at[s], sibling)

    far_first = (4, 3, 5, 2, 6, 1, 7, 0)

    x_a = remote(dq_ref.at[x_over], x_opp, x_send.at[0], x_recv.at[0], dev_to)
    x_b = remote(dq_ref.at[x_back], x_near, x_send.at[1], x_recv.at[1], dev_back)
    x_c = remote(x_sum, x_far, x_send.at[2], x_recv.at[2], dev_to)
    for d in far_first:
        zz = (z + d) % 8
        for yy in (y_opp, y_back, y_to, y):
            sib_copy(yy * 8 + zz).start()
        if d == 3:
            x_a.start()
            x_b.start()

    def with_sibling(s):
        sib_copy(s).wait_recv()
        return add(kv_ref[core * 32 + s], sib_got[s])

    def a_copy(zz):
        return remote(kv_sum.at[y_opp * 8 + zz], opp_got.at[zz], a_send.at[zz], a_recv.at[zz], to_next)

    def b_copy(zz):
        return remote(kv_sum.at[y_back * 8 + zz], near_got.at[zz], b_send.at[zz], b_recv.at[zz], to_back)

    def c_copy(zz):
        return remote(kv_sum.at[y_to * 8 + zz], far_got.at[zz], c_send.at[zz], c_recv.at[zz], to_next)

    def z_copy(zz):
        return remote(kv_sum.at[y * 8 + zz], z_got.at[z], z_send.at[zz], z_recv.at[z], device(x, y, zz, core))

    def step_a(d):
        zz = (z + d) % 8
        s = y_opp * 8 + zz
        kv_sum[s] = with_sibling(s).astype(jnp.bfloat16)
        a_copy(zz).start()

    def step_b(d):
        zz = (z + d) % 8
        s = y_back * 8 + zz
        kv_sum[s] = with_sibling(s).astype(jnp.bfloat16)
        b_copy(zz).start()

    def step_c(d):
        zz = (z + d) % 8
        s = y_to * 8 + zz
        total = with_sibling(s)
        a_copy(zz).wait_recv()
        kv_sum[s] = add(total, opp_got[zz]).astype(jnp.bfloat16)
        c_copy(zz).start()

    def total_here(zz):
        s = y * 8 + zz
        total = with_sibling(s)
        b_copy(zz).wait_recv()
        c_copy(zz).wait_recv()
        return add(total, near_got[zz], far_got[zz])

    def step_z(d):
        zz = (z + d) % 8
        kv_sum[y * 8 + zz] = total_here(zz).astype(jnp.bfloat16)
        z_copy(zz).start()

    def sum_x(h, c):
        rows = pl.ds(pl.multiple_of(h * 16, 16), 16)
        x_sum[rows, :] = add(dq_ref[x_to, rows, :], x_opp[rows, :]).astype(jnp.bfloat16)
        return c

    for n in range(11):
        if n < 8:
            step_a(far_first[n])
        if 0 <= n - 2 < 8:
            step_b(far_first[n - 2])
            step_c(far_first[n - 2])
        if 0 <= n - 4 < 7:
            step_z(far_first[n - 4])
        if n == 6:
            x_a.wait_recv()
            lax.fori_loop(0, 8, sum_x, 0)
            x_c.start()

    x_b.wait_recv()
    x_c.wait_recv()
    for h in range(HEADS):
        cols = slice(h * DIM, (h + 1) * DIM)
        total = add(dq_ref[x, :, cols], x_near[:, cols], x_far[:, cols])
        dq_out[:, cols] = jnp.transpose(total).astype(jnp.bfloat16)

    total = total_here(z)
    for d in range(1, 8):
        who = (z + d) % 8
        remote(kv_sum.at[0], z_got.at[who], z_send.at[0], z_recv.at[who], sibling).wait_recv()
        total = add(total, z_got[who])
    dk_out[...] = total[:, 0:DIM].astype(jnp.bfloat16)
    dv_out[...] = total[:, DIM:].astype(jnp.bfloat16)

    def sib_sent(s, c):
        sib_copy(s).wait_send()
        return c

    lax.fori_loop(0, 32, sib_sent, 0)

    def sent(d, c):
        zz = (z + d) % 8
        a_copy(zz).wait_send()
        b_copy(zz).wait_send()
        c_copy(zz).wait_send()
        return c

    lax.fori_loop(0, 8, sent, 0)

    def z_sent(d, c):
        z_copy((z + d) % 8).wait_send()
        return c

    lax.fori_loop(1, 8, z_sent, 0)
    x_a.wait_send()
    x_b.wait_send()
    x_c.wait_send()


def smem():
    return pl.BlockSpec(memory_space=pltpu.SMEM)


def vmem():
    return pl.BlockSpec(memory_space=pltpu.VMEM)


def hbm():
    return pl.BlockSpec(memory_space=pl.ANY)


def bf16(*shape):
    return jax.ShapeDtypeStruct(shape, jnp.bfloat16)


def f32(*shape):
    return jax.ShapeDtypeStruct(shape, jnp.float32)


def dma(*shape):
    return pltpu.SemaphoreType.DMA(shape)


def params(collective_id=None, vmem_mib=48):
    return pltpu.CompilerParams(
        collective_id=collective_id, has_side_effects=collective_id is not None, vmem_limit_bytes=vmem_mib << 20
    )


def gather_call(queries, exps, keys, values, outs, grads):
    return pl.pallas_call(
        gather_kernel,
        out_shape=(bf16(NQ, 2, WIDE, DIM), bf16(NK, 2, STRIPE, DIM), f32(NQ, HEADS, STRIPE)),
        in_specs=[hbm()] * 6,
        out_specs=(hbm(), hbm(), hbm()),
        scratch_shapes=[
            pltpu.VMEM((STRIPE, WIDE), jnp.bfloat16),
            pltpu.VMEM((1, STRIPE), jnp.int32),
            pltpu.VMEM((STRIPE, WIDE), jnp.bfloat16),
            pltpu.VMEM((STRIPE, WIDE), jnp.bfloat16),
            pltpu.VMEM((2, STRIPE, DIM), jnp.bfloat16),
            pltpu.VMEM((2, WIDE, DIM), jnp.bfloat16),
            pltpu.VMEM((HEADS, STRIPE), jnp.float32),
            dma(NK), dma(2, 8, 4), dma(8, 2), pltpu.SemaphoreType.DMA, dma(32), dma(2, 2), dma(2), dma(NQ, 2), dma(3), dma(NQ), dma(3), dma(6),
        ],
        compiler_params=params(0, 8),
        name="gather",
    )(queries, exps, keys, values, outs, grads)


def stats_call(win, order, qg, kv):
    return pl.pallas_call(
        stats_kernel,
        out_shape=f32(NQ, WIDE),
        in_specs=[smem(), hbm()] + [vmem()] * 2,
        out_specs=vmem(),
        scratch_shapes=[
            pltpu.SMEM((256,), jnp.int32),
            pltpu.SemaphoreType.DMA,
            pltpu.SMEM((NK,), jnp.int32),
            pltpu.SMEM((NK + 1,), jnp.int32),
            pltpu.SMEM((NK + 1,), jnp.int32),
            pltpu.VMEM((8, WIDE), jnp.float32),
            pltpu.VMEM((8, WIDE), jnp.float32),
        ],
        compiler_params=params(None, 16),
        name="stats",
    )(win, order, qg, kv)


def norm_call(part):
    return pl.pallas_call(
        norm_kernel,
        out_shape=f32(NQ, WIDE),
        in_specs=[vmem()],
        out_specs=vmem(),
        scratch_shapes=[pltpu.VMEM((NQ, NQ, WIDE), jnp.float32), dma(3), dma(NQ)],
        compiler_params=params(1, 4),
        name="norm",
    )(part)


def grads_call(win, order, qg, kv, norm, delta):
    return pl.pallas_call(
        grads_kernel,
        out_shape=(bf16(NQ, DIM, WIDE), bf16(NK, STRIPE, 2 * DIM)),
        in_specs=[smem(), hbm()] + [vmem()] * 4,
        out_specs=(vmem(), vmem()),
        scratch_shapes=[
            pltpu.SMEM((256,), jnp.int32),
            pltpu.SemaphoreType.DMA,
            pltpu.SMEM((NK,), jnp.int32),
            pltpu.SMEM((NK + 1,), jnp.int32),
            pltpu.SMEM((NK + 1,), jnp.int32),
            pltpu.VMEM((NK, STRIPE, 2 * DIM), jnp.float32),
            pltpu.VMEM((DIM, WIDE), jnp.float32),
            pltpu.VMEM((2, WIDE), jnp.float32),
        ],
        compiler_params=params(None, 32),
        name="grads",
    )(win, order, qg, kv, norm, delta)


def reduce_call(dq, dkv):
    tile = (STRIPE, 2 * DIM)
    return pl.pallas_call(
        reduce_kernel,
        out_shape=(bf16(STRIPE, WIDE), bf16(STRIPE, DIM), bf16(STRIPE, DIM)),
        in_specs=[vmem()] * 2,
        out_specs=(vmem(), vmem(), vmem()),
        scratch_shapes=[
            pltpu.VMEM((32, *tile), jnp.bfloat16),
            pltpu.VMEM((32, *tile), jnp.bfloat16),
            pltpu.VMEM((8, *tile), jnp.bfloat16),
            pltpu.VMEM((8, *tile), jnp.bfloat16),
            pltpu.VMEM((8, *tile), jnp.bfloat16),
            pltpu.VMEM((8, *tile), jnp.bfloat16),
            pltpu.VMEM((DIM, WIDE), jnp.bfloat16),
            pltpu.VMEM((DIM, WIDE), jnp.bfloat16),
            pltpu.VMEM((DIM, WIDE), jnp.bfloat16),
            pltpu.VMEM((DIM, WIDE), jnp.bfloat16),
            dma(32), dma(32), dma(8), dma(8), dma(8), dma(8), dma(8), dma(8), dma(8), dma(8), dma(3), dma(3),
        ],
        compiler_params=params(2, 20),
        name="reduce",
    )(dq, dkv)


def finish_kernel(a_in, b_in, c_in, a_out, b_out, c_out, sem):
    copies = [
        pltpu.make_async_copy(src, dst, sem.at[n])
        for n, (src, dst) in enumerate(((a_in, a_out), (b_in, b_out), (c_in, c_out)))
    ]
    for copy in copies:
        copy.start()
    for copy in copies:
        copy.wait()


def finish_call(dq, dk, dv):
    return pl.pallas_call(
        finish_kernel,
        out_shape=(bf16(STRIPE, WIDE), bf16(STRIPE, DIM), bf16(STRIPE, DIM)),
        in_specs=[hbm()] * 3,
        out_specs=(hbm(),) * 3,
        scratch_shapes=[dma(3)],
        compiler_params=params(None, 4),
        name="finish",
    )(dq, dk, dv)


def per_device(
    queries, query_exps, key_head, value_head, forward_out, output_grad, stripe_order, window_size
):
    held = [
        pltpu.with_memory_space_constraint(a, pltpu.HBM)
        for a in (
            queries, query_exps.reshape(1, STRIPE), key_head, value_head, forward_out, output_grad, stripe_order
        )
    ]
    qg, kv, delta = gather_call(*held[:6])
    part = stats_call(window_size, held[6], qg, kv)
    norm = norm_call(part)
    dq, dkv = grads_call(window_size, held[6], qg, kv, norm, delta)
    return finish_call(*reduce_call(dq, dkv))


def solution(mesh):
    return jax.shard_map(
        per_device,
        mesh=mesh,
        in_specs=(
            P(("row", "col"), None),
            P(("row", "col")),
            P(("col", "row"), None),
            P(("col", "row"), None),
            P(("row", "col"), None),
            P(("row", "col"), None),
            P(),
            P(),
        ),
        out_specs=(P(("row", "col"), None), P(("col", "row"), None), P(("col", "row"), None)),
        check_vma=False,
    )
```

```python
import functools
import math

import jax
import jax.numpy as jnp
from jax import lax
from jax.experimental import pallas as pl
from jax.experimental.pallas import tpu as pltpu
from jax.sharding import PartitionSpec as P

STRIPE = 128
HEADS = 8
DIM = 128
WIDE = HEADS * STRIPE
NQ = 4
NK = 64
MESH = pl.DeviceIdType.MESH
NEG = -1e30
LIMIT = 2.0**100
FAR = -(1 << 20)
SCALE = 1.0 / math.sqrt(DIM)
SCALE2 = math.log2(math.e) / math.sqrt(DIM)


def coords():
    row, col = lax.axis_index("row"), lax.axis_index("col")
    x, y, core = row // 2, col // 8, col % 2
    z = ((col // 2) % 4) * 2 + row % 2
    return x, y, z, core


def device(x, y, z, core):
    return (x * 2 + z % 2, y * 8 + (z // 2) * 2 + core)


def slot_of(y, z, core):
    return core * 32 + y * 8 + z


def positions(order, pos):
    row, col = lax.axis_index("row"), lax.axis_index("col")

    def one(s, c):
        y, z, core = (s // 8) % 4, s % 8, s // 32
        stored = (y * 8 + (z // 2) * 2 + core) * 8 + (row // 2) * 2 + z % 2
        pos[s] = order[stored] * STRIPE
        return c

    lax.fori_loop(0, NK, one, 0, unroll=8)
    for j in range(NQ):
        pos[NK + j] = order[(j * 2 + row % 2) * 32 + col] * STRIPE


class Listed:
    def __init__(self, lists, j):
        self.lists, self.at, self.count_at = lists, j * (NK + 16), 2 * NQ * (NK + 16) + j

    def index(self, n):
        return self.lists[self.at + n]

    def gap(self, n):
        return self.lists[NQ * (NK + 16) + self.at + n]

    def put(self, n, index, gap):
        self.lists[self.at + n] = index
        self.lists[NQ * (NK + 16) + self.at + n] = gap

    def count(self):
        return self.lists[self.count_at]


def build_list(listed, q_at, pos, window):
    def one(k, n):
        distance = q_at - pos[k]
        seen = (distance >= 0) & (distance - (STRIPE - 1) < window)
        listed.put(n, k, distance)
        return n + seen.astype(jnp.int32)

    n = lax.fori_loop(0, NK, one, jnp.int32(0), unroll=8)
    listed.put(n, 0, FAR)
    listed.lists[listed.count_at] = n
    return n


def over_list(n, step, most):
    done = 0
    while most > 2:
        full = n // most
        lax.fori_loop(done * 2 // most, full, lambda t, c, most=most: step(most, most * t, c), 0)
        done = full * (most // 2)
        most //= 2
    lax.fori_loop(done, (n + 1) // 2, lambda t, c: step(2, 2 * t, c), 0)


def tile_mask(gaps, window):
    delta = lax.broadcasted_iota(jnp.int32, (STRIPE, STRIPE), 1) - lax.broadcasted_iota(
        jnp.int32, (STRIPE, STRIPE), 0
    )
    parts = []
    for g in gaps:
        distance = delta + g
        parts.append((distance >= 0) & (distance < window))
    rows = jnp.concatenate(parts, axis=0)
    return jnp.concatenate([rows, rows], axis=1)


def dot_nt(a, b):
    return lax.dot_general(a, b, (((1,), (1,)), ((), ())), preferred_element_type=jnp.float32)


def dot_nn(a, b):
    return lax.dot_general(a, b, (((1,), (0,)), ((), ())), preferred_element_type=jnp.float32)


def stats_kernel(win, pos, qg_ref, kv_ref, out_ref, lists, m_ref, l_ref):
    window = win[0]

    def per_query(j, carry):
        listed = Listed(lists, j)
        n = build_list(listed, pos[NK + j], pos, window)

        def scores(group, first, b):
            keys = jnp.concatenate([kv_ref[listed.index(first + i), 0] for i in range(group)], axis=0)
            return dot_nt(keys, qg_ref[j, 0, pl.ds(b * 256, 256), :])

        def restart():
            m_ref[...] = jnp.full_like(m_ref, NEG)
            l_ref[...] = jnp.zeros_like(l_ref)

        def online(group, first, c=0):
            mask = tile_mask([listed.gap(first + i) for i in range(group)], window)
            for b in range(HEADS // 2):
                cols = pl.ds(b * 256, 256)
                s = jnp.where(mask, scores(group, first, b), NEG).reshape(group * 16, 8, 256)
                m_old = m_ref[:, cols]
                m_new = jnp.maximum(m_old, jnp.max(s, axis=0))
                e = jnp.exp2((s - m_new[None]) * SCALE2)
                l_ref[:, cols] = l_ref[:, cols] * jnp.exp2((m_old - m_new) * SCALE2) + jnp.sum(e, axis=0)
                m_ref[:, cols] = m_new
            return c

        def settle():
            m_all = m_ref[...]
            top = jnp.max(m_all, axis=0, keepdims=True)
            l_ref[...] = l_ref[...] * jnp.exp2((m_all - top) * SCALE2)
            m_ref[...] = jnp.broadcast_to(top * SCALE2, m_all.shape)

        def shifted(group, first, c=0):
            gaps = [listed.gap(first + i) for i in range(group)]

            def add(masked):
                mask = tile_mask(gaps, window) if masked else None
                for b in range(HEADS // 2):
                    cols = pl.ds(b * 256, 256)
                    s = scores(group, first, b)
                    s = jnp.where(mask, s, NEG) if masked else s
                    e = jnp.exp2(s.reshape(group * 16, 8, 256) * SCALE2 - m_ref[:, cols][None])
                    l_ref[:, cols] += jnp.sum(e, axis=0)

            whole = functools.reduce(
                jnp.logical_and, [(g >= STRIPE) & (g <= window - STRIPE) for g in gaps]
            )
            pl.when(whole)(lambda: add(False))
            pl.when(jnp.logical_not(whole))(lambda: add(True))
            return c

        restart()
        pl.when(n >= 8)(lambda: online(8, 0) or None)
        pl.when((n >= 4) & (n < 8))(lambda: online(4, 0) or None)
        pl.when((n >= 1) & (n < 4))(lambda: online(2, 0) or None)
        settle()
        eights, fours = n // 8, n // 4
        lax.fori_loop(1, eights, lambda t, c: shifted(8, 8 * t, c), 0)
        lax.fori_loop(jnp.where(n >= 8, 2 * eights, 1), fours, lambda t, c: shifted(4, 4 * t, c), 0)
        lax.fori_loop(jnp.where(n >= 4, 2 * fours, 1), (n + 1) // 2, lambda t, c: shifted(2, 2 * t, c), 0)

        @pl.when(jnp.max(l_ref[...]) > LIMIT)
        def _():
            restart()
            over_list(n, online, 8)
            settle()

        total = jnp.sum(l_ref[...], axis=0, keepdims=True)
        out_ref[pl.ds(j, 1), :] = m_ref[0:1, :] + jnp.log2(jnp.maximum(total, 1e-30))
        return carry

    lax.fori_loop(0, NQ, per_query, 0)


def grads_kernel(
    win, lists, qg_ref, kv_ref, norm_ref, delta_ref, dq_ref, dkv_ref,
    acc_ref, dq_acc, stat_ref,
):
    window = win[0]

    def clear(k, c):
        acc_ref[k] = jnp.zeros((STRIPE, 2 * DIM), jnp.float32)
        return c

    lax.fori_loop(0, NK, clear, 0)

    def per_query(j, carry):
        listed = Listed(lists, j)
        dq_acc[...] = jnp.zeros_like(dq_acc)
        stat_ref[0:1, :] = norm_ref[pl.ds(j, 1), :]
        for h in range(HEADS):
            stat_ref[1:2, h * DIM : (h + 1) * DIM] = delta_ref[j, h : h + 1, :]

        def step(group, first, c):
            at = [listed.index(first + i) for i in range(group)]
            keys = jnp.concatenate([kv_ref[i, 0] for i in at], axis=0)
            vals = jnp.concatenate([kv_ref[i, 1] for i in at], axis=0)
            keys_t = jnp.transpose(keys)
            mask = tile_mask([listed.gap(first + i) for i in range(group)], window)
            weights, score_grads = [], []
            for b in range(HEADS // 2):
                cols = pl.ds(b * 256, 256)
                s = dot_nt(keys, qg_ref[j, 0, cols, :])
                p = jnp.where(mask, jnp.exp2(s * SCALE2 - stat_ref[0:1, cols]), 0.0)
                w = dot_nt(vals, qg_ref[j, 1, cols, :])
                score_grads.append((p * (w - stat_ref[1:2, cols])).astype(jnp.bfloat16))
                weights.append(p.astype(jnp.bfloat16))
            weights = jnp.concatenate(weights, axis=1)
            score_grads = jnp.concatenate(score_grads, axis=1)
            dv = dot_nn(weights, qg_ref[j, 1])
            dk = dot_nn(score_grads, qg_ref[j, 0])
            dq_acc[...] += dot_nn(keys_t, score_grads)
            for i, k in enumerate(at):
                rows = slice(i * STRIPE, (i + 1) * STRIPE)
                acc_ref[k, :, 0:DIM] += dk[rows]
                acc_ref[k, :, DIM:] += dv[rows]
            return c

        over_list(listed.count(), step, 8)
        dq_ref[j] = (dq_acc[...] * SCALE).astype(jnp.bfloat16)
        return carry

    lax.fori_loop(0, NQ, per_query, 0)

    def finish(k, c):
        dkv_ref[k, :, 0:DIM] = (acc_ref[k, :, 0:DIM] * SCALE).astype(jnp.bfloat16)
        dkv_ref[k, :, DIM:] = acc_ref[k, :, DIM:].astype(jnp.bfloat16)
        return c

    lax.fori_loop(0, NK, finish, 0)


def remote(src, dst, send_sem, recv_sem, to):
    return pltpu.make_async_remote_copy(
        src_ref=src, dst_ref=dst, send_sem=send_sem, recv_sem=recv_sem, device_id=to, device_id_type=MESH
    )


def greet(peers):
    barrier = pltpu.get_barrier_semaphore()
    for peer in peers:
        pl.semaphore_signal(barrier, inc=1, device_id=peer, device_id_type=MESH)
    pl.semaphore_wait(barrier, len(peers))


def plane_peers(x, y, z, core):
    peers = [device(x, y, z, 1 - core)]
    peers += [device((x + d) % 4, y, z, core) for d in (1, 3)]
    peers += [device(x, (y + d) % 4, z, core) for d in (1, 3)]
    peers += [device(x, y, (z + d) % 8, core) for d in range(1, 8)]
    return peers


def gather_kernel(
    q_in, exp_in, k_in, v_in, o_in, g_in, order_in, qg_out, kv_out, delta_out, pos,
    order,
    q_ref, exp_ref, o_ref, g_ref, kv_own, qg_own, delta_own,
    kv_recv, z_send, y_send, y_pass, sib_send, x_send, x_pass, x_recv, d_send, d_recv, local, load,
):
    loads = [
        pltpu.make_async_copy(src, dst, load.at[n])
        for n, (src, dst) in enumerate(
            (
                (k_in, kv_own.at[0]), (v_in, kv_own.at[1]), (exp_in, exp_ref), (q_in, q_ref), (g_in, g_ref), (o_in, o_ref),
                (order_in, order),
            )
        )
    ]
    for copy in loads:
        copy.start()

    x, y, z, core = coords()
    mine = slot_of(y, z, core)
    sibling = device(x, y, z, 1 - core)
    y_up, y_down = (y + 1) % 4, (y + 3) % 4
    sign = 1 - 2 * core
    x_to, x_from = (x + sign + 4) % 4, (x - sign + 4) % 4

    greet(
        [device(x, y, z, 1 - core)]
        + [device((x + d) % 4, y, z, core) for d in (1, 3, 2)]
        + [device(x, (y + d) % 4, z, core) for d in (1, 3, 2)]
        + [device(x, y, (z + d) % 8, core) for d in (1, 7, 2, 6)]
    )

    def slot_copy(s, src, send, to):
        return remote(src, kv_out.at[s], send, kv_recv.at[s], to)

    def arrived(s):
        slot_copy(s, kv_own, local.at[0], sibling).wait_recv()

    y_far = (y + 2) % 4
    z_steps = (1, 7, 2, 6)

    def z_copy(d, src, n, far=0):
        to = device(x, y, (z + z_steps[n]) % 8, core)
        s = slot_of(y_far if far else y, (z + d) % 8, core)
        return slot_copy(s, src, z_send.at[far, d, n], to)

    def y_copy(d, src, up):
        to = device(x, y_up if up else y_down, z, core)
        return slot_copy(slot_of(y, (z + d) % 8, core), src, y_send.at[d, 0 if up else 1], to)

    def far_copy():
        return slot_copy(mine, kv_own, y_pass, device(x, y_far, z, core))

    def sib_copy(s, src):
        return slot_copy(s, src, sib_send.at[s % 32], sibling)

    def spread(d, src):
        y_copy(d, src, True).start()
        y_copy(d, src, False).start()
        sib_copy(slot_of(y, (z + d) % 8, core), src).start()

    loads[0].wait()
    loads[1].wait()
    for n in range(4):
        z_copy(0, kv_own, n).start()
    far_copy().start()
    spread(0, kv_own)

    loads[2].wait()
    loads[3].wait()
    scale = jnp.transpose(jnp.broadcast_to(jnp.exp2(exp_ref[...].astype(jnp.float32)), (STRIPE, STRIPE)))

    def x_copy(p, n):
        to = device((x + 1 + 2 * n) % 4, y, z, core)
        return remote(qg_own.at[p], qg_out.at[x, p], x_send.at[p, n], x_recv.at[x, p], to)

    for h in range(HEADS):
        cols = slice(h * DIM, (h + 1) * DIM)
        qg_own[0, cols, :] = (q_ref[:, cols].astype(jnp.float32) * scale).astype(jnp.bfloat16)
    x_copy(0, 0).start()
    x_copy(0, 1).start()
    loads[4].wait()
    for h in range(HEADS):
        cols = slice(h * DIM, (h + 1) * DIM)
        qg_own[1, cols, :] = g_ref[:, cols]
    x_copy(1, 0).start()
    x_copy(1, 1).start()

    def x_arrived(who, p):
        remote(qg_own.at[p], qg_out.at[who, p], local.at[0], x_recv.at[who, p], sibling).wait_recv()

    def x_forward(p):
        block = qg_out.at[x_from, p]
        return remote(block, block, x_pass.at[p], x_recv.at[x_from, p], device(x_to, y, z, core))

    def onward(d, n, far):
        s = slot_of(y_far if far else y, (z + d) % 8, core)
        if d in (6, 2):
            z_copy(d, kv_out.at[s], n, far).start()
        elif d in (5, 3):
            @pl.when(core == n)
            def _():
                z_copy(d, kv_out.at[s], n, far).start()

    def from_z(d):
        s = slot_of(y, (z + d) % 8, core)
        arrived(s)
        onward(d, 0 if d > 4 else 1, 0)
        spread(d, kv_out.at[s])

    def from_far(d):
        s = slot_of(y_far, (z + d) % 8, core)
        arrived(s)
        onward(d, 0 if d > 4 else 1, 1)
        sib_copy(s, kv_out.at[s]).start()

    def from_y(d):
        for yy in (y_down, y_up):
            s = slot_of(yy, (z + d) % 8, core)
            arrived(s)
            sib_copy(s, kv_out.at[s]).start()

    from_z(7)
    from_z(1)
    from_z(6)
    from_z(2)

    own_kv = pltpu.make_async_copy(kv_own, kv_out.at[mine], local.at[0])
    own_qg = pltpu.make_async_copy(qg_own, qg_out.at[x], local.at[1])
    own_kv.start()
    own_qg.start()

    from_far(0)
    for n in range(4):
        z_copy(0, kv_out.at[slot_of(y_far, z, core)], n, 1).start()
    from_y(0)
    from_z(5)
    from_z(3)
    from_y(7)
    from_y(1)
    from_far(7)
    from_far(1)
    from_far(6)
    from_far(2)
    from_z(4)
    x_arrived(x_from, 0)
    x_forward(0).start()

    loads[5].wait()
    for h in range(HEADS):
        cols = slice(h * DIM, (h + 1) * DIM)
        product = g_ref[:, cols].astype(jnp.float32) * o_ref[:, cols].astype(jnp.float32)
        sums = jnp.sum(jnp.transpose(product), axis=0, keepdims=True)
        delta_own[h : h + 1, :] = sums.astype(jnp.bfloat16).astype(jnp.float32)

    def d_copy(n):
        return remote(delta_own, delta_out.at[x], d_send.at[n], d_recv.at[x], device((x + 1 + n) % 4, y, z, core))

    for n in range(3):
        d_copy(n).start()
    own_delta = pltpu.make_async_copy(delta_own, delta_out.at[x], local.at[2])
    own_delta.start()
    loads[6].wait()
    positions(order, pos)

    from_y(6)
    from_y(2)
    from_far(5)
    from_far(3)
    x_arrived(x_from, 1)
    x_forward(1).start()
    from_y(5)
    from_y(3)
    from_far(4)
    from_y(4)

    for p in range(2):
        x_arrived(x_to, p)
        x_arrived((x + 2) % 4, p)
    for n in range(1, 4):
        who = (x + n) % 4
        remote(delta_own, delta_out.at[who], local.at[0], d_recv.at[who], sibling).wait_recv()

    def from_sibling(s, c):
        arrived((1 - core) * 32 + s)
        return c

    lax.fori_loop(0, 32, from_sibling, 0)

    def sent(d, c):
        y_copy(d, kv_own, True).wait_send()
        y_copy(d, kv_own, False).wait_send()
        return c

    lax.fori_loop(0, 8, sent, 0)

    def sib_sent(s, c):
        sib_copy(s, kv_own).wait_send()
        return c

    lax.fori_loop(0, 32, sib_sent, 0)
    far_copy().wait_send()
    for far in range(2):
        for d, n in ((0, 0), (0, 1), (0, 2), (0, 3), (6, 0), (2, 1)):
            z_copy(d, kv_own, n, far).wait_send()

    @pl.when(core == 0)
    def _():
        z_copy(5, kv_own, 0, 0).wait_send()
        z_copy(5, kv_own, 0, 1).wait_send()

    @pl.when(core == 1)
    def _():
        z_copy(3, kv_own, 1, 0).wait_send()
        z_copy(3, kv_own, 1, 1).wait_send()

    for p in range(2):
        x_copy(p, 0).wait_send()
        x_copy(p, 1).wait_send()
        x_forward(p).wait_send()
    for n in range(3):
        d_copy(n).wait_send()
    own_kv.wait()
    own_qg.wait()
    own_delta.wait()


def norm_kernel(part_ref, out_ref, got, send, recv):
    x, y, z, core = coords()
    peers = [device((x + d) % 4, y, z, core) for d in (1, 3, 2)]
    greet(peers)

    def copy(n):
        return remote(part_ref, got.at[x], send.at[n], recv.at[x], peers[n])

    for n in range(3):
        copy(n).start()
    for n in range(1, 4):
        who = (x + n) % 4
        remote(part_ref, got.at[who], send.at[0], recv.at[who], peers[0]).wait_recv()
    logs = [part_ref[...]] + [got[(x + n) % 4] for n in range(1, 4)]
    top = functools.reduce(jnp.maximum, logs)
    out_ref[...] = top + jnp.log2(functools.reduce(jnp.add, [jnp.exp2(v - top) for v in logs]))
    for n in range(3):
        copy(n).wait_send()


def reduce_kernel(
    dq_ref, kv_ref, dq_out, dk_out, dv_out,
    sib_got, kv_sum, opp_got, near_got, far_got, z_got, x_opp, x_near, x_far, x_sum,
    sib_send, sib_recv, a_send, a_recv, b_send, b_recv, c_send, c_recv, z_send, z_recv, x_send, x_recv,
):
    x, y, z, core = coords()
    sign = 1 - 2 * core
    sibling = device(x, y, z, 1 - core)
    y_to, y_back, y_opp = (y + sign + 4) % 4, (y - sign + 4) % 4, (y + 2) % 4
    x_to, x_back, x_over = (x + sign + 4) % 4, (x - sign + 4) % 4, (x + 2) % 4
    to_next, to_back = device(x, y_to, z, core), device(x, y_back, z, core)
    dev_to, dev_back = device(x_to, y, z, core), device(x_back, y, z, core)

    greet(plane_peers(x, y, z, core))

    def add(*parts):
        return functools.reduce(jnp.add, [p.astype(jnp.float32) for p in parts])

    def sib_copy(s):
        return remote(kv_ref.at[(1 - core) * 32 + s], sib_got.at[s], sib_send.at[s], sib_recv.at[s], sibling)

    far_first = (4, 3, 5, 2, 6, 1, 7, 0)

    x_a = remote(dq_ref.at[x_over], x_opp, x_send.at[0], x_recv.at[0], dev_to)
    x_b = remote(dq_ref.at[x_back], x_near, x_send.at[1], x_recv.at[1], dev_back)
    x_c = remote(x_sum, x_far, x_send.at[2], x_recv.at[2], dev_to)
    for d in far_first:
        zz = (z + d) % 8
        for yy in (y_opp, y_back, y_to, y):
            sib_copy(yy * 8 + zz).start()
        if d == 3:
            x_a.start()
            x_b.start()

    def with_sibling(s):
        sib_copy(s).wait_recv()
        return add(kv_ref[core * 32 + s], sib_got[s])

    def a_copy(zz):
        return remote(kv_sum.at[y_opp * 8 + zz], opp_got.at[zz], a_send.at[zz], a_recv.at[zz], to_next)

    def b_copy(zz):
        return remote(kv_sum.at[y_back * 8 + zz], near_got.at[zz], b_send.at[zz], b_recv.at[zz], to_back)

    def c_copy(zz):
        return remote(kv_sum.at[y_to * 8 + zz], far_got.at[zz], c_send.at[zz], c_recv.at[zz], to_next)

    def z_copy(zz):
        return remote(kv_sum.at[y * 8 + zz], z_got.at[z], z_send.at[zz], z_recv.at[z], device(x, y, zz, core))

    def step_a(d):
        zz = (z + d) % 8
        s = y_opp * 8 + zz
        kv_sum[s] = with_sibling(s).astype(jnp.bfloat16)
        a_copy(zz).start()

    def step_b(d):
        zz = (z + d) % 8
        s = y_back * 8 + zz
        kv_sum[s] = with_sibling(s).astype(jnp.bfloat16)
        b_copy(zz).start()

    def step_c(d):
        zz = (z + d) % 8
        s = y_to * 8 + zz
        total = with_sibling(s)
        a_copy(zz).wait_recv()
        kv_sum[s] = add(total, opp_got[zz]).astype(jnp.bfloat16)
        c_copy(zz).start()

    def total_here(zz):
        s = y * 8 + zz
        total = with_sibling(s)
        b_copy(zz).wait_recv()
        c_copy(zz).wait_recv()
        return add(total, near_got[zz], far_got[zz])

    def step_z(d):
        zz = (z + d) % 8
        kv_sum[y * 8 + zz] = total_here(zz).astype(jnp.bfloat16)
        z_copy(zz).start()

    def sum_x(h, c):
        rows = pl.ds(pl.multiple_of(h * 16, 16), 16)
        x_sum[rows, :] = add(dq_ref[x_to, rows, :], x_opp[rows, :]).astype(jnp.bfloat16)
        return c

    for n in range(11):
        if n < 8:
            step_a(far_first[n])
        if 0 <= n - 2 < 8:
            step_b(far_first[n - 2])
            step_c(far_first[n - 2])
        if 0 <= n - 4 < 7:
            step_z(far_first[n - 4])
        if n == 6:
            x_a.wait_recv()
            lax.fori_loop(0, 8, sum_x, 0)
            x_c.start()

    x_b.wait_recv()
    x_c.wait_recv()
    for h in range(HEADS):
        cols = slice(h * DIM, (h + 1) * DIM)
        total = add(dq_ref[x, :, cols], x_near[:, cols], x_far[:, cols])
        dq_out[:, cols] = jnp.transpose(total).astype(jnp.bfloat16)

    total = total_here(z)
    for d in range(1, 8):
        who = (z + d) % 8
        remote(kv_sum.at[0], z_got.at[who], z_send.at[0], z_recv.at[who], sibling).wait_recv()
        total = add(total, z_got[who])
    dk_out[...] = total[:, 0:DIM].astype(jnp.bfloat16)
    dv_out[...] = total[:, DIM:].astype(jnp.bfloat16)

    def sib_sent(s, c):
        sib_copy(s).wait_send()
        return c

    lax.fori_loop(0, 32, sib_sent, 0)

    def sent(d, c):
        zz = (z + d) % 8
        a_copy(zz).wait_send()
        b_copy(zz).wait_send()
        c_copy(zz).wait_send()
        return c

    lax.fori_loop(0, 8, sent, 0)

    def z_sent(d, c):
        z_copy((z + d) % 8).wait_send()
        return c

    lax.fori_loop(1, 8, z_sent, 0)
    x_a.wait_send()
    x_b.wait_send()
    x_c.wait_send()


def smem():
    return pl.BlockSpec(memory_space=pltpu.SMEM)


def vmem():
    return pl.BlockSpec(memory_space=pltpu.VMEM)


def hbm():
    return pl.BlockSpec(memory_space=pl.ANY)


def bf16(*shape):
    return jax.ShapeDtypeStruct(shape, jnp.bfloat16)


def i32(*shape):
    return jax.ShapeDtypeStruct(shape, jnp.int32)


def f32(*shape):
    return jax.ShapeDtypeStruct(shape, jnp.float32)


def dma(*shape):
    return pltpu.SemaphoreType.DMA(shape)


def params(collective_id=None, vmem_mib=48):
    return pltpu.CompilerParams(
        collective_id=collective_id, has_side_effects=collective_id is not None, vmem_limit_bytes=vmem_mib << 20
    )


def gather_call(queries, exps, keys, values, outs, grads, order):
    return pl.pallas_call(
        gather_kernel,
        out_shape=(bf16(NQ, 2, WIDE, DIM), bf16(NK, 2, STRIPE, DIM), f32(NQ, HEADS, STRIPE), i32(128)),
        in_specs=[hbm()] * 7,
        out_specs=(hbm(), hbm(), hbm(), smem()),
        scratch_shapes=[
            pltpu.SMEM((256,), jnp.int32),
            pltpu.VMEM((STRIPE, WIDE), jnp.bfloat16),
            pltpu.VMEM((1, STRIPE), jnp.int32),
            pltpu.VMEM((STRIPE, WIDE), jnp.bfloat16),
            pltpu.VMEM((STRIPE, WIDE), jnp.bfloat16),
            pltpu.VMEM((2, STRIPE, DIM), jnp.bfloat16),
            pltpu.VMEM((2, WIDE, DIM), jnp.bfloat16),
            pltpu.VMEM((HEADS, STRIPE), jnp.float32),
            dma(NK), dma(2, 8, 4), dma(8, 2), pltpu.SemaphoreType.DMA, dma(32), dma(2, 2), dma(2), dma(NQ, 2), dma(3), dma(NQ), dma(3), dma(7),
        ],
        compiler_params=params(0, 8),
        name="gather",
    )(queries, exps, keys, values, outs, grads, order)


def stats_call(win, pos, qg, kv):
    return pl.pallas_call(
        stats_kernel,
        out_shape=(f32(NQ, WIDE), i32(1024)),
        in_specs=[smem()] * 2 + [vmem()] * 2,
        out_specs=(vmem(), smem()),
        scratch_shapes=[
            pltpu.VMEM((8, WIDE), jnp.float32),
            pltpu.VMEM((8, WIDE), jnp.float32),
        ],
        compiler_params=params(None, 16),
        name="stats",
    )(win, pos, qg, kv)


def norm_call(part):
    return pl.pallas_call(
        norm_kernel,
        out_shape=f32(NQ, WIDE),
        in_specs=[vmem()],
        out_specs=vmem(),
        scratch_shapes=[pltpu.VMEM((NQ, NQ, WIDE), jnp.float32), dma(3), dma(NQ)],
        compiler_params=params(1, 4),
        name="norm",
    )(part)


def grads_call(win, lists, qg, kv, norm, delta):
    return pl.pallas_call(
        grads_kernel,
        out_shape=(bf16(NQ, DIM, WIDE), bf16(NK, STRIPE, 2 * DIM)),
        in_specs=[smem()] * 2 + [vmem()] * 4,
        out_specs=(vmem(), vmem()),
        scratch_shapes=[
            pltpu.VMEM((NK, STRIPE, 2 * DIM), jnp.float32),
            pltpu.VMEM((DIM, WIDE), jnp.float32),
            pltpu.VMEM((2, WIDE), jnp.float32),
        ],
        compiler_params=params(None, 40),
        name="grads",
    )(win, lists, qg, kv, norm, delta)


def reduce_call(dq, dkv):
    tile = (STRIPE, 2 * DIM)
    return pl.pallas_call(
        reduce_kernel,
        out_shape=(bf16(STRIPE, WIDE), bf16(STRIPE, DIM), bf16(STRIPE, DIM)),
        in_specs=[vmem()] * 2,
        out_specs=(vmem(), vmem(), vmem()),
        scratch_shapes=[
            pltpu.VMEM((32, *tile), jnp.bfloat16),
            pltpu.VMEM((32, *tile), jnp.bfloat16),
            pltpu.VMEM((8, *tile), jnp.bfloat16),
            pltpu.VMEM((8, *tile), jnp.bfloat16),
            pltpu.VMEM((8, *tile), jnp.bfloat16),
            pltpu.VMEM((8, *tile), jnp.bfloat16),
            pltpu.VMEM((DIM, WIDE), jnp.bfloat16),
            pltpu.VMEM((DIM, WIDE), jnp.bfloat16),
            pltpu.VMEM((DIM, WIDE), jnp.bfloat16),
            pltpu.VMEM((DIM, WIDE), jnp.bfloat16),
            dma(32), dma(32), dma(8), dma(8), dma(8), dma(8), dma(8), dma(8), dma(8), dma(8), dma(3), dma(3),
        ],
        compiler_params=params(2, 20),
        name="reduce",
    )(dq, dkv)


def finish_kernel(a_in, b_in, c_in, a_out, b_out, c_out, sem):
    copies = [
        pltpu.make_async_copy(src, dst, sem.at[n])
        for n, (src, dst) in enumerate(((a_in, a_out), (b_in, b_out), (c_in, c_out)))
    ]
    for copy in copies:
        copy.start()
    for copy in copies:
        copy.wait()


def finish_call(dq, dk, dv):
    return pl.pallas_call(
        finish_kernel,
        out_shape=(bf16(STRIPE, WIDE), bf16(STRIPE, DIM), bf16(STRIPE, DIM)),
        in_specs=[hbm()] * 3,
        out_specs=(hbm(),) * 3,
        scratch_shapes=[dma(3)],
        compiler_params=params(None, 4),
        name="finish",
    )(dq, dk, dv)


def per_device(
    queries, query_exps, key_head, value_head, forward_out, output_grad, stripe_order, window_size
):
    held = [
        pltpu.with_memory_space_constraint(a, pltpu.HBM)
        for a in (
            queries, query_exps.reshape(1, STRIPE), key_head, value_head, forward_out, output_grad, stripe_order
        )
    ]
    qg, kv, delta, pos = gather_call(*held)
    part, lists = stats_call(window_size, pos, qg, kv)
    norm = norm_call(part)
    dq, dkv = grads_call(window_size, lists, qg, kv, norm, delta)
    return finish_call(*reduce_call(dq, dkv))


def solution(mesh):
    return jax.shard_map(
        per_device,
        mesh=mesh,
        in_specs=(
            P(("row", "col"), None),
            P(("row", "col")),
            P(("col", "row"), None),
            P(("col", "row"), None),
            P(("row", "col"), None),
            P(("row", "col"), None),
            P(),
            P(),
        ),
        out_specs=(P(("row", "col"), None), P(("col", "row"), None), P(("col", "row"), None)),
        check_vma=False,
    )
```

```python
import functools
import math

import jax
import jax.numpy as jnp
from jax import lax
from jax.experimental import pallas as pl
from jax.experimental.pallas import tpu as pltpu
from jax.sharding import PartitionSpec as P

STRIPE = 128
HEADS = 8
DIM = 128
WIDE = HEADS * STRIPE
NQ = 4
NK = 64
MESH = pl.DeviceIdType.MESH
NEG = -1e30
LIMIT = 2.0**100
FAR = -(1 << 20)
SCALE = 1.0 / math.sqrt(DIM)
SCALE2 = math.log2(math.e) / math.sqrt(DIM)


def coords():
    row, col = lax.axis_index("row"), lax.axis_index("col")
    x, y, core = row // 2, col // 8, col % 2
    z = ((col // 2) % 4) * 2 + row % 2
    return x, y, z, core


def device(x, y, z, core):
    return (x * 2 + z % 2, y * 8 + (z // 2) * 2 + core)


def slot_of(y, z, core):
    return core * 32 + y * 8 + z


def positions(order, pos):
    row, col = lax.axis_index("row"), lax.axis_index("col")

    def one(s, c):
        y, z, core = (s // 8) % 4, s % 8, s // 32
        stored = (y * 8 + (z // 2) * 2 + core) * 8 + (row // 2) * 2 + z % 2
        pos[s] = order[stored] * STRIPE
        return c

    lax.fori_loop(0, NK, one, 0, unroll=8)
    for j in range(NQ):
        pos[NK + j] = order[(j * 2 + row % 2) * 32 + col] * STRIPE


class Listed:
    def __init__(self, lists, j):
        self.lists, self.at, self.count_at = lists, j * (NK + 16), 2 * NQ * (NK + 16) + j

    def index(self, n):
        return self.lists[self.at + n]

    def gap(self, n):
        return self.lists[NQ * (NK + 16) + self.at + n]

    def put(self, n, index, gap):
        self.lists[self.at + n] = index
        self.lists[NQ * (NK + 16) + self.at + n] = gap

    def count(self):
        return self.lists[self.count_at]


def build_list(listed, q_at, pos, window):
    def one(k, n):
        distance = q_at - pos[k]
        seen = (distance >= 0) & (distance - (STRIPE - 1) < window)
        listed.put(n, k, distance)
        return n + seen.astype(jnp.int32)

    n = lax.fori_loop(0, NK, one, jnp.int32(0), unroll=8)
    listed.put(n, 0, FAR)
    listed.lists[listed.count_at] = n
    return n


def over_list(n, step, most):
    done = 0
    while most > 2:
        full = n // most
        lax.fori_loop(done * 2 // most, full, lambda t, c, most=most: step(most, most * t, c), 0)
        done = full * (most // 2)
        most //= 2
    lax.fori_loop(done, (n + 1) // 2, lambda t, c: step(2, 2 * t, c), 0)


def tile_mask(gaps, window):
    delta = lax.broadcasted_iota(jnp.int32, (STRIPE, STRIPE), 1) - lax.broadcasted_iota(
        jnp.int32, (STRIPE, STRIPE), 0
    )
    parts = []
    for g in gaps:
        distance = delta + g
        parts.append((distance >= 0) & (distance < window))
    rows = jnp.concatenate(parts, axis=0)
    return jnp.concatenate([rows, rows], axis=1)


def dot_nt(a, b):
    return lax.dot_general(a, b, (((1,), (1,)), ((), ())), preferred_element_type=jnp.float32)


def dot_nn(a, b):
    return lax.dot_general(a, b, (((1,), (0,)), ((), ())), preferred_element_type=jnp.float32)


def stats_kernel(win, pos, qg_ref, kv_ref, out_ref, lists, m_ref, l_ref):
    window = win[0]

    def per_query(j, carry):
        listed = Listed(lists, j)
        n = build_list(listed, pos[NK + j], pos, window)

        def scores(group, first, b):
            keys = jnp.concatenate([kv_ref[listed.index(first + i), 0] for i in range(group)], axis=0)
            return dot_nt(keys, qg_ref[j, 0, pl.ds(b * 256, 256), :])

        def restart():
            m_ref[...] = jnp.full_like(m_ref, NEG)
            l_ref[...] = jnp.zeros_like(l_ref)

        def online(group, first, c=0):
            mask = tile_mask([listed.gap(first + i) for i in range(group)], window)
            for b in range(HEADS // 2):
                cols = pl.ds(b * 256, 256)
                s = jnp.where(mask, scores(group, first, b), NEG).reshape(group * 16, 8, 256)
                m_old = m_ref[:, cols]
                m_new = jnp.maximum(m_old, jnp.max(s, axis=0))
                e = jnp.exp2((s - m_new[None]) * SCALE2)
                l_ref[:, cols] = l_ref[:, cols] * jnp.exp2((m_old - m_new) * SCALE2) + jnp.sum(e, axis=0)
                m_ref[:, cols] = m_new
            return c

        def settle():
            m_all = m_ref[...]
            top = jnp.max(m_all, axis=0, keepdims=True)
            l_ref[...] = l_ref[...] * jnp.exp2((m_all - top) * SCALE2)
            m_ref[...] = jnp.broadcast_to(top * SCALE2, m_all.shape)

        def shifted(group, first, c=0):
            gaps = [listed.gap(first + i) for i in range(group)]

            def add(masked):
                mask = tile_mask(gaps, window) if masked else None
                for b in range(HEADS // 2):
                    cols = pl.ds(b * 256, 256)
                    s = scores(group, first, b)
                    s = jnp.where(mask, s, NEG) if masked else s
                    e = jnp.exp2(s.reshape(group * 16, 8, 256) * SCALE2 - m_ref[:, cols][None])
                    l_ref[:, cols] += jnp.sum(e, axis=0)

            whole = functools.reduce(
                jnp.logical_and, [(g >= STRIPE) & (g <= window - STRIPE) for g in gaps]
            )
            pl.when(whole)(lambda: add(False))
            pl.when(jnp.logical_not(whole))(lambda: add(True))
            return c

        restart()
        pl.when(n >= 8)(lambda: online(8, 0) or None)
        pl.when((n >= 4) & (n < 8))(lambda: online(4, 0) or None)
        pl.when((n >= 1) & (n < 4))(lambda: online(2, 0) or None)
        settle()
        eights, fours = n // 8, n // 4
        lax.fori_loop(1, eights, lambda t, c: shifted(8, 8 * t, c), 0)
        lax.fori_loop(jnp.where(n >= 8, 2 * eights, 1), fours, lambda t, c: shifted(4, 4 * t, c), 0)
        lax.fori_loop(jnp.where(n >= 4, 2 * fours, 1), (n + 1) // 2, lambda t, c: shifted(2, 2 * t, c), 0)

        @pl.when(jnp.max(l_ref[...]) > LIMIT)
        def _():
            restart()
            over_list(n, online, 8)
            settle()

        total = jnp.sum(l_ref[...], axis=0, keepdims=True)
        out_ref[pl.ds(j, 1), :] = m_ref[0:1, :] + jnp.log2(jnp.maximum(total, 1e-30))
        return carry

    lax.fori_loop(0, NQ, per_query, 0)


def grads_kernel(
    win, lists, qg_ref, kv_ref, norm_ref, delta_ref, dq_ref, dkv_ref,
    acc_ref, dq_acc, stat_ref,
):
    window = win[0]

    def clear(k, c):
        acc_ref[k] = jnp.zeros((STRIPE, 2 * DIM), jnp.float32)
        return c

    lax.fori_loop(0, NK, clear, 0)

    def per_query(j, carry):
        listed = Listed(lists, j)
        dq_acc[...] = jnp.zeros_like(dq_acc)
        stat_ref[0:1, :] = norm_ref[pl.ds(j, 1), :]
        for h in range(HEADS):
            stat_ref[1:2, h * DIM : (h + 1) * DIM] = delta_ref[j, h : h + 1, :]

        def step(group, first, c):
            at = [listed.index(first + i) for i in range(group)]
            keys = jnp.concatenate([kv_ref[i, 0] for i in at], axis=0)
            vals = jnp.concatenate([kv_ref[i, 1] for i in at], axis=0)
            keys_t = jnp.transpose(keys)
            mask = tile_mask([listed.gap(first + i) for i in range(group)], window)
            weights, score_grads = [], []
            for b in range(HEADS // 2):
                cols = pl.ds(b * 256, 256)
                s = dot_nt(keys, qg_ref[j, 0, cols, :])
                p = jnp.where(mask, jnp.exp2(s * SCALE2 - stat_ref[0:1, cols]), 0.0)
                w = dot_nt(vals, qg_ref[j, 1, cols, :])
                score_grads.append((p * (w - stat_ref[1:2, cols])).astype(jnp.bfloat16))
                weights.append(p.astype(jnp.bfloat16))
            weights = jnp.concatenate(weights, axis=1)
            score_grads = jnp.concatenate(score_grads, axis=1)
            dv = dot_nn(weights, qg_ref[j, 1])
            dk = dot_nn(score_grads, qg_ref[j, 0])
            dq_acc[...] += dot_nn(keys_t, score_grads)
            for i, k in enumerate(at):
                rows = slice(i * STRIPE, (i + 1) * STRIPE)
                acc_ref[k, :, 0:DIM] += dk[rows]
                acc_ref[k, :, DIM:] += dv[rows]
            return c

        over_list(listed.count(), step, 8)
        dq_ref[j] = (dq_acc[...] * SCALE).astype(jnp.bfloat16)
        return carry

    lax.fori_loop(0, NQ, per_query, 0)

    def finish(k, c):
        dkv_ref[k, :, 0:DIM] = (acc_ref[k, :, 0:DIM] * SCALE).astype(jnp.bfloat16)
        dkv_ref[k, :, DIM:] = acc_ref[k, :, DIM:].astype(jnp.bfloat16)
        return c

    lax.fori_loop(0, NK, finish, 0)


def remote(src, dst, send_sem, recv_sem, to):
    return pltpu.make_async_remote_copy(
        src_ref=src, dst_ref=dst, send_sem=send_sem, recv_sem=recv_sem, device_id=to, device_id_type=MESH
    )


def greet(peers):
    barrier = pltpu.get_barrier_semaphore()
    for peer in peers:
        pl.semaphore_signal(barrier, inc=1, device_id=peer, device_id_type=MESH)
    pl.semaphore_wait(barrier, len(peers))


def plane_peers(x, y, z, core):
    peers = [device(x, y, z, 1 - core)]
    peers += [device((x + d) % 4, y, z, core) for d in (1, 3)]
    peers += [device(x, (y + d) % 4, z, core) for d in (1, 3)]
    peers += [device(x, y, (z + d) % 8, core) for d in range(1, 8)]
    return peers


def gather_kernel(
    q_in, exp_in, k_in, v_in, o_in, g_in, order_in, qg_out, kv_out, delta_out, pos,
    order,
    q_ref, exp_ref, o_ref, g_ref, kv_own, qg_own, delta_own,
    kv_recv, z_send, y_send, y_recv, sib_send, sib_recv, x_send, x_pass, x_recv, d_send, d_recv, local, load,
):
    loads = [
        pltpu.make_async_copy(src, dst, load.at[n])
        for n, (src, dst) in enumerate(
            (
                (k_in, kv_own.at[0]), (v_in, kv_own.at[1]), (exp_in, exp_ref), (q_in, q_ref), (g_in, g_ref), (o_in, o_ref),
                (order_in, order),
            )
        )
    ]
    for copy in loads:
        copy.start()

    x, y, z, core = coords()
    mine = slot_of(y, z, core)
    sibling = device(x, y, z, 1 - core)
    y_up, y_down = (y + 1) % 4, (y + 3) % 4
    sign = 1 - 2 * core
    x_to, x_from = (x + sign + 4) % 4, (x - sign + 4) % 4

    greet(
        [device(x, y, z, 1 - core)]
        + [device((x + d) % 4, y, z, core) for d in (1, 3, 2)]
        + [device(x, (y + d) % 4, z, core) for d in (1, 3, 2)]
        + [device(x, y, (z + d) % 8, core) for d in (1, 7, 2, 6)]
    )

    y_far = (y + 2) % 4
    z_steps = (1, 7, 2, 6)

    def slot_copy(s, src, send, recv, to):
        return remote(src, kv_out.at[s], send, recv, to)

    def arrived(s):
        slot_copy(s, kv_own, z_send, kv_recv.at[s], sibling).wait_recv()

    def z_copy(d, src, n, far=0):
        to = device(x, y, (z + z_steps[n]) % 8, core)
        s = slot_of(y_far if far else y, (z + d) % 8, core)
        return slot_copy(s, src, z_send, kv_recv.at[s], to)

    def y_copy(d, src, n):
        to = device(x, y_down if n else y_up, z, core)
        return slot_copy(slot_of(y, (z + d) % 8, core), src, y_send, y_recv.at[n], to)

    def far_copy():
        return slot_copy(mine, kv_own, y_send, kv_recv.at[mine], device(x, y_far, z, core))

    def slots(first, count):
        block = kv_out.at[pl.ds(first, count)]
        return block, block

    def sib_row(yy):
        return remote(*slots(slot_of(yy, 0, core), 8), sib_send, sib_recv, sibling)

    def spread(d, src):
        y_copy(d, src, 0).start()
        y_copy(d, src, 1).start()

    loads[0].wait()
    loads[1].wait()
    for n in range(4):
        z_copy(0, kv_own, n).start()
    far_copy().start()
    spread(0, kv_own)

    loads[2].wait()
    loads[3].wait()
    scale = jnp.transpose(jnp.broadcast_to(jnp.exp2(exp_ref[...].astype(jnp.float32)), (STRIPE, STRIPE)))

    def x_copy(p, n):
        to = device((x + 1 + 2 * n) % 4, y, z, core)
        return remote(qg_own.at[p], qg_out.at[x, p], x_send.at[p, n], x_recv.at[x, p], to)

    for h in range(HEADS):
        cols = slice(h * DIM, (h + 1) * DIM)
        qg_own[0, cols, :] = (q_ref[:, cols].astype(jnp.float32) * scale).astype(jnp.bfloat16)
    x_copy(0, 0).start()
    x_copy(0, 1).start()
    loads[4].wait()
    for h in range(HEADS):
        cols = slice(h * DIM, (h + 1) * DIM)
        qg_own[1, cols, :] = g_ref[:, cols]
    x_copy(1, 0).start()
    x_copy(1, 1).start()

    def x_arrived(who, p):
        remote(qg_own.at[p], qg_out.at[who, p], local.at[0], x_recv.at[who, p], sibling).wait_recv()

    def x_forward(p):
        block = qg_out.at[x_from, p]
        return remote(block, block, x_pass.at[p], x_recv.at[x_from, p], device(x_to, y, z, core))

    def onward(d, n, far):
        s = slot_of(y_far if far else y, (z + d) % 8, core)
        if d in (6, 2):
            z_copy(d, kv_out.at[s], n, far).start()
        elif d in (5, 3):
            @pl.when(core == n)
            def _():
                z_copy(d, kv_out.at[s], n, far).start()

    def from_z(d):
        s = slot_of(y, (z + d) % 8, core)
        arrived(s)
        onward(d, 0 if d > 4 else 1, 0)
        spread(d, kv_out.at[s])

    def from_far(d):
        arrived(slot_of(y_far, (z + d) % 8, core))
        onward(d, 0 if d > 4 else 1, 1)

    from_z(7)
    from_z(1)
    from_z(6)
    from_z(2)

    own_kv = pltpu.make_async_copy(kv_own, kv_out.at[mine], local.at[0])
    own_qg = pltpu.make_async_copy(qg_own, qg_out.at[x], local.at[1])
    own_kv.start()
    own_qg.start()

    from_far(0)
    for n in range(4):
        z_copy(0, kv_out.at[slot_of(y_far, z, core)], n, 1).start()
    from_z(5)
    from_z(3)
    from_far(6)
    from_far(2)
    from_z(4)
    own_kv.wait()
    sib_row(y).start()
    x_arrived(x_from, 0)
    x_forward(0).start()

    loads[5].wait()
    for h in range(HEADS):
        cols = slice(h * DIM, (h + 1) * DIM)
        product = g_ref[:, cols].astype(jnp.float32) * o_ref[:, cols].astype(jnp.float32)
        sums = jnp.sum(jnp.transpose(product), axis=0, keepdims=True)
        delta_own[h : h + 1, :] = sums.astype(jnp.bfloat16).astype(jnp.float32)

    def d_copy(n):
        return remote(delta_own, delta_out.at[x], d_send.at[n], d_recv.at[x], device((x + 1 + n) % 4, y, z, core))

    for n in range(3):
        d_copy(n).start()
    own_delta = pltpu.make_async_copy(delta_own, delta_out.at[x], local.at[2])
    own_delta.start()
    loads[6].wait()
    positions(order, pos)

    from_far(5)
    from_far(3)
    x_arrived(x_from, 1)
    x_forward(1).start()
    for n, yy in enumerate((y_down, y_up)):
        remote(*slots(0, 8), z_send, y_recv.at[n], sibling).wait_recv()
        sib_row(yy).start()
    for d in (7, 1, 4):
        from_far(d)
    sib_row(y_far).start()

    for p in range(2):
        x_arrived(x_to, p)
        x_arrived((x + 2) % 4, p)
    for n in range(1, 4):
        who = (x + n) % 4
        remote(delta_own, delta_out.at[who], local.at[0], d_recv.at[who], sibling).wait_recv()

    remote(*slots(0, 32), z_send, sib_recv, sibling).wait_recv()
    remote(*slots(0, 14), z_send, sib_recv, sibling).wait_send()
    remote(*slots(0, 17), y_send, sib_recv, sibling).wait_send()
    remote(*slots(0, 32), sib_send, sib_recv, sibling).wait_send()
    for p in range(2):
        x_copy(p, 0).wait_send()
        x_copy(p, 1).wait_send()
        x_forward(p).wait_send()
    for n in range(3):
        d_copy(n).wait_send()
    own_qg.wait()
    own_delta.wait()


def norm_kernel(part_ref, out_ref, got, send, recv):
    x, y, z, core = coords()
    peers = [device((x + d) % 4, y, z, core) for d in (1, 3, 2)]
    greet(peers)

    def copy(n):
        return remote(part_ref, got.at[x], send.at[n], recv.at[x], peers[n])

    for n in range(3):
        copy(n).start()
    for n in range(1, 4):
        who = (x + n) % 4
        remote(part_ref, got.at[who], send.at[0], recv.at[who], peers[0]).wait_recv()
    logs = [part_ref[...]] + [got[(x + n) % 4] for n in range(1, 4)]
    top = functools.reduce(jnp.maximum, logs)
    out_ref[...] = top + jnp.log2(functools.reduce(jnp.add, [jnp.exp2(v - top) for v in logs]))
    for n in range(3):
        copy(n).wait_send()


def reduce_kernel(
    dq_ref, kv_ref, dq_out, dk_out, dv_out,
    sib_got, kv_sum, opp_got, near_got, far_got, z_got, x_opp, x_near, x_far, x_sum,
    sib_send, sib_recv, a_send, a_recv, b_send, b_recv, c_send, c_recv, z_send, z_recv, x_send, x_recv,
):
    x, y, z, core = coords()
    sign = 1 - 2 * core
    sibling = device(x, y, z, 1 - core)
    y_to, y_back, y_opp = (y + sign + 4) % 4, (y - sign + 4) % 4, (y + 2) % 4
    x_to, x_back, x_over = (x + sign + 4) % 4, (x - sign + 4) % 4, (x + 2) % 4
    to_next, to_back = device(x, y_to, z, core), device(x, y_back, z, core)
    dev_to, dev_back = device(x_to, y, z, core), device(x_back, y, z, core)

    greet(plane_peers(x, y, z, core))

    def add(*parts):
        return functools.reduce(jnp.add, [p.astype(jnp.float32) for p in parts])

    def sib_copy(zz):
        return remote(kv_ref.at[1 - core, :, zz], sib_got.at[:, zz], sib_send, sib_recv.at[zz], sibling)

    far_first = (4, 3, 5, 2, 6, 1, 7, 0)

    x_a = remote(dq_ref.at[x_over], x_opp, x_send.at[0], x_recv.at[0], dev_to)
    x_b = remote(dq_ref.at[x_back], x_near, x_send.at[1], x_recv.at[1], dev_back)
    x_c = remote(x_sum, x_far, x_send.at[2], x_recv.at[2], dev_to)
    for d in far_first:
        sib_copy((z + d) % 8).start()
        if d == 3:
            x_a.start()
            x_b.start()

    def with_sibling(yy, zz):
        return add(kv_ref[core, yy, zz], sib_got[yy, zz])

    def a_copy(zz):
        return remote(kv_sum.at[y_opp, zz], opp_got.at[zz], a_send, a_recv.at[zz], to_next)

    def b_copy(zz):
        return remote(kv_sum.at[y_back, zz], near_got.at[zz], b_send, b_recv.at[zz], to_back)

    def c_copy(zz):
        return remote(kv_sum.at[y_to, zz], far_got.at[zz], c_send, c_recv.at[zz], to_next)

    def z_copy(zz):
        return remote(kv_sum.at[y, zz], z_got.at[z], z_send, z_recv, device(x, y, zz, core))

    def step_a(d):
        zz = (z + d) % 8
        sib_copy(zz).wait_recv()
        kv_sum[y_opp, zz] = with_sibling(y_opp, zz).astype(jnp.bfloat16)
        a_copy(zz).start()

    def step_b(d):
        zz = (z + d) % 8
        kv_sum[y_back, zz] = with_sibling(y_back, zz).astype(jnp.bfloat16)
        b_copy(zz).start()

    def step_c(d):
        zz = (z + d) % 8
        total = with_sibling(y_to, zz)
        a_copy(zz).wait_recv()
        kv_sum[y_to, zz] = add(total, opp_got[zz]).astype(jnp.bfloat16)
        c_copy(zz).start()

    def total_here(zz):
        total = with_sibling(y, zz)
        b_copy(zz).wait_recv()
        c_copy(zz).wait_recv()
        return add(total, near_got[zz], far_got[zz])

    def step_z(d):
        zz = (z + d) % 8
        kv_sum[y, zz] = total_here(zz).astype(jnp.bfloat16)
        z_copy(zz).start()

    def sum_x(h, c):
        rows = pl.ds(pl.multiple_of(h * 16, 16), 16)
        x_sum[rows, :] = add(dq_ref[x_to, rows, :], x_opp[rows, :]).astype(jnp.bfloat16)
        return c

    for n in range(11):
        if n < 8:
            step_a(far_first[n])
        if 0 <= n - 2 < 8:
            step_b(far_first[n - 2])
            step_c(far_first[n - 2])
        if 0 <= n - 4 < 7:
            step_z(far_first[n - 4])
        if n == 6:
            x_a.wait_recv()
            lax.fori_loop(0, 8, sum_x, 0)
            x_c.start()

    x_b.wait_recv()
    x_c.wait_recv()
    for h in range(HEADS):
        cols = slice(h * DIM, (h + 1) * DIM)
        total = add(dq_ref[x, :, cols], x_near[:, cols], x_far[:, cols])
        dq_out[:, cols] = jnp.transpose(total).astype(jnp.bfloat16)

    total = total_here(z)
    seven = kv_sum.at[0, pl.ds(0, 7)]
    remote(seven, seven, z_send, z_recv, sibling).wait_recv()
    for d in range(1, 8):
        total = add(total, z_got[(z + d) % 8])
    dk_out[...] = total[:, 0:DIM].astype(jnp.bfloat16)
    dv_out[...] = total[:, DIM:].astype(jnp.bfloat16)

    remote(sib_got, sib_got, sib_send, z_recv, sibling).wait_send()
    for send in (a_send, b_send, c_send):
        remote(kv_sum.at[0], kv_sum.at[0], send, z_recv, sibling).wait_send()
    remote(seven, seven, z_send, z_recv, sibling).wait_send()
    x_a.wait_send()
    x_b.wait_send()
    x_c.wait_send()


def smem():
    return pl.BlockSpec(memory_space=pltpu.SMEM)


def vmem():
    return pl.BlockSpec(memory_space=pltpu.VMEM)


def hbm():
    return pl.BlockSpec(memory_space=pl.ANY)


def bf16(*shape):
    return jax.ShapeDtypeStruct(shape, jnp.bfloat16)


def i32(*shape):
    return jax.ShapeDtypeStruct(shape, jnp.int32)


def f32(*shape):
    return jax.ShapeDtypeStruct(shape, jnp.float32)


def dma(*shape):
    return pltpu.SemaphoreType.DMA(shape) if shape else pltpu.SemaphoreType.DMA


def params(collective_id=None, vmem_mib=48):
    return pltpu.CompilerParams(
        collective_id=collective_id, has_side_effects=collective_id is not None, vmem_limit_bytes=vmem_mib << 20
    )


def gather_call(queries, exps, keys, values, outs, grads, order):
    return pl.pallas_call(
        gather_kernel,
        out_shape=(bf16(NQ, 2, WIDE, DIM), bf16(NK, 2, STRIPE, DIM), f32(NQ, HEADS, STRIPE), i32(128)),
        in_specs=[hbm()] * 7,
        out_specs=(hbm(), hbm(), hbm(), smem()),
        scratch_shapes=[
            pltpu.SMEM((256,), jnp.int32),
            pltpu.VMEM((STRIPE, WIDE), jnp.bfloat16),
            pltpu.VMEM((1, STRIPE), jnp.int32),
            pltpu.VMEM((STRIPE, WIDE), jnp.bfloat16),
            pltpu.VMEM((STRIPE, WIDE), jnp.bfloat16),
            pltpu.VMEM((2, STRIPE, DIM), jnp.bfloat16),
            pltpu.VMEM((2, WIDE, DIM), jnp.bfloat16),
            pltpu.VMEM((HEADS, STRIPE), jnp.float32),
            dma(NK), dma(), dma(), dma(2), dma(), dma(), dma(2, 2), dma(2), dma(NQ, 2), dma(3), dma(NQ), dma(3), dma(7),
        ],
        compiler_params=params(0, 8),
        name="gather",
    )(queries, exps, keys, values, outs, grads, order)


def stats_call(win, pos, qg, kv):
    return pl.pallas_call(
        stats_kernel,
        out_shape=(f32(NQ, WIDE), i32(1024)),
        in_specs=[smem()] * 2 + [vmem()] * 2,
        out_specs=(vmem(), smem()),
        scratch_shapes=[
            pltpu.VMEM((8, WIDE), jnp.float32),
            pltpu.VMEM((8, WIDE), jnp.float32),
        ],
        compiler_params=params(None, 16),
        name="stats",
    )(win, pos, qg, kv)


def norm_call(part):
    return pl.pallas_call(
        norm_kernel,
        out_shape=f32(NQ, WIDE),
        in_specs=[vmem()],
        out_specs=vmem(),
        scratch_shapes=[pltpu.VMEM((NQ, NQ, WIDE), jnp.float32), dma(3), dma(NQ)],
        compiler_params=params(1, 4),
        name="norm",
    )(part)


def grads_call(win, lists, qg, kv, norm, delta):
    return pl.pallas_call(
        grads_kernel,
        out_shape=(bf16(NQ, DIM, WIDE), bf16(NK, STRIPE, 2 * DIM)),
        in_specs=[smem()] * 2 + [vmem()] * 4,
        out_specs=(vmem(), vmem()),
        scratch_shapes=[
            pltpu.VMEM((NK, STRIPE, 2 * DIM), jnp.float32),
            pltpu.VMEM((DIM, WIDE), jnp.float32),
            pltpu.VMEM((2, WIDE), jnp.float32),
        ],
        compiler_params=params(None, 40),
        name="grads",
    )(win, lists, qg, kv, norm, delta)


def reduce_call(dq, dkv):
    tile = (STRIPE, 2 * DIM)
    return pl.pallas_call(
        reduce_kernel,
        out_shape=(bf16(STRIPE, WIDE), bf16(STRIPE, DIM), bf16(STRIPE, DIM)),
        in_specs=[vmem()] * 2,
        out_specs=(vmem(), vmem(), vmem()),
        scratch_shapes=[
            pltpu.VMEM((4, 8, *tile), jnp.bfloat16),
            pltpu.VMEM((4, 8, *tile), jnp.bfloat16),
            pltpu.VMEM((8, *tile), jnp.bfloat16),
            pltpu.VMEM((8, *tile), jnp.bfloat16),
            pltpu.VMEM((8, *tile), jnp.bfloat16),
            pltpu.VMEM((8, *tile), jnp.bfloat16),
            pltpu.VMEM((DIM, WIDE), jnp.bfloat16),
            pltpu.VMEM((DIM, WIDE), jnp.bfloat16),
            pltpu.VMEM((DIM, WIDE), jnp.bfloat16),
            pltpu.VMEM((DIM, WIDE), jnp.bfloat16),
            dma(), dma(8), dma(), dma(8), dma(), dma(8), dma(), dma(8), dma(), dma(), dma(3), dma(3),
        ],
        compiler_params=params(2, 20),
        name="reduce",
    )(dq, dkv.reshape(2, 4, 8, *tile))


def finish_kernel(a_in, b_in, c_in, a_out, b_out, c_out, sem):
    copies = [
        pltpu.make_async_copy(src, dst, sem.at[n])
        for n, (src, dst) in enumerate(((a_in, a_out), (b_in, b_out), (c_in, c_out)))
    ]
    for copy in copies:
        copy.start()
    for copy in copies:
        copy.wait()


def finish_call(dq, dk, dv):
    return pl.pallas_call(
        finish_kernel,
        out_shape=(bf16(STRIPE, WIDE), bf16(STRIPE, DIM), bf16(STRIPE, DIM)),
        in_specs=[hbm()] * 3,
        out_specs=(hbm(),) * 3,
        scratch_shapes=[dma(3)],
        compiler_params=params(None, 4),
        name="finish",
    )(dq, dk, dv)


def per_device(
    queries, query_exps, key_head, value_head, forward_out, output_grad, stripe_order, window_size
):
    held = [
        pltpu.with_memory_space_constraint(a, pltpu.HBM)
        for a in (
            queries, query_exps.reshape(1, STRIPE), key_head, value_head, forward_out, output_grad, stripe_order
        )
    ]
    qg, kv, delta, pos = gather_call(*held)
    part, lists = stats_call(window_size, pos, qg, kv)
    norm = norm_call(part)
    dq, dkv = grads_call(window_size, lists, qg, kv, norm, delta)
    return finish_call(*reduce_call(dq, dkv))


def solution(mesh):
    return jax.shard_map(
        per_device,
        mesh=mesh,
        in_specs=(
            P(("row", "col"), None),
            P(("row", "col")),
            P(("col", "row"), None),
            P(("col", "row"), None),
            P(("row", "col"), None),
            P(("row", "col"), None),
            P(),
            P(),
        ),
        out_specs=(P(("row", "col"), None), P(("col", "row"), None), P(("col", "row"), None)),
        check_vma=False,
    )
```

```python
import functools
import math

import jax
import jax.numpy as jnp
from jax import lax
from jax.experimental import pallas as pl
from jax.experimental.pallas import tpu as pltpu
from jax.sharding import PartitionSpec as P

STRIPE = 128
HEADS = 8
DIM = 128
WIDE = HEADS * STRIPE
NQ = 4
NK = 64
MESH = pl.DeviceIdType.MESH
NEG = -1e30
LIMIT = 2.0**100
FAR = -(1 << 20)
SCALE = 1.0 / math.sqrt(DIM)
SCALE2 = math.log2(math.e) / math.sqrt(DIM)


def coords():
    row, col = lax.axis_index("row"), lax.axis_index("col")
    x, y, core = row // 2, col // 8, col % 2
    z = ((col // 2) % 4) * 2 + row % 2
    return x, y, z, core


def device(x, y, z, core):
    return (x * 2 + z % 2, y * 8 + (z // 2) * 2 + core)


def slot_of(y, z, core):
    return core * 32 + y * 8 + z


def positions(order, pos):
    row, col = lax.axis_index("row"), lax.axis_index("col")

    def one(s, c):
        y, z, core = (s // 8) % 4, s % 8, s // 32
        stored = (y * 8 + (z // 2) * 2 + core) * 8 + (row // 2) * 2 + z % 2
        pos[s] = order[stored] * STRIPE
        return c

    lax.fori_loop(0, NK, one, 0, unroll=8)
    for j in range(NQ):
        pos[NK + j] = order[(j * 2 + row % 2) * 32 + col] * STRIPE


class Listed:
    def __init__(self, lists, j):
        self.lists, self.at, self.count_at = lists, j * (NK + 16), 2 * NQ * (NK + 16) + j

    def index(self, n):
        return self.lists[self.at + n]

    def gap(self, n):
        return self.lists[NQ * (NK + 16) + self.at + n]

    def put(self, n, index, gap):
        self.lists[self.at + n] = index
        self.lists[NQ * (NK + 16) + self.at + n] = gap

    def count(self):
        return self.lists[self.count_at]


def build_list(listed, q_at, pos, window):
    def one(k, n):
        distance = q_at - pos[k]
        seen = (distance >= 0) & (distance - (STRIPE - 1) < window)
        listed.put(n, k, distance)
        return n + seen.astype(jnp.int32)

    n = lax.fori_loop(0, NK, one, jnp.int32(0), unroll=8)
    listed.put(n, 0, FAR)
    listed.lists[listed.count_at] = n
    return n


def over_list(n, step, most):
    done = 0
    while most > 2:
        full = n // most
        lax.fori_loop(done * 2 // most, full, lambda t, c, most=most: step(most, most * t, c), 0)
        done = full * (most // 2)
        most //= 2
    lax.fori_loop(done, (n + 1) // 2, lambda t, c: step(2, 2 * t, c), 0)


def tile_mask(gaps, window):
    delta = lax.broadcasted_iota(jnp.int32, (STRIPE, STRIPE), 1) - lax.broadcasted_iota(
        jnp.int32, (STRIPE, STRIPE), 0
    )
    parts = []
    for g in gaps:
        distance = delta + g
        parts.append((distance >= 0) & (distance < window))
    rows = jnp.concatenate(parts, axis=0)
    return jnp.concatenate([rows, rows], axis=1)


def dot_nt(a, b):
    return lax.dot_general(a, b, (((1,), (1,)), ((), ())), preferred_element_type=jnp.float32)


def dot_nn(a, b):
    return lax.dot_general(a, b, (((1,), (0,)), ((), ())), preferred_element_type=jnp.float32)


def stats_kernel(win, pos, qg_ref, kv_ref, out_ref, lists, m_ref, l_ref):
    window = win[0]

    def per_query(j, carry):
        listed = Listed(lists, j)
        n = build_list(listed, pos[NK + j], pos, window)

        def scores(group, first, b):
            keys = jnp.concatenate([kv_ref[listed.index(first + i), 0] for i in range(group)], axis=0)
            return dot_nt(keys, qg_ref[j, 0, pl.ds(b * 256, 256), :])

        def restart():
            m_ref[...] = jnp.full_like(m_ref, NEG)
            l_ref[...] = jnp.zeros_like(l_ref)

        def online(group, first, c=0):
            mask = tile_mask([listed.gap(first + i) for i in range(group)], window)
            for b in range(HEADS // 2):
                cols = pl.ds(b * 256, 256)
                s = jnp.where(mask, scores(group, first, b), NEG).reshape(group * 16, 8, 256)
                m_old = m_ref[:, cols]
                m_new = jnp.maximum(m_old, jnp.max(s, axis=0))
                e = jnp.exp2((s - m_new[None]) * SCALE2)
                l_ref[:, cols] = l_ref[:, cols] * jnp.exp2((m_old - m_new) * SCALE2) + jnp.sum(e, axis=0)
                m_ref[:, cols] = m_new
            return c

        def settle():
            m_all = m_ref[...]
            top = jnp.max(m_all, axis=0, keepdims=True)
            l_ref[...] = l_ref[...] * jnp.exp2((m_all - top) * SCALE2)
            m_ref[...] = jnp.broadcast_to(top * SCALE2, m_all.shape)

        def shifted(group, first, c=0):
            gaps = [listed.gap(first + i) for i in range(group)]

            def add(masked):
                mask = tile_mask(gaps, window) if masked else None
                for b in range(HEADS // 2):
                    cols = pl.ds(b * 256, 256)
                    s = scores(group, first, b)
                    s = jnp.where(mask, s, NEG) if masked else s
                    e = jnp.exp2(s.reshape(group * 16, 8, 256) * SCALE2 - m_ref[:, cols][None])
                    l_ref[:, cols] += jnp.sum(e, axis=0)

            whole = functools.reduce(
                jnp.logical_and, [(g >= STRIPE) & (g <= window - STRIPE) for g in gaps]
            )
            pl.when(whole)(lambda: add(False))
            pl.when(jnp.logical_not(whole))(lambda: add(True))
            return c

        restart()
        pl.when(n >= 8)(lambda: online(8, 0) or None)
        pl.when((n >= 4) & (n < 8))(lambda: online(4, 0) or None)
        pl.when((n >= 1) & (n < 4))(lambda: online(2, 0) or None)
        settle()
        eights, fours = n // 8, n // 4
        lax.fori_loop(1, eights, lambda t, c: shifted(8, 8 * t, c), 0)
        lax.fori_loop(jnp.where(n >= 8, 2 * eights, 1), fours, lambda t, c: shifted(4, 4 * t, c), 0)
        lax.fori_loop(jnp.where(n >= 4, 2 * fours, 1), (n + 1) // 2, lambda t, c: shifted(2, 2 * t, c), 0)

        @pl.when(jnp.max(l_ref[...]) > LIMIT)
        def _():
            restart()
            over_list(n, online, 8)
            settle()

        total = jnp.sum(l_ref[...], axis=0, keepdims=True)
        out_ref[pl.ds(j, 1), :] = m_ref[0:1, :] + jnp.log2(jnp.maximum(total, 1e-30))
        return carry

    lax.fori_loop(0, NQ, per_query, 0)


def grads_kernel(
    win, lists, qg_ref, kv_ref, norm_ref, delta_ref, dq_ref, dkv_ref,
    acc_ref, dq_acc, stat_ref,
):
    window = win[0]

    def clear(k, c):
        acc_ref[k] = jnp.zeros((STRIPE, 2 * DIM), jnp.float32)
        return c

    lax.fori_loop(0, NK, clear, 0)

    def per_query(j, carry):
        listed = Listed(lists, j)
        dq_acc[...] = jnp.zeros_like(dq_acc)
        stat_ref[0:1, :] = norm_ref[pl.ds(j, 1), :]
        for h in range(HEADS):
            stat_ref[1:2, h * DIM : (h + 1) * DIM] = delta_ref[j, h : h + 1, :]

        def step(group, first, c):
            at = [listed.index(first + i) for i in range(group)]
            keys = jnp.concatenate([kv_ref[i, 0] for i in at], axis=0)
            vals = jnp.concatenate([kv_ref[i, 1] for i in at], axis=0)
            keys_t = jnp.transpose(keys)
            mask = tile_mask([listed.gap(first + i) for i in range(group)], window)
            weights, score_grads = [], []
            for b in range(HEADS // 2):
                cols = pl.ds(b * 256, 256)
                s = dot_nt(keys, qg_ref[j, 0, cols, :])
                p = jnp.where(mask, jnp.exp2(s * SCALE2 - stat_ref[0:1, cols]), 0.0)
                w = dot_nt(vals, qg_ref[j, 1, cols, :])
                score_grads.append((p * (w - stat_ref[1:2, cols])).astype(jnp.bfloat16))
                weights.append(p.astype(jnp.bfloat16))
            weights = jnp.concatenate(weights, axis=1)
            score_grads = jnp.concatenate(score_grads, axis=1)
            dv = dot_nn(weights, qg_ref[j, 1])
            dk = dot_nn(score_grads, qg_ref[j, 0])
            dq_acc[...] += dot_nn(keys_t, score_grads)
            for i, k in enumerate(at):
                rows = slice(i * STRIPE, (i + 1) * STRIPE)
                acc_ref[k, :, 0:DIM] += dk[rows]
                acc_ref[k, :, DIM:] += dv[rows]
            return c

        over_list(listed.count(), step, 8)
        dq_ref[j] = (dq_acc[...] * SCALE).astype(jnp.bfloat16)
        return carry

    lax.fori_loop(0, NQ, per_query, 0)

    def finish(k, c):
        dkv_ref[k, :, 0:DIM] = (acc_ref[k, :, 0:DIM] * SCALE).astype(jnp.bfloat16)
        dkv_ref[k, :, DIM:] = acc_ref[k, :, DIM:].astype(jnp.bfloat16)
        return c

    lax.fori_loop(0, NK, finish, 0)


def remote(src, dst, send_sem, recv_sem, to):
    return pltpu.make_async_remote_copy(
        src_ref=src, dst_ref=dst, send_sem=send_sem, recv_sem=recv_sem, device_id=to, device_id_type=MESH
    )


def greet(peers):
    barrier = pltpu.get_barrier_semaphore()
    for peer in peers:
        pl.semaphore_signal(barrier, inc=1, device_id=peer, device_id_type=MESH)
    pl.semaphore_wait(barrier, len(peers))


def plane_peers(x, y, z, core):
    peers = [device(x, y, z, 1 - core)]
    peers += [device((x + d) % 4, y, z, core) for d in (1, 3)]
    peers += [device(x, (y + d) % 4, z, core) for d in (1, 3)]
    peers += [device(x, y, (z + d) % 8, core) for d in range(1, 8)]
    return peers


def gather_kernel(
    q_in, exp_in, k_in, v_in, o_in, g_in, order_in, qg_out, kv_out, delta_out, pos,
    order,
    q_ref, exp_ref, o_ref, g_ref, kv_own, qg_own, delta_own,
    kv_recv, z_send, y_send, y_recv, sib_send, sib_recv, x_send, x_pass, x_recv, d_send, d_recv, local, load,
):
    loads = [
        pltpu.make_async_copy(src, dst, load.at[n])
        for n, (src, dst) in enumerate(
            (
                (k_in, kv_own.at[0]), (v_in, kv_own.at[1]), (exp_in, exp_ref), (q_in, q_ref), (g_in, g_ref), (o_in, o_ref),
                (order_in, order),
            )
        )
    ]
    for copy in loads:
        copy.start()

    x, y, z, core = coords()
    mine = slot_of(y, z, core)
    sibling = device(x, y, z, 1 - core)
    y_up, y_down = (y + 1) % 4, (y + 3) % 4
    sign = 1 - 2 * core
    x_to, x_from = (x + sign + 4) % 4, (x - sign + 4) % 4

    greet(
        [device(x, y, z, 1 - core)]
        + [device((x + d) % 4, y, z, core) for d in (1, 3, 2)]
        + [device(x, (y + d) % 4, z, core) for d in (1, 3, 2)]
        + [device(x, y, (z + d) % 8, core) for d in (1, 7, 2, 6)]
    )

    y_far = (y + 2) % 4
    z_steps = (1, 7, 2, 6)

    def slot_copy(s, src, send, recv, to):
        return remote(src, kv_out.at[s], send, recv, to)

    def arrived(s):
        slot_copy(s, kv_own, z_send, kv_recv.at[s], sibling).wait_recv()

    def z_copy(d, src, n, far=0):
        to = device(x, y, (z + z_steps[n]) % 8, core)
        s = slot_of(y_far if far else y, (z + d) % 8, core)
        return slot_copy(s, src, z_send, kv_recv.at[s], to)

    def y_copy(d, src, n):
        to = device(x, y_down if n else y_up, z, core)
        return slot_copy(slot_of(y, (z + d) % 8, core), src, y_send, y_recv.at[n], to)

    def far_copy():
        return slot_copy(mine, kv_own, y_send, kv_recv.at[mine], device(x, y_far, z, core))

    def slots(first, count):
        block = kv_out.at[pl.ds(first, count)]
        return block, block

    def sib_row(yy):
        return remote(*slots(slot_of(yy, 0, core), 8), sib_send, sib_recv, sibling)

    def spread(d, src):
        y_copy(d, src, 0).start()
        y_copy(d, src, 1).start()

    loads[0].wait()
    loads[1].wait()
    for n in range(4):
        z_copy(0, kv_own, n).start()
    far_copy().start()
    spread(0, kv_own)

    loads[2].wait()
    loads[3].wait()
    scale = jnp.transpose(jnp.broadcast_to(jnp.exp2(exp_ref[...].astype(jnp.float32)), (STRIPE, STRIPE)))

    def x_copy(p, n):
        to = device((x + 1 + 2 * n) % 4, y, z, core)
        return remote(qg_own.at[p], qg_out.at[x, p], x_send.at[p, n], x_recv.at[x, p], to)

    for h in range(HEADS):
        cols = slice(h * DIM, (h + 1) * DIM)
        qg_own[0, cols, :] = (q_ref[:, cols].astype(jnp.float32) * scale).astype(jnp.bfloat16)
    x_copy(0, 0).start()
    x_copy(0, 1).start()
    loads[4].wait()
    for h in range(HEADS):
        cols = slice(h * DIM, (h + 1) * DIM)
        qg_own[1, cols, :] = g_ref[:, cols]
    x_copy(1, 0).start()
    x_copy(1, 1).start()

    def x_arrived(who, p):
        remote(qg_own.at[p], qg_out.at[who, p], local.at[0], x_recv.at[who, p], sibling).wait_recv()

    def x_forward(p):
        block = qg_out.at[x_from, p]
        return remote(block, block, x_pass.at[p], x_recv.at[x_from, p], device(x_to, y, z, core))

    def onward(d, n, far):
        s = slot_of(y_far if far else y, (z + d) % 8, core)
        if d in (6, 2):
            z_copy(d, kv_out.at[s], n, far).start()
        elif d in (5, 3):
            @pl.when(core == n)
            def _():
                z_copy(d, kv_out.at[s], n, far).start()

    def from_z(d):
        s = slot_of(y, (z + d) % 8, core)
        arrived(s)
        onward(d, 0 if d > 4 else 1, 0)
        spread(d, kv_out.at[s])

    def from_far(d):
        arrived(slot_of(y_far, (z + d) % 8, core))
        onward(d, 0 if d > 4 else 1, 1)

    from_z(7)
    from_z(1)
    from_z(6)
    from_z(2)

    own_kv = pltpu.make_async_copy(kv_own, kv_out.at[mine], local.at[0])
    own_qg = pltpu.make_async_copy(qg_own, qg_out.at[x], local.at[1])
    own_kv.start()
    own_qg.start()

    from_far(0)
    for n in range(4):
        z_copy(0, kv_out.at[slot_of(y_far, z, core)], n, 1).start()
    from_z(5)
    from_z(3)
    from_far(6)
    from_far(2)
    from_z(4)
    own_kv.wait()
    sib_row(y).start()
    from_far(5)
    from_far(3)
    x_arrived(x_from, 0)
    x_forward(0).start()

    loads[5].wait()
    for h in range(HEADS):
        cols = slice(h * DIM, (h + 1) * DIM)
        product = g_ref[:, cols].astype(jnp.float32) * o_ref[:, cols].astype(jnp.float32)
        sums = jnp.sum(jnp.transpose(product), axis=0, keepdims=True)
        delta_own[h : h + 1, :] = sums.astype(jnp.bfloat16).astype(jnp.float32)

    def d_copy(n):
        return remote(delta_own, delta_out.at[x], d_send.at[n], d_recv.at[x], device((x + 1 + n) % 4, y, z, core))

    for n in range(3):
        d_copy(n).start()
    own_delta = pltpu.make_async_copy(delta_own, delta_out.at[x], local.at[2])
    own_delta.start()
    loads[6].wait()
    positions(order, pos)

    x_arrived(x_from, 1)
    x_forward(1).start()
    for n, yy in enumerate((y_down, y_up)):
        remote(*slots(0, 8), z_send, y_recv.at[n], sibling).wait_recv()
        sib_row(yy).start()
    for d in (7, 1, 4):
        from_far(d)
    sib_row(y_far).start()

    for p in range(2):
        x_arrived(x_to, p)
        x_arrived((x + 2) % 4, p)
    for n in range(1, 4):
        who = (x + n) % 4
        remote(delta_own, delta_out.at[who], local.at[0], d_recv.at[who], sibling).wait_recv()

    remote(*slots(0, 32), z_send, sib_recv, sibling).wait_recv()
    remote(*slots(0, 14), z_send, sib_recv, sibling).wait_send()
    remote(*slots(0, 17), y_send, sib_recv, sibling).wait_send()
    remote(*slots(0, 32), sib_send, sib_recv, sibling).wait_send()
    for p in range(2):
        x_copy(p, 0).wait_send()
        x_copy(p, 1).wait_send()
        x_forward(p).wait_send()
    for n in range(3):
        d_copy(n).wait_send()
    own_qg.wait()
    own_delta.wait()


def norm_kernel(part_ref, out_ref, got, send, recv):
    x, y, z, core = coords()
    peers = [device((x + d) % 4, y, z, core) for d in (1, 3, 2)]
    greet(peers)

    def copy(n):
        return remote(part_ref, got.at[x], send.at[n], recv.at[x], peers[n])

    for n in range(3):
        copy(n).start()
    for n in range(1, 4):
        who = (x + n) % 4
        remote(part_ref, got.at[who], send.at[0], recv.at[who], peers[0]).wait_recv()
    logs = [part_ref[...]] + [got[(x + n) % 4] for n in range(1, 4)]
    top = functools.reduce(jnp.maximum, logs)
    out_ref[...] = top + jnp.log2(functools.reduce(jnp.add, [jnp.exp2(v - top) for v in logs]))
    for n in range(3):
        copy(n).wait_send()


def reduce_kernel(
    dq_ref, kv_ref, dq_out, dk_out, dv_out,
    sib_got, kv_sum, opp_got, near_got, far_got, z_got, x_opp, x_near, x_far, x_sum,
    sib_send, sib_recv, a_send, a_recv, b_send, b_recv, c_send, c_recv, z_send, z_recv, x_send, x_recv,
):
    x, y, z, core = coords()
    sign = 1 - 2 * core
    sibling = device(x, y, z, 1 - core)
    y_to, y_back, y_opp = (y + sign + 4) % 4, (y - sign + 4) % 4, (y + 2) % 4
    x_to, x_back, x_over = (x + sign + 4) % 4, (x - sign + 4) % 4, (x + 2) % 4
    to_next, to_back = device(x, y_to, z, core), device(x, y_back, z, core)
    dev_to, dev_back = device(x_to, y, z, core), device(x_back, y, z, core)

    greet(plane_peers(x, y, z, core))

    def add(*parts):
        return functools.reduce(jnp.add, [p.astype(jnp.float32) for p in parts])

    def sib_copy(zz):
        return remote(kv_ref.at[1 - core, :, zz], sib_got.at[:, zz], sib_send, sib_recv.at[zz], sibling)

    far_first = (4, 3, 5, 2, 6, 1, 7, 0)

    x_a = remote(dq_ref.at[x_over], x_opp, x_send.at[0], x_recv.at[0], dev_to)
    x_b = remote(dq_ref.at[x_back], x_near, x_send.at[1], x_recv.at[1], dev_back)
    x_c = remote(x_sum, x_far, x_send.at[2], x_recv.at[2], dev_to)
    for d in far_first:
        sib_copy((z + d) % 8).start()
        if d == 3:
            x_a.start()
            x_b.start()

    def with_sibling(yy, zz):
        return add(kv_ref[core, yy, zz], sib_got[yy, zz])

    def a_copy(zz):
        return remote(kv_sum.at[y_opp, zz], opp_got.at[zz], a_send, a_recv.at[zz], to_next)

    def b_copy(zz):
        return remote(kv_sum.at[y_back, zz], near_got.at[zz], b_send, b_recv.at[zz], to_back)

    def c_copy(zz):
        return remote(kv_sum.at[y_to, zz], far_got.at[zz], c_send, c_recv.at[zz], to_next)

    def z_copy(zz):
        return remote(kv_sum.at[y, zz], z_got.at[z], z_send, z_recv, device(x, y, zz, core))

    def step_a(d):
        zz = (z + d) % 8
        sib_copy(zz).wait_recv()
        kv_sum[y_opp, zz] = with_sibling(y_opp, zz).astype(jnp.bfloat16)
        a_copy(zz).start()

    def step_b(d):
        zz = (z + d) % 8
        kv_sum[y_back, zz] = with_sibling(y_back, zz).astype(jnp.bfloat16)
        b_copy(zz).start()

    def step_c(d):
        zz = (z + d) % 8
        total = with_sibling(y_to, zz)
        a_copy(zz).wait_recv()
        kv_sum[y_to, zz] = add(total, opp_got[zz]).astype(jnp.bfloat16)
        c_copy(zz).start()

    def total_here(zz):
        total = with_sibling(y, zz)
        b_copy(zz).wait_recv()
        c_copy(zz).wait_recv()
        return add(total, near_got[zz], far_got[zz])

    def step_z(d):
        zz = (z + d) % 8
        kv_sum[y, zz] = total_here(zz).astype(jnp.bfloat16)
        z_copy(zz).start()

    def sum_x(h, c):
        rows = pl.ds(pl.multiple_of(h * 16, 16), 16)
        x_sum[rows, :] = add(dq_ref[x_to, rows, :], x_opp[rows, :]).astype(jnp.bfloat16)
        return c

    for n in range(11):
        if n < 8:
            step_a(far_first[n])
        if 0 <= n - 2 < 8:
            step_b(far_first[n - 2])
            step_c(far_first[n - 2])
        if 0 <= n - 4 < 7:
            step_z(far_first[n - 4])
        if n == 6:
            x_a.wait_recv()
            lax.fori_loop(0, 8, sum_x, 0)
            x_c.start()

    x_b.wait_recv()
    x_c.wait_recv()
    for h in range(HEADS):
        cols = slice(h * DIM, (h + 1) * DIM)
        total = add(dq_ref[x, :, cols], x_near[:, cols], x_far[:, cols])
        dq_out[:, cols] = jnp.transpose(total).astype(jnp.bfloat16)

    total = total_here(z)
    seven = kv_sum.at[0, pl.ds(0, 7)]
    remote(seven, seven, z_send, z_recv, sibling).wait_recv()
    for d in range(1, 8):
        total = add(total, z_got[(z + d) % 8])
    dk_out[...] = total[:, 0:DIM].astype(jnp.bfloat16)
    dv_out[...] = total[:, DIM:].astype(jnp.bfloat16)

    remote(sib_got, sib_got, sib_send, z_recv, sibling).wait_send()
    for send in (a_send, b_send, c_send):
        remote(kv_sum.at[0], kv_sum.at[0], send, z_recv, sibling).wait_send()
    remote(seven, seven, z_send, z_recv, sibling).wait_send()
    x_a.wait_send()
    x_b.wait_send()
    x_c.wait_send()


def smem():
    return pl.BlockSpec(memory_space=pltpu.SMEM)


def vmem():
    return pl.BlockSpec(memory_space=pltpu.VMEM)


def hbm():
    return pl.BlockSpec(memory_space=pl.ANY)


def bf16(*shape):
    return jax.ShapeDtypeStruct(shape, jnp.bfloat16)


def i32(*shape):
    return jax.ShapeDtypeStruct(shape, jnp.int32)


def f32(*shape):
    return jax.ShapeDtypeStruct(shape, jnp.float32)


def dma(*shape):
    return pltpu.SemaphoreType.DMA(shape) if shape else pltpu.SemaphoreType.DMA


def params(collective_id=None, vmem_mib=48):
    return pltpu.CompilerParams(
        collective_id=collective_id, has_side_effects=collective_id is not None, vmem_limit_bytes=vmem_mib << 20
    )


def gather_call(queries, exps, keys, values, outs, grads, order):
    return pl.pallas_call(
        gather_kernel,
        out_shape=(bf16(NQ, 2, WIDE, DIM), bf16(NK, 2, STRIPE, DIM), f32(NQ, HEADS, STRIPE), i32(128)),
        in_specs=[hbm()] * 7,
        out_specs=(hbm(), hbm(), hbm(), smem()),
        scratch_shapes=[
            pltpu.SMEM((256,), jnp.int32),
            pltpu.VMEM((STRIPE, WIDE), jnp.bfloat16),
            pltpu.VMEM((1, STRIPE), jnp.int32),
            pltpu.VMEM((STRIPE, WIDE), jnp.bfloat16),
            pltpu.VMEM((STRIPE, WIDE), jnp.bfloat16),
            pltpu.VMEM((2, STRIPE, DIM), jnp.bfloat16),
            pltpu.VMEM((2, WIDE, DIM), jnp.bfloat16),
            pltpu.VMEM((HEADS, STRIPE), jnp.float32),
            dma(NK), dma(), dma(), dma(2), dma(), dma(), dma(2, 2), dma(2), dma(NQ, 2), dma(3), dma(NQ), dma(3), dma(7),
        ],
        compiler_params=params(0, 8),
        name="gather",
    )(queries, exps, keys, values, outs, grads, order)


def stats_call(win, pos, qg, kv):
    return pl.pallas_call(
        stats_kernel,
        out_shape=(f32(NQ, WIDE), i32(1024)),
        in_specs=[smem()] * 2 + [vmem()] * 2,
        out_specs=(vmem(), smem()),
        scratch_shapes=[
            pltpu.VMEM((8, WIDE), jnp.float32),
            pltpu.VMEM((8, WIDE), jnp.float32),
        ],
        compiler_params=params(None, 16),
        name="stats",
    )(win, pos, qg, kv)


def norm_call(part):
    return pl.pallas_call(
        norm_kernel,
        out_shape=f32(NQ, WIDE),
        in_specs=[vmem()],
        out_specs=vmem(),
        scratch_shapes=[pltpu.VMEM((NQ, NQ, WIDE), jnp.float32), dma(3), dma(NQ)],
        compiler_params=params(1, 4),
        name="norm",
    )(part)


def grads_call(win, lists, qg, kv, norm, delta):
    return pl.pallas_call(
        grads_kernel,
        out_shape=(bf16(NQ, DIM, WIDE), bf16(NK, STRIPE, 2 * DIM)),
        in_specs=[smem()] * 2 + [vmem()] * 4,
        out_specs=(vmem(), vmem()),
        scratch_shapes=[
            pltpu.VMEM((NK, STRIPE, 2 * DIM), jnp.float32),
            pltpu.VMEM((DIM, WIDE), jnp.float32),
            pltpu.VMEM((2, WIDE), jnp.float32),
        ],
        compiler_params=params(None, 40),
        name="grads",
    )(win, lists, qg, kv, norm, delta)


def reduce_call(dq, dkv):
    tile = (STRIPE, 2 * DIM)
    return pl.pallas_call(
        reduce_kernel,
        out_shape=(bf16(STRIPE, WIDE), bf16(STRIPE, DIM), bf16(STRIPE, DIM)),
        in_specs=[vmem()] * 2,
        out_specs=(vmem(), vmem(), vmem()),
        scratch_shapes=[
            pltpu.VMEM((4, 8, *tile), jnp.bfloat16),
            pltpu.VMEM((4, 8, *tile), jnp.bfloat16),
            pltpu.VMEM((8, *tile), jnp.bfloat16),
            pltpu.VMEM((8, *tile), jnp.bfloat16),
            pltpu.VMEM((8, *tile), jnp.bfloat16),
            pltpu.VMEM((8, *tile), jnp.bfloat16),
            pltpu.VMEM((DIM, WIDE), jnp.bfloat16),
            pltpu.VMEM((DIM, WIDE), jnp.bfloat16),
            pltpu.VMEM((DIM, WIDE), jnp.bfloat16),
            pltpu.VMEM((DIM, WIDE), jnp.bfloat16),
            dma(), dma(8), dma(), dma(8), dma(), dma(8), dma(), dma(8), dma(), dma(), dma(3), dma(3),
        ],
        compiler_params=params(2, 20),
        name="reduce",
    )(dq, dkv.reshape(2, 4, 8, *tile))


def finish_kernel(a_in, b_in, c_in, a_out, b_out, c_out, sem):
    copies = [
        pltpu.make_async_copy(src, dst, sem.at[n])
        for n, (src, dst) in enumerate(((a_in, a_out), (b_in, b_out), (c_in, c_out)))
    ]
    for copy in copies:
        copy.start()
    for copy in copies:
        copy.wait()


def finish_call(dq, dk, dv):
    return pl.pallas_call(
        finish_kernel,
        out_shape=(bf16(STRIPE, WIDE), bf16(STRIPE, DIM), bf16(STRIPE, DIM)),
        in_specs=[hbm()] * 3,
        out_specs=(hbm(),) * 3,
        scratch_shapes=[dma(3)],
        compiler_params=params(None, 4),
        name="finish",
    )(dq, dk, dv)


def per_device(
    queries, query_exps, key_head, value_head, forward_out, output_grad, stripe_order, window_size
):
    held = [
        pltpu.with_memory_space_constraint(a, pltpu.HBM)
        for a in (
            queries, query_exps.reshape(1, STRIPE), key_head, value_head, forward_out, output_grad, stripe_order
        )
    ]
    qg, kv, delta, pos = gather_call(*held)
    part, lists = stats_call(window_size, pos, qg, kv)
    norm = norm_call(part)
    dq, dkv = grads_call(window_size, lists, qg, kv, norm, delta)
    return finish_call(*reduce_call(dq, dkv))


def solution(mesh):
    return jax.shard_map(
        per_device,
        mesh=mesh,
        in_specs=(
            P(("row", "col"), None),
            P(("row", "col")),
            P(("col", "row"), None),
            P(("col", "row"), None),
            P(("row", "col"), None),
            P(("row", "col"), None),
            P(),
            P(),
        ),
        out_specs=(P(("row", "col"), None), P(("col", "row"), None), P(("col", "row"), None)),
        check_vma=False,
    )
```
